32 devices in a mesh: lat: 4 (over x, core), lon: 8 (over z, y).
Axes of the slice: x: 2, y: 2, z: 4, core: 2. Of those that a mesh axis runs over, the one named last changes fastest.
Arguments:
- control: float32 [256, 512, 128], P('lat', 'lon'), may hold values from -6 to 6
- kappa: float32 [256, 512], P('lat', 'lon'), may hold values from 0.1 to 0.24
- sigma: float32 [256, 512, 128], P('lat', 'lon'), may hold values from 0.5 to 2
- vertical: float32 [128, 128], replicated, may hold values from -0.5 to 0.5
- channel_table: bfloat16 [616, 128], replicated, may hold values from -0.5 to 0.5
- channel_pick: int32 [64], replicated, may hold values from 0 to 615
- r_inverse: float32 [64, 64], replicated, may hold values from -1 to 4, as said below
- innovations: float32 [32768, 64], P(('lat', 'lon')), may hold values from -6 to 6
- error_scale: float32 [32768], P(('lat', 'lon')), may hold values from 0.5 to 2
- obs_owner: int32 [32768, 1], P(('lat', 'lon')), may hold values from 0 to 31; in each aligned block of 1024 rows (0 to 1023, 1024 to 2047, ...) at most 64 rows name the same one
- obs_cell: int32 [32768], P(('lat', 'lon')), may hold values from 0 to 4095
- obs_count: int32 [32], P(('lat', 'lon')), may hold values from 128 to 1024, as said below
Outputs:
- gradient: float32 [256, 512, 128], P('lat', 'lon')
- departures: float32 [32768, 64], P(('lat', 'lon'))
The draws below stay inside these ranges and needn't reach their ends.
Inputs may be any that keep to these rules, and one draw needn't show every extreme that they name: `obs_owner`: in the rows of one device, at most 64 observations name one owner, a bound that some block reaches of them. `obs_count`: some device holds 1024 valid observations; the valid ones are the first of a device's slots. `r_inverse`: Symmetric.
All inputs are finite; a program needn't handle non-finite values.
Results may differ from the reference program's by a relative error of at most 0.0013.
Values may be sent and summed in bfloat16 or wider, within the bound.
No kernel may reach another device: no remote copies, remote signals or barrier semaphores. Data moves between devices by JAX's collectives and lax.ppermute only.
A program may use at most 64 MiB of HBM per device.

```python
import math
import jax
import jax.numpy as jnp
import numpy as np
from jax import lax

CLAT = 64
CLON = 64
LEV = 128
CHAN = 64
CH_ALL = 616
NSTEP = 4
OBS_DEV = 1024
CAP = 64
NLAT = 256
NLON = 512
OBS = 32768
N_LAT = 4
N_LON = 8


def draw_r_inverse(key, part):
    first, second = jax.random.split(jax.random.fold_in(key, 11))
    off_part = jax.random.normal(first, (CHAN, CHAN), jnp.float32)
    off_part = (off_part + off_part.T) * (0.2 / math.sqrt(CHAN))
    diagonal = jnp.exp(jax.random.uniform(second, (CHAN,), jnp.float32, 0.0, math.log(4.0)))
    identity = jnp.eye(CHAN, dtype=jnp.float32)
    return off_part * (1.0 - identity) + identity * diagonal[None, :]


def draw_obs_count(key, part):
    first, second = jax.random.split(jax.random.fold_in(key, 23))
    devices_all = N_LAT * N_LON
    shifts = jax.random.randint(first, (devices_all,), 0, 4)
    counts = jnp.right_shift(jnp.full((devices_all,), OBS_DEV, jnp.int32), shifts.astype(jnp.int32))
    full_one = jax.random.randint(second, (), 0, devices_all)
    return jnp.where(jnp.arange(devices_all) == full_one, OBS_DEV, counts).astype(jnp.int32)


def place_ends(array, own_key, least, largest):
    index_at = [jax.random.randint(jax.random.fold_in(own_key, axis), (), 0, length) for axis, length in enumerate(array.shape)]
    longest = array.shape.index(max(array.shape))
    beside = index_at[:longest] + [(index_at[longest] + 1) % array.shape[longest]] + index_at[longest + 1:]
    return array.at[tuple(index_at)].set(least).at[tuple(beside)].set(largest)


def steps_of(rng, dims, cuts, least, top_value):
    def one(position, blocks):
        heights = jax.random.uniform(jax.random.fold_in(jax.random.fold_in(rng, 6), position), (blocks,), jnp.float32, least / len(cuts), top_value / len(cuts))
        return jnp.repeat(jnp.exp(heights), dims[position] // blocks).reshape((-1,) + (1,) * (len(dims) - position - 1))

    factor_of = one(*cuts[0])
    for cut in cuts[1:]:
        factor_of = factor_of * one(*cut)
    return factor_of


def deal_out(key, own, number, rows, count, top, reach, lean):
    sequence = jax.random.permutation(key, count)
    packed, ordinary = load_shares(count, rows * top, reach, lean, True), load_shares(count, rows * top, reach, lean, False)
    places = jnp.arange(count)

    def named(tallies, rotation):
        used = int((tallies > 0).sum())
        fixed = max(1, used // 4)
        moved = fixed + (places - fixed + rotation * (used - fixed)) % max(1, count - fixed)
        return jnp.zeros((count,), jnp.int32).at[sequence[jnp.where(places < fixed, places, moved)]].set(jnp.asarray(tallies, jnp.int32))

    tallies = jnp.where(number % 4 == 0, named(packed, number // 4), named(ordinary, number - number // 4 - 1))
    mixed = jax.random.permutation(jax.random.fold_in(own, 3), count)
    giver, sink = mixed[0:count // 2 * 2:2], mixed[1:count // 2 * 2:2]
    margin = jnp.minimum(tallies[giver] - 1, reach - tallies[sink]) // 2
    margin = jnp.where((giver == sequence[0]) | (sink == sequence[0]) | (tallies[sink] == 0), 0, jnp.maximum(margin, 0))
    moved = jax.random.randint(jax.random.fold_in(own, 4), (count // 2,), 0, 1 << 20) % (margin + 1)
    tallies = tallies.at[giver].add(-moved).at[sink].add(moved)
    labels = jnp.searchsorted(jnp.cumsum(tallies), jnp.arange(rows * top), side="right").astype(jnp.int32)
    listing = labels.reshape(top, rows).T
    listing = listing[jax.random.permutation(jax.random.fold_in(own, 1), rows)]
    rotation = jax.random.randint(jax.random.fold_in(own, 2), (rows, 1), 0, top)
    return jnp.take_along_axis(listing, (jnp.arange(top)[None, :] + rotation) % top, axis=1)


def load_shares(count, total, reach, lean, full):
    weights = [(1 << 20) // math.isqrt(rank ** lean) + 1 for rank in range(1, count + 1)]
    largest = reach if full else min(reach, max(-(-total // count), total * weights[0] // sum(weights)))
    least = 1 if total - largest >= count - 1 else 0
    given, spare = [largest] + [least] * (count - 1), total - largest - least * (count - 1)
    while spare > 0:
        candidates = [i for i in range(1, count) if given[i] < largest] or [i for i in range(1, count) if given[i] < reach]
        whole, budget = sum([weights[i] for i in candidates]), spare
        for i in candidates:
            more = min(reach - given[i], max(1, budget * weights[i] // whole), spare)
            given[i] = given[i] + more
            spare = spare - more
    return np.array(given)


def bell_draw(own_key, dims, width, limit, shards=(), held_as=jnp.bfloat16):
    values = width * jax.random.normal(own_key, dims, jnp.float32)
    if shards:
        values = values * steps_of(own_key, dims, shards, -0.22, 0.18)
    return jnp.clip(values, -limit, limit).astype(held_as)


def setup_inputs(seed: int = 0) -> dict:
    keys = jax.random.split(jax.random.key(seed), 13)
    control = bell_draw(keys[0], (NLAT, NLON, LEV), 1.0, 6.0, ((0, 4), (1, 8)), jnp.float32)
    kappa = jnp.clip(0.1 + 0.13999999 * jax.random.uniform(keys[1], (NLAT, NLON), jnp.float32) ** steps_of(keys[1], (NLAT, NLON), ((0, 4), (1, 8)), -0.2, 0.2), 0.1, 0.24)
    sigma = jnp.clip(jnp.exp(math.log(2.0) - 1.3862944 * jax.random.uniform(keys[2], (NLAT, NLON, LEV), jnp.float32) ** steps_of(keys[2], (NLAT, NLON, LEV), ((0, 4), (1, 8)), -0.2, 0.2)), 0.5, 2.0)
    vertical = bell_draw(keys[3], (LEV, LEV), LEV ** -0.5, 0.5, (), jnp.float32)
    channel_table = bell_draw(keys[4], (CH_ALL, LEV), LEV ** -0.5, 0.5)
    channel_pick = place_ends(jax.random.randint(keys[5], (CHAN,), 0, CH_ALL), jax.random.fold_in(keys[5], 1), 0, CH_ALL - 1).astype(jnp.int32)
    r_inverse = draw_r_inverse(jax.random.fold_in(keys[12], 71), 0)
    innovations = bell_draw(keys[7], (OBS, CHAN), 1.0, 6.0, ((0, 32),), jnp.float32)
    error_scale = jnp.clip(jnp.exp(math.log(2.0) - 1.3862944 * jax.random.uniform(keys[8], (OBS,), jnp.float32) ** steps_of(keys[8], (OBS,), ((0, 32),), -0.2, 0.2)), 0.5, 2.0)
    obs_owner_keys = jax.random.split(jax.random.fold_in(keys[9], 1), OBS // OBS_DEV)
    obs_owner_turns = jax.random.permutation(jax.random.fold_in(keys[9], 3), OBS // OBS_DEV)
    obs_owner = jax.vmap(lambda own, number: deal_out(jax.random.fold_in(keys[9], 2), own, number, OBS_DEV, N_LAT * N_LON, 1, CAP, 2))(obs_owner_keys, obs_owner_turns).reshape((OBS, 1))
    obs_cell = place_ends(jax.random.randint(keys[10], (OBS,), 0, CLAT * CLON), jax.random.fold_in(keys[10], 1), 0, (CLAT * CLON) - 1).astype(jnp.int32)
    obs_count = draw_obs_count(jax.random.fold_in(keys[12], 71), 0)
    return {"control": control, "kappa": kappa, "sigma": sigma, "vertical": vertical, "channel_table": channel_table, "channel_pick": channel_pick, "r_inverse": r_inverse, "innovations": innovations, "error_scale": error_scale, "obs_owner": obs_owner, "obs_cell": obs_cell, "obs_count": obs_count}


def laplacian(padded):
    return padded[2:, 1:-1] + padded[:-2, 1:-1] + padded[1:-1, 2:] + padded[1:-1, :-2] - 4.0 * padded[1:-1, 1:-1]


def pad_grid(field):
    field = jnp.concatenate([field[:, -1:], field, field[:, :1]], axis=1)
    zeros = jnp.zeros_like(field[:1])
    return jnp.concatenate([zeros, field, zeros], axis=0)


def reference(control, kappa, sigma, vertical, channel_table, channel_pick, r_inverse, innovations, error_scale, obs_owner, obs_cell, obs_count):
    state = jnp.dot(control.reshape(-1, LEV), vertical, precision=lax.Precision.HIGHEST, preferred_element_type=jnp.float32).reshape(NLAT, NLON, LEV)
    kappa_cols = kappa[:, :, None]
    for sweep in range(NSTEP):
        state = state + kappa_cols * laplacian(pad_grid(state))
    profiles = (sigma * state).astype(jnp.bfloat16).reshape(NLAT * NLON, LEV)
    picked = channel_table[channel_pick]
    owner = obs_owner[:, 0]
    column_lat = (owner // N_LON) * CLAT + obs_cell // CLON
    column_lon = (owner % N_LON) * CLON + obs_cell % CLON
    column = (column_lat * NLON + column_lon).astype(jnp.int32)
    slot_index = jnp.arange(OBS, dtype=jnp.int32)
    valid = (slot_index % OBS_DEV) < obs_count[slot_index // OBS_DEV]
    weight = jnp.where(valid, 1.0 / (error_scale * error_scale), jnp.float32(0.0))
    profile = profiles[column]
    evolved = lax.dot_general(profile, picked, (((1,), (1,)), ((), ())), preferred_element_type=jnp.float32)
    departures = jnp.dot(evolved - innovations, r_inverse, precision=lax.Precision.HIGHEST, preferred_element_type=jnp.float32) * weight[:, None]
    rounded = departures.astype(jnp.bfloat16)
    increments = jnp.dot(rounded, picked, preferred_element_type=jnp.float32)
    obs_gradient = jnp.zeros((NLAT * NLON, LEV), jnp.float32).at[column].add(increments).reshape(NLAT, NLON, LEV)
    adjoint = sigma * obs_gradient
    for sweep in range(NSTEP):
        adjoint = adjoint + laplacian(pad_grid(kappa_cols * adjoint))
    back = lax.dot_general(adjoint.reshape(-1, LEV), vertical, (((1,), (1,)), ((), ())), precision=lax.Precision.HIGHEST, preferred_element_type=jnp.float32)
    gradient = control + back.reshape(NLAT, NLON, LEV)
    return gradient, departures
```

```python
import functools

import jax
import jax.numpy as jnp
from jax import lax
from jax.experimental import pallas as pl
from jax.experimental.pallas import tpu as pltpu
from jax.sharding import PartitionSpec as P

NSTEP = 4
F32 = jnp.float32
BF16 = jnp.bfloat16
I32 = jnp.int32
INNOV_MAX = 6.0
INNOV_STEP = INNOV_MAX / 32767.0
WEIGHT_MAX = 4.0
WEIGHT_STEP = WEIGHT_MAX / 65535.0
VMEM_BYTES = 56 * 1024 * 1024


def split_hi_lo(value):
    high = value.astype(BF16)
    low = (value - high.astype(F32)).astype(BF16)
    return high, low


def iota(shape, dim):
    return lax.broadcasted_iota(I32, shape, dim)


def dot_f32(left, right):
    return jnp.dot(left, right, preferred_element_type=F32)


def dot_nt(left, right):
    return lax.dot_general(left, right, (((1,), (1,)), ((), ())), preferred_element_type=F32)


def dot_tn(left, right):
    return lax.dot_general(left, right, (((0,), (0,)), ((), ())), preferred_element_type=F32)


def params():
    return pltpu.CompilerParams(vmem_limit_bytes=VMEM_BYTES)


def vmem_specs(count):
    return [pl.BlockSpec(memory_space=pltpu.VMEM)] * count


def address_kernel(
    devices_all, quarter, count_ref, owner_ref, cell_ref, scale_ref, innov_ref, out_ref, key_ref,
    rhs_ref, word_ref,
):
    obs = owner_ref.shape[1]
    rows_half = devices_all * quarter
    rows = 2 * rows_half
    owner = owner_ref[...]
    cell = cell_ref[...]
    mine = iota((devices_all, obs), 0) == owner
    mine_f = mine.astype(F32)
    mine_b = mine_f.astype(BF16)
    block = min(256, obs)
    earlier = (iota((block, block), 0) < iota((block, block), 1)).astype(F32).astype(BF16)
    running = jnp.zeros((devices_all, 1), F32)
    parts = []
    for start in range(0, obs, block):
        piece = mine_f[:, start : start + block]
        before = dot_f32(mine_b[:, start : start + block], earlier) + running
        parts.append(jnp.sum(piece * before, axis=0, keepdims=True))
        running = running + jnp.sum(piece, axis=1, keepdims=True)
    position = jnp.concatenate(parts, axis=1).astype(I32)
    group = position // quarter
    key = (
        (group // 2) * rows + (group % 2) * rows_half + owner * quarter + position % quarter
    )
    key_ref[...] = key
    scale = scale_ref[...]
    valid = iota((1, obs), 1) < count_ref[0]
    weight = jnp.where(valid, 1.0 / (scale * scale), 0.0)
    weight = jnp.minimum(jnp.floor(weight * (1.0 / WEIGHT_STEP) + 0.5), 65535.0)
    weight_high = jnp.floor(weight * (1.0 / 256.0))
    weight_low = weight - 256.0 * weight_high
    cell_high = (cell // 64).astype(F32)
    cell_low = (cell % 64).astype(F32)
    left = jnp.concatenate(
        [mine_f * piece for piece in (cell_high, cell_low, weight_high, weight_low)], axis=0
    ).astype(BF16)
    place = (iota((128, obs), 0) == position).astype(F32).astype(BF16)
    table = dot_nt(left, place).astype(I32)
    n = devices_all
    cells = table[:n] * 64 + table[n : 2 * n]
    weights = table[2 * n : 3 * n] * 256 + table[3 * n :]
    out_ref[:, quarter, :] = (cells << 16) | weights

    twice = innov_ref[...]
    level = jnp.floor(jnp.clip(twice, -INNOV_MAX, INNOV_MAX) * (1.0 / INNOV_STEP) + 0.5)
    high = jnp.floor(level * (1.0 / 256.0))
    low = level - 256.0 * high
    left_lane = iota((obs, 128), 1) < 64
    zero = jnp.zeros_like(high)
    for side in range(2):
        keep = left_lane if side == 0 else jnp.logical_not(left_lane)
        rhs_ref[side * obs : (side + 1) * obs, :128] = jnp.where(keep, high, zero).astype(BF16)
        rhs_ref[side * obs : (side + 1) * obs, 128:] = jnp.where(keep, low, zero).astype(BF16)
    chunk = min(256, rows_half)

    def fill(step, carry):
        base = step * chunk
        total = []
        for half in range(2):
            row = iota((chunk, obs), 0) + (base + half * rows_half)
            acc = jnp.zeros((chunk, 256), F32)
            for side in range(2):
                hot = (row + side * rows == key).astype(F32).astype(BF16)
                acc = acc + dot_f32(hot, rhs_ref[side * obs : (side + 1) * obs, :])
            total.append((acc[:, :128] * 256.0 + acc[:, 128:]).astype(I32))
        word_ref[pl.ds(pl.multiple_of(base, chunk), chunk), :] = (total[0] << 16) | (
            total[1] & 0xFFFF
        )
        return carry

    lax.fori_loop(0, rows_half // chunk, fill, 0)
    for device in range(devices_all):
        out_ref[device, :quarter, :] = word_ref[device * quarter : (device + 1) * quarter, :]


def fill_wide(wide_ref, tile, sides, north, south, north_on, south_on):
    rows, cols = tile.shape[0], tile.shape[1]
    wide_ref[NSTEP : NSTEP + rows, :cols, :] = tile
    wide_ref[NSTEP : NSTEP + rows, cols:, :] = sides.astype(F32)
    wide_ref[:NSTEP] = north.astype(F32) * north_on
    wide_ref[NSTEP + rows :] = south.astype(F32) * south_on


def broadcast_kappa(kappa):
    rows, cols = kappa.shape
    spread = jnp.where(
        iota((rows, cols, cols), 1) == iota((rows, cols, cols), 2), kappa[:, None, :], 0.0
    )
    return jnp.broadcast_to(jnp.sum(spread, axis=2, keepdims=True), (rows, cols, 128))


def neighbours(ref, row):
    here = ref[row]
    cols = here.shape[0]
    return (
        ref[row - 1]
        + ref[row + 1]
        + pltpu.roll(here, 1, 0)
        + pltpu.roll(here, cols - 1, 0)
        - 4.0 * here
    ), here


def forward_kernel(
    poles_ref, control_ref, sides_ref, north_ref, south_ref, kappa_ref, sigma_ref, vertical_ref,
    picked_ref, out_ref, first_ref, second_ref, kap_ref, prof_ref, pick_ref,
):
    rows, cols, levels = control_ref.shape
    north_on, south_on = poles_ref[0], poles_ref[1]
    fill_wide(
        first_ref, control_ref[...], sides_ref[0], north_ref[0], south_ref[0], north_on, south_on
    )
    fill_wide(
        kap_ref, broadcast_kappa(kappa_ref[...]), sides_ref[1], north_ref[1], south_ref[1],
        north_on, south_on,
    )
    source, target = first_ref, second_ref
    for sweep in range(1, NSTEP + 1):

        def step(row, carry, source=source, target=target):
            change, here = neighbours(source, row)
            target[row] = here + kap_ref[row] * change
            return carry

        lax.fori_loop(sweep, rows + 2 * NSTEP - sweep, step, 0)
        source, target = target, source
    high, low = split_hi_lo(vertical_ref[...])
    mixing = jnp.concatenate(
        [jnp.concatenate([high, low], axis=1), jnp.concatenate([high, low], axis=1)], axis=0
    )
    quarter = rows // 4
    step_rows = 4
    for part in range(4):

        def mix(step, carry, part=part):
            row = part * quarter + step * step_rows
            block = source[pl.ds(NSTEP + row, step_rows), :cols, :].reshape(step_rows * cols, levels)
            pair = jnp.concatenate(split_hi_lo(block), axis=1)
            both = dot_f32(pair, mixing)
            state = both[:, :levels] + both[:, levels:]
            dev = sigma_ref[pl.ds(row, step_rows)].reshape(step_rows * cols, levels)
            prof_ref[
                pl.ds(pl.multiple_of(step * step_rows * cols, step_rows * cols), step_rows * cols),
                part * levels : (part + 1) * levels,
            ] = (dev * state).astype(BF16)
            return carry

        lax.fori_loop(0, quarter // step_rows, mix, 0)
    fill_picked(pick_ref, picked_ref[...])

    def project(step, carry):
        where = pl.ds(pl.multiple_of(step * 256, 256), 256)
        value = dot_nt(prof_ref[where, :], pick_ref[...])
        high, low = split_hi_lo(value)
        out_ref[where, :] = jnp.concatenate([high, low], axis=1)
        return carry

    lax.fori_loop(0, prof_ref.shape[0] // 256, project, 0)


def fill_picked(pick_ref, picked):
    channels, levels = picked.shape
    pick_ref[...] = jnp.zeros_like(pick_ref)
    for part in range(4):
        pick_ref[
            part * channels : (part + 1) * channels, part * levels : (part + 1) * levels
        ] = picked


def owner_kernel(
    devices_all, quarter, recv_ref, evolved_ref, rinv_ref, picked_ref, sigma_ref, ret_ref, adj_ref,
    word_ref, dep_ref, acc_ref, pick_ref,
):
    rows_half = devices_all * quarter
    rows = 2 * rows_half
    cells_part = evolved_ref.shape[0]
    shift = cells_part.bit_length() - 1
    for device in range(devices_all):
        word_ref[device * quarter : (device + 1) * quarter, :] = recv_ref[device, :quarter, :]
    meta = recv_ref[:, quarter, :]
    cells, weights = meta >> 16, meta & 0xFFFF
    table = jnp.concatenate(
        [
            piece.astype(F32).astype(BF16)
            for piece in (cells >> 6, cells & 63, weights >> 8, weights & 255)
        ],
        axis=1,
    )
    high, low = split_hi_lo(rinv_ref[...])
    zero = jnp.zeros_like(high)
    mixing = jnp.concatenate(
        [jnp.concatenate([high, low], axis=1), jnp.concatenate([high, zero], axis=1)], axis=0
    )
    acc_ref[...] = jnp.zeros_like(acc_ref)
    chunk = min(256, rows_half)
    left_lane = iota((chunk, 128), 1) < 64
    lane_half = iota((chunk, 128), 1) // 64
    per_half = rows_half // chunk

    def work(step, carry):
        half = step // per_half
        base = (step % per_half) * chunk
        row = iota((chunk, devices_all), 0) + base
        spread = (row // quarter == iota((chunk, devices_all), 1)).astype(F32).astype(BF16)
        found = dot_f32(spread, table)
        cell_lane = found[:, :128] * 64.0 + found[:, 128:256]
        weight_lane = (found[:, 256:384] * 256.0 + found[:, 384:]) * WEIGHT_STEP
        lane = iota((chunk, 128), 1)
        r = (iota((chunk, 128), 0) + base) % quarter
        hots, parts, weight, values = [], [], [], []
        for side in range(2):
            pick = lane == (2 * side + half) * quarter + r
            cell = jnp.sum(jnp.where(pick, cell_lane, 0.0), axis=1, keepdims=True).astype(I32)
            weight.append(jnp.sum(jnp.where(pick, weight_lane, 0.0), axis=1, keepdims=True))
            part = cell >> shift
            inside = cell & (cells_part - 1)
            hot = (iota((chunk, cells_part), 1) == inside).astype(F32).astype(BF16)
            got = dot_f32(hot, evolved_ref[...])
            got = got[:, :256] + got[:, 256:]
            lanes = jnp.where(part >= 2, got[:, 128:], got[:, :128])
            swapped = pltpu.roll(lanes, 64, 1)
            odd = (part & 1) == 1
            values.append(
                jnp.where(odd, swapped, lanes) if side == 0 else jnp.where(odd, lanes, swapped)
            )
            hots.append(hot)
            parts.append(part)
        evolved = jnp.where(left_lane, values[0], values[1])
        words = word_ref[pl.ds(pl.multiple_of(base, chunk), chunk), :]
        words = jnp.where(half == 0, words, words << 16) >> 16
        gap = evolved - words.astype(F32) * INNOV_STEP
        both = dot_f32(jnp.concatenate(split_hi_lo(gap), axis=1), mixing)
        dep = (both[:, :128] + both[:, 128:]) * jnp.where(left_lane, weight[0], weight[1])
        dep_ref[pl.ds(pl.multiple_of(step * chunk, chunk), chunk), :] = dep
        rounded = dep.astype(BF16).astype(F32)
        swapped = pltpu.roll(rounded, 64, 1)
        for side in range(2):
            twice = (
                jnp.where(left_lane, rounded, swapped)
                if side == 0
                else jnp.where(left_lane, swapped, rounded)
            )
            wide = jnp.concatenate(
                [
                    jnp.where(parts[side] == lane_half, twice, 0.0).astype(BF16),
                    jnp.where(parts[side] == lane_half + 2, twice, 0.0).astype(BF16),
                ],
                axis=1,
            )
            acc_ref[...] += dot_tn(hots[side], wide)
        return carry

    lax.fori_loop(0, rows // chunk, work, 0)
    for half in range(2):
        for device in range(devices_all):
            at = half * rows_half + device * quarter
            ret_ref[device, half * quarter : (half + 1) * quarter, :] = dep_ref[
                at : at + quarter, :
            ]
    fill_picked(pick_ref, picked_ref[...])
    lat_rows, cols, levels = sigma_ref.shape
    quarter_rows = lat_rows // 4
    step_rows = 4

    def spread_out(step, carry):
        where = pl.ds(pl.multiple_of(step * step_rows * cols, step_rows * cols), step_rows * cols)
        high, low = split_hi_lo(acc_ref[where, :])
        both = dot_f32(high, pick_ref[...]) + dot_f32(low, pick_ref[...])
        for part in range(4):
            at = pl.ds(part * quarter_rows + step * step_rows, step_rows)
            adj_ref[at] = sigma_ref[at] * both[:, part * levels : (part + 1) * levels].reshape(
                step_rows, cols, levels
            )
        return carry

    lax.fori_loop(0, quarter_rows // step_rows, spread_out, 0)


def backward_kernel(
    poles_ref, adj_ref, sides_ref, north_ref, south_ref, kappa_ref, ksides_ref, knorth_ref,
    ksouth_ref, vertical_ref, control_ref, out_ref, first_ref, second_ref, kap_ref,
):
    rows, cols, levels = control_ref.shape
    north_on, south_on = poles_ref[0], poles_ref[1]
    fill_wide(first_ref, adj_ref[...], sides_ref[...], north_ref[...], south_ref[...], north_on, south_on)
    fill_wide(
        kap_ref, broadcast_kappa(kappa_ref[...]), ksides_ref[1], knorth_ref[1], ksouth_ref[1],
        north_on, south_on,
    )

    def scale(row, carry):
        second_ref[row] = first_ref[row] * kap_ref[row]
        return carry

    wide_rows = rows + 2 * NSTEP
    lax.fori_loop(0, wide_rows, scale, 0)
    for sweep in range(1, NSTEP + 1):

        def step(row, carry):
            change, _ = neighbours(second_ref, row)
            first_ref[row] = first_ref[row] + change
            return carry

        lax.fori_loop(sweep, wide_rows - sweep, step, 0)
        if sweep < NSTEP:
            lax.fori_loop(sweep, wide_rows - sweep, scale, 0)
    high, low = split_hi_lo(vertical_ref[...])
    mixing = jnp.concatenate(
        [jnp.concatenate([high, high], axis=1), jnp.concatenate([low, low], axis=1)], axis=0
    )
    step_rows = 4

    def mix(step, carry):
        row = step * step_rows
        block = first_ref[pl.ds(NSTEP + row, step_rows), :cols, :].reshape(step_rows * cols, levels)
        pair = jnp.concatenate(split_hi_lo(block), axis=1)
        both = dot_nt(pair, mixing)
        back = (both[:, :levels] + both[:, levels:]).reshape(step_rows, cols, levels)
        at = pl.ds(row, step_rows)
        out_ref[at] = control_ref[at] + back
        return carry

    lax.fori_loop(0, rows // step_rows, mix, 0)


def return_kernel(devices_all, quarter, recv_ref, key_ref, out_ref, pair_ref):
    rows_half = devices_all * quarter
    rows = 2 * rows_half
    obs = out_ref.shape[0]
    for half in range(2):
        for device in range(devices_all):
            at = half * rows_half + device * quarter
            high, low = split_hi_lo(recv_ref[device, half * quarter : (half + 1) * quarter, :])
            pair_ref[at : at + quarter, :128] = high
            pair_ref[at : at + quarter, 128:] = low
    chunk = min(256, obs)
    for start in range(0, obs, chunk):
        key_rows = jnp.broadcast_to(key_ref[:, start : start + chunk], (128, chunk))
        key = jnp.transpose(key_rows.astype(F32))
        side = key >= rows
        row = jnp.where(side, key - rows, key)[:, :1].astype(I32)
        hot = (iota((chunk, rows), 1) == row).astype(F32).astype(BF16)
        both = dot_f32(hot, pair_ref[...])
        both = both[:, :128] + both[:, 128:]
        out_ref[start : start + chunk, :] = jnp.where(side, pltpu.roll(both, 64, 1), both)[:, :64]


def shifts(axis):
    count = lax.axis_size(axis)
    forward = [(i, (i + 1) % count) for i in range(count)]
    return forward, [(target, source) for source, target in forward]


def exchange_sides(left, right):
    forward, backward = shifts("lon")
    east = lax.ppermute(left, "lon", backward)
    west = lax.ppermute(right, "lon", forward)
    return jnp.concatenate([east, west], axis=-2)


def exchange_rims(top, bottom):
    forward, backward = shifts("lat")
    south = lax.ppermute(top, "lat", backward)
    north = lax.ppermute(bottom, "lat", forward)
    return north, south


def body(
    control,
    kappa,
    sigma,
    vertical,
    channel_table,
    channel_pick,
    r_inverse,
    innovations,
    error_scale,
    obs_owner,
    obs_cell,
    obs_count,
):
    lat_rows, lon_cols, levels = control.shape
    lat_at, lat_count = lax.axis_index("lat"), lax.axis_size("lat")
    poles = jnp.stack([lat_at > 0, lat_at < lat_count - 1]).astype(F32)
    obs_slots = obs_cell.shape[0]
    channels = innovations.shape[1]
    devices_all = lat_count * lax.axis_size("lon")
    capacity = max(4, 2 * obs_slots // devices_all)
    quarter = capacity // 4
    rows_half = devices_all * quarter
    wide = (lat_rows + 2 * NSTEP, lon_cols + 2 * NSTEP, levels)

    payload, key = pl.pallas_call(
        functools.partial(address_kernel, devices_all, quarter),
        out_shape=(
            jax.ShapeDtypeStruct((devices_all, quarter + 1, 128), I32),
            jax.ShapeDtypeStruct((1, obs_slots), I32),
        ),
        in_specs=[pl.BlockSpec(memory_space=pltpu.SMEM)] + vmem_specs(4),
        out_specs=tuple(vmem_specs(2)),
        scratch_shapes=[
            pltpu.VMEM((2 * obs_slots, 256), BF16),
            pltpu.VMEM((rows_half, 128), I32),
        ],
        compiler_params=params(),
        name="address",
    )(
        obs_count,
        obs_owner.reshape(1, obs_slots),
        obs_cell.reshape(1, obs_slots),
        error_scale.reshape(1, obs_slots),
        jnp.concatenate([innovations, innovations], axis=1),
    )
    received = lax.all_to_all(payload, ("lat", "lon"), split_axis=0, concat_axis=0, tiled=True)

    both = jnp.stack(
        [control, jnp.broadcast_to(kappa[:, :, None], control.shape)]
    )
    sides = exchange_sides(both[:, :, :NSTEP].astype(BF16), both[:, :, -NSTEP:].astype(BF16))
    top = jnp.concatenate([both[:, :NSTEP].astype(BF16), sides[:, :NSTEP]], axis=2)
    bottom = jnp.concatenate([both[:, -NSTEP:].astype(BF16), sides[:, -NSTEP:]], axis=2)
    north, south = exchange_rims(top, bottom)

    table_rows = channel_table.shape[0]
    pick_table = (channel_pick[:, None] == jnp.arange(table_rows, dtype=I32)[None, :]).astype(BF16)
    picked = jnp.dot(pick_table, channel_table, preferred_element_type=F32).astype(BF16)

    columns = lat_rows * lon_cols
    evolved = pl.pallas_call(
        forward_kernel,
        out_shape=jax.ShapeDtypeStruct((columns // 4, 8 * channels), BF16),
        in_specs=[pl.BlockSpec(memory_space=pltpu.SMEM)] + vmem_specs(8),
        out_specs=vmem_specs(1)[0],
        scratch_shapes=[pltpu.VMEM(wide, F32)] * 3
        + [
            pltpu.VMEM((columns // 4, 4 * levels), BF16),
            pltpu.VMEM((4 * channels, 4 * levels), BF16),
        ],
        compiler_params=params(),
        name="forward",
    )(poles, control, sides, north, south, kappa, sigma, vertical, picked)

    rinv_pair = jnp.kron(jnp.eye(2, dtype=F32), r_inverse)
    returned, adjoint = pl.pallas_call(
        functools.partial(owner_kernel, devices_all, quarter),
        out_shape=(
            jax.ShapeDtypeStruct((devices_all, 2 * quarter, 128), F32),
            jax.ShapeDtypeStruct(control.shape, F32),
        ),
        in_specs=vmem_specs(5),
        out_specs=tuple(vmem_specs(2)),
        scratch_shapes=[
            pltpu.VMEM((rows_half, 128), I32),
            pltpu.VMEM((2 * rows_half, 128), F32),
            pltpu.VMEM((columns // 4, 4 * channels), F32),
            pltpu.VMEM((4 * channels, 4 * levels), BF16),
        ],
        compiler_params=params(),
        name="owner",
    )(received, evolved, rinv_pair, picked, sigma)
    home = lax.all_to_all(returned, ("lat", "lon"), split_axis=0, concat_axis=0, tiled=True)

    asides = exchange_sides(adjoint[:, :NSTEP].astype(BF16), adjoint[:, -NSTEP:].astype(BF16))
    atop = jnp.concatenate([adjoint[:NSTEP].astype(BF16), asides[:NSTEP]], axis=1)
    abottom = jnp.concatenate([adjoint[-NSTEP:].astype(BF16), asides[-NSTEP:]], axis=1)
    anorth, asouth = exchange_rims(atop, abottom)
    gradient = pl.pallas_call(
        backward_kernel,
        out_shape=jax.ShapeDtypeStruct(control.shape, F32),
        in_specs=[pl.BlockSpec(memory_space=pltpu.SMEM)] + vmem_specs(10),
        out_specs=vmem_specs(1)[0],
        scratch_shapes=[pltpu.VMEM(wide, F32)] * 3,
        compiler_params=params(),
        name="backward",
    )(poles, adjoint, asides, anorth, asouth, kappa, sides, north, south, vertical, control)

    departures = pl.pallas_call(
        functools.partial(return_kernel, devices_all, quarter),
        out_shape=jax.ShapeDtypeStruct(innovations.shape, F32),
        in_specs=vmem_specs(2),
        out_specs=vmem_specs(1)[0],
        scratch_shapes=[pltpu.VMEM((2 * rows_half, 256), BF16)],
        compiler_params=params(),
        name="give_back",
    )(home, key)
    return (gradient, departures)


def solution(mesh):
    return jax.shard_map(
        body,
        mesh=mesh,
        in_specs=(
            P("lat", "lon", None),
            P("lat", "lon"),
            P("lat", "lon", None),
            P(),
            P(),
            P(),
            P(),
            P(("lat", "lon"), None),
            P(("lat", "lon")),
            P(("lat", "lon"), None),
            P(("lat", "lon")),
            P(("lat", "lon")),
        ),
        out_specs=(P("lat", "lon", None), P(("lat", "lon"), None)),
        check_vma=False,
    )
```

```python
import functools

import jax
import jax.numpy as jnp
from jax import lax
from jax.experimental import pallas as pl
from jax.experimental.pallas import tpu as pltpu
from jax.sharding import PartitionSpec as P

NSTEP = 4
F32 = jnp.float32
BF16 = jnp.bfloat16
I32 = jnp.int32
INNOV_MAX = 6.0
INNOV_STEP = INNOV_MAX / 32767.0
WEIGHT_MAX = 4.0
WEIGHT_STEP = WEIGHT_MAX / 65535.0
VMEM_BYTES = 56 * 1024 * 1024


def split_hi_lo(value):
    high = value.astype(BF16)
    low = (value - high.astype(F32)).astype(BF16)
    return high, low


def iota(shape, dim):
    return lax.broadcasted_iota(I32, shape, dim)


def dot_f32(left, right):
    return jnp.dot(left, right, preferred_element_type=F32)


def dot_nt(left, right):
    return lax.dot_general(left, right, (((1,), (1,)), ((), ())), preferred_element_type=F32)


def dot_tn(left, right):
    return lax.dot_general(left, right, (((0,), (0,)), ((), ())), preferred_element_type=F32)


def params():
    return pltpu.CompilerParams(vmem_limit_bytes=VMEM_BYTES)


def vmem_specs(count):
    return [pl.BlockSpec(memory_space=pltpu.VMEM)] * count


def address_kernel(
    devices_all, quarter, count_ref, owner_ref, cell_ref, scale_ref, innov_ref, out_ref, key_ref,
    word_ref,
):
    obs = owner_ref.shape[1]
    rows_half = devices_all * quarter
    rows = 2 * rows_half
    owner = owner_ref[...]
    cell = cell_ref[...]
    mine = iota((devices_all, obs), 0) == owner
    mine_f = mine.astype(F32)
    mine_b = mine_f.astype(BF16)
    block = min(256, obs)
    earlier = (iota((block, block), 0) < iota((block, block), 1)).astype(F32).astype(BF16)
    running = jnp.zeros((devices_all, 1), F32)
    parts = []
    for start in range(0, obs, block):
        piece = mine_f[:, start : start + block]
        before = dot_f32(mine_b[:, start : start + block], earlier) + running
        parts.append(jnp.sum(piece * before, axis=0, keepdims=True))
        running = running + jnp.sum(piece, axis=1, keepdims=True)
    position = jnp.concatenate(parts, axis=1).astype(I32)
    group = position // quarter
    key = (
        (group // 2) * rows + (group % 2) * rows_half + owner * quarter + position % quarter
    )
    key_ref[...] = key
    scale = scale_ref[...]
    valid = iota((1, obs), 1) < count_ref[0]
    weight = jnp.where(valid, 1.0 / (scale * scale), 0.0)
    weight = jnp.minimum(jnp.floor(weight * (1.0 / WEIGHT_STEP) + 0.5), 65535.0)
    weight_high = jnp.floor(weight * (1.0 / 256.0))
    weight_low = weight - 256.0 * weight_high
    cell_high = (cell // 64).astype(F32)
    cell_low = (cell % 64).astype(F32)
    left = jnp.concatenate(
        [mine_f * piece for piece in (cell_high, cell_low, weight_high, weight_low)], axis=0
    ).astype(BF16)
    place = (iota((128, obs), 0) == position).astype(F32).astype(BF16)
    table = dot_nt(left, place).astype(I32)
    n = devices_all
    cells = table[:n] * 64 + table[n : 2 * n]
    weights = table[2 * n : 3 * n] * 256 + table[3 * n :]
    out_ref[:, quarter, :] = (cells << 16) | weights

    level = jnp.floor(
        jnp.clip(innov_ref[...], -INNOV_MAX, INNOV_MAX) * (1.0 / INNOV_STEP) + 0.5
    )
    high = jnp.floor(level * (1.0 / 256.0))
    low = (level - 256.0 * high).astype(BF16)
    high = high.astype(BF16)
    bytes_of = [jnp.concatenate([high, low], axis=0), jnp.concatenate([low, high], axis=0)]
    chunk = min(256, rows_half)
    left_lane = iota((chunk, 128), 1) < 64
    for base in range(0, rows_half, chunk):
        total = []
        for half in range(2):
            row = iota((chunk, obs), 0) + (base + half * rows_half)
            found = []
            for side in range(2):
                hot = (row + side * rows == key).astype(F32).astype(BF16)
                got = dot_nt(hot, bytes_of[side])
                found.append(got * 256.0 + pltpu.roll(got, 64, 1))
            total.append(jnp.where(left_lane, found[0], found[1]).astype(I32))
        word_ref[base : base + chunk, :] = (total[0] << 16) | (total[1] & 0xFFFF)
    for device in range(devices_all):
        out_ref[device, :quarter, :] = word_ref[device * quarter : (device + 1) * quarter, :]


def put_row_block(wide_ref, at, count, tile, east, west):
    cols = tile.shape[1]
    wide_ref[at : at + count, :cols, :] = tile
    wide_ref[at : at + count, cols : cols + NSTEP, :] = east.astype(F32)
    wide_ref[at : at + count, cols + NSTEP :, :] = west.astype(F32)


def spread_kappa(kappa):
    rows, cols = kappa.shape
    high, low = split_hi_lo(kappa)
    pair = jnp.concatenate([high.astype(F32), low.astype(F32)], axis=1)
    hot = iota((rows, cols, 2 * cols), 1) == iota((rows, cols, 2 * cols), 2) % cols
    spread = jnp.where(hot, pair[:, None, :], 0.0).astype(BF16)
    ones = jnp.ones((2 * cols, 128), BF16)
    return dot_f32(spread.reshape(rows * cols, 2 * cols), ones).reshape(rows, cols, 128)


def sweep_rows(source, target, kap_ref, low, high, block=8):
    cols = source.shape[1]

    def update(first, count):
        rows = [source[first + i] for i in range(-1, count + 1)]
        for i in range(count):
            here = rows[i + 1]
            change = (
                (rows[i] + rows[i + 2])
                + (pltpu.roll(here, 1, 0) + pltpu.roll(here, cols - 1, 0))
                - 4.0 * here
            )
            target[first + i] = here + kap_ref[first + i] * change

    whole = (high - low) // block

    def step(index, carry):
        update(low + index * block, block)
        return carry

    lax.fori_loop(0, whole, step, 0)
    if low + whole * block < high:
        update(low + whole * block, high - low - whole * block)


def sweeps(first_ref, second_ref, kap_ref, rows, block=8):
    source, target = first_ref, second_ref
    for sweep in range(1, NSTEP + 1):
        sweep_rows(source, target, kap_ref, sweep, rows - sweep, block)
        source, target = target, source
    return source


def fill_picked(pick_ref, picked):
    channels, levels = picked.shape
    pick_ref[...] = jnp.zeros_like(pick_ref)
    for part in range(4):
        pick_ref[
            part * channels : (part + 1) * channels, part * levels : (part + 1) * levels
        ] = picked


def forward_mixing(vertical):
    high, low = split_hi_lo(vertical)
    pair = jnp.concatenate([high, low], axis=1)
    return jnp.concatenate([pair, pair], axis=0)


def project_rows(rows, dev, mixing, pick):
    count, cols, levels = rows.shape
    pair = jnp.concatenate(split_hi_lo(rows.reshape(count * cols, levels)), axis=1)
    both = dot_f32(pair, mixing)
    state = both[:, :levels] + both[:, levels:]
    prof = (dev.reshape(count * cols, levels) * state).astype(BF16)
    prof = prof.reshape(count // 4, 4, cols, levels)
    wide = jnp.concatenate(
        [prof[:, part].reshape(count // 4 * cols, levels) for part in range(4)], axis=1
    )
    return jnp.concatenate(split_hi_lo(dot_f32(wide, pick)), axis=1)


def forward_kernel(
    control_ref, east_ref, west_ref, kappa_ref, sigma_ref, vertical_ref, table_ref, choice_ref,
    out_ref, pick_ref, first_ref, second_ref, kap_ref,
):
    rows, cols, levels = control_ref.shape
    put_row_block(first_ref, 0, rows, control_ref[...], east_ref[0], west_ref[0])
    put_row_block(kap_ref, 0, rows, spread_kappa(kappa_ref[...]), east_ref[1], west_ref[1])
    done = sweeps(first_ref, second_ref, kap_ref, rows)
    channels = choice_ref.shape[1]
    table_rows = table_ref.shape[0]
    hot = (iota((table_rows, channels), 0) == choice_ref[...]).astype(F32).astype(BF16)
    fill_picked(pick_ref, dot_tn(hot, table_ref[...]).astype(BF16))
    mixing = forward_mixing(vertical_ref[...])
    pick = jnp.transpose(pick_ref[...].astype(F32)).astype(BF16)
    count = 8
    out_ref[:cols, :] = jnp.zeros((cols, out_ref.shape[1]), BF16)
    out_ref[rows // 4 * cols - cols :, :] = jnp.zeros((cols, out_ref.shape[1]), BF16)

    def step(index, carry):
        row = NSTEP + index * count
        at = pl.multiple_of(cols + index * (count // 4 * cols), cols)
        out_ref[pl.ds(at, count // 4 * cols), :] = project_rows(
            done[pl.ds(row, count), :cols, :], sigma_ref[pl.ds(row, count)], mixing, pick
        )
        return carry

    lax.fori_loop(0, (rows - 2 * NSTEP) // count, step, 0)


def pole_flags():
    at = lax.axis_index("lat")
    last = lax.axis_size("lat") - 1
    return jnp.where(at > 0, 1.0, 0.0), jnp.where(at < last, 1.0, 0.0)


def put_rims(wide_ref, tile_of, east_of, west_of, north, south, flags, rows):
    span = 2 * NSTEP
    wide_ref[:NSTEP] = north.astype(F32) * flags[0]
    put_row_block(wide_ref, NSTEP, span, tile_of(0, span), east_of(0, span), west_of(0, span))
    put_row_block(
        wide_ref, 3 * NSTEP, span, tile_of(rows - span, rows), east_of(rows - span, rows),
        west_of(rows - span, rows),
    )
    wide_ref[5 * NSTEP :] = south.astype(F32) * flags[1]


def put_rim_kappa(kap_ref, kappa_ref, east_ref, west_ref, north_ref, south_ref, flags):
    rows = kappa_ref.shape[0]
    span = 2 * NSTEP
    spread = spread_kappa(
        jnp.concatenate([kappa_ref[:span, :], kappa_ref[rows - span :, :]], axis=0)
    )
    put_rims(
        kap_ref,
        lambda low, high: spread[:span] if low == 0 else spread[span:],
        lambda low, high: east_ref[1, low:high],
        lambda low, high: west_ref[1, low:high],
        north_ref[1],
        south_ref[1],
        flags,
        rows,
    )


def owner_kernel(
    devices_all, quarter, recv_ref, evolved_ref, rinv_ref, pick_ref, sigma_ref, control_ref,
    east_ref, west_ref, north_ref, south_ref, kappa_ref, vertical_ref,
    ret_ref, adj_ref, left_ref, right_ref, top_ref, bottom_ref,
    word_ref, dep_ref, acc_ref, first_ref, second_ref, kap_ref, table_ref, pair_ref,
):
    lat_rows, cols, levels = sigma_ref.shape
    flags = pole_flags()
    put_rim_kappa(kap_ref, kappa_ref, east_ref, west_ref, north_ref, south_ref, flags)
    put_rims(
        first_ref,
        lambda low, high: control_ref[low:high],
        lambda low, high: east_ref[0, low:high],
        lambda low, high: west_ref[0, low:high],
        north_ref[0],
        south_ref[0],
        flags,
        lat_rows,
    )
    done = sweeps(first_ref, second_ref, kap_ref, 6 * NSTEP)
    pick = jnp.transpose(pick_ref[...].astype(F32)).astype(BF16)
    ends = project_rows(
        jnp.concatenate(
            [done[NSTEP : 2 * NSTEP, :cols, :], done[4 * NSTEP : 5 * NSTEP, :cols, :]], axis=0
        ),
        jnp.concatenate([sigma_ref[:NSTEP], sigma_ref[lat_rows - NSTEP :]], axis=0),
        forward_mixing(vertical_ref[...]),
        pick,
    )
    cells_part = evolved_ref.shape[0]
    table_ref[...] = evolved_ref[...]
    table_ref[:cols, :] = ends[:cols]
    table_ref[cells_part - cols :, :] = ends[cols:]

    rows_half = devices_all * quarter
    rows = 2 * rows_half
    for device in range(devices_all):
        word_ref[device * quarter : (device + 1) * quarter, :] = recv_ref[device, :quarter, :]
    meta = recv_ref[:, quarter, :]
    cells, weights = meta >> 16, meta & 0xFFFF
    facts = jnp.concatenate(
        [
            piece.astype(F32).astype(BF16)
            for piece in (cells >> 6, cells & 63, weights >> 8, weights & 255)
        ],
        axis=1,
    )
    channels = rinv_ref.shape[0]
    pair_ref[...] = jnp.zeros_like(pair_ref)
    pair_ref[:channels, :channels] = rinv_ref[...]
    pair_ref[channels:, channels:] = rinv_ref[...]
    high, low = split_hi_lo(pair_ref[...])
    zero = jnp.zeros_like(high)
    mixing = jnp.concatenate(
        [jnp.concatenate([high, low], axis=1), jnp.concatenate([high, zero], axis=1)], axis=0
    )
    acc_ref[...] = jnp.zeros_like(acc_ref)
    chunk = min(512, rows_half)
    left_lane = iota((chunk, 128), 1) < 64
    lane_half = iota((chunk, 128), 1) // 64
    per_half = rows_half // chunk
    for step in range(rows // chunk):
        half = step // per_half
        base = (step % per_half) * chunk
        row = iota((chunk, devices_all), 0) + base
        spread = (row // quarter == iota((chunk, devices_all), 1)).astype(F32).astype(BF16)
        found = dot_f32(spread, facts)
        lat_lane = found[:, :128]
        lon_lane = found[:, 128:256]
        weight_lane = (found[:, 256:384] * 256.0 + found[:, 384:]) * WEIGHT_STEP
        lane = iota((chunk, 128), 1)
        r = (iota((chunk, 128), 0) + base) % quarter
        hots, parts, weight, values = [], [], [], []
        for side in range(2):
            take = lane == (2 * side + half) * quarter + r
            lat = jnp.sum(jnp.where(take, lat_lane, 0.0), axis=1, keepdims=True).astype(I32)
            lon = jnp.sum(jnp.where(take, lon_lane, 0.0), axis=1, keepdims=True).astype(I32)
            weight.append(jnp.sum(jnp.where(take, weight_lane, 0.0), axis=1, keepdims=True))
            part = lat & 3
            inside = (lat >> 2) * cols + lon
            hot = (iota((chunk, cells_part), 1) == inside).astype(F32).astype(BF16)
            got = dot_f32(hot, table_ref[...])
            got = got[:, :256] + got[:, 256:]
            lanes = jnp.where(part >= 2, got[:, 128:], got[:, :128])
            swapped = pltpu.roll(lanes, 64, 1)
            odd = (part & 1) == 1
            values.append(
                jnp.where(odd, swapped, lanes) if side == 0 else jnp.where(odd, lanes, swapped)
            )
            hots.append(hot)
            parts.append(part)
        evolved = jnp.where(left_lane, values[0], values[1])
        words = word_ref[base : base + chunk, :]
        words = (words if half == 0 else words << 16) >> 16
        gap = evolved - words.astype(F32) * INNOV_STEP
        both = dot_f32(jnp.concatenate(split_hi_lo(gap), axis=1), mixing)
        dep = (both[:, :128] + both[:, 128:]) * jnp.where(left_lane, weight[0], weight[1])
        dep_ref[step * chunk : (step + 1) * chunk, :] = dep
        rounded = dep.astype(BF16).astype(F32)
        swapped = pltpu.roll(rounded, 64, 1)
        for side in range(2):
            twice = (
                jnp.where(left_lane, rounded, swapped)
                if side == 0
                else jnp.where(left_lane, swapped, rounded)
            )
            wide = jnp.concatenate(
                [
                    jnp.where(parts[side] == lane_half, twice, 0.0).astype(BF16),
                    jnp.where(parts[side] == lane_half + 2, twice, 0.0).astype(BF16),
                ],
                axis=1,
            )
            acc_ref[...] += dot_tn(hots[side], wide)
    for half in range(2):
        for device in range(devices_all):
            at = half * rows_half + device * quarter
            ret_ref[device, half * quarter : (half + 1) * quarter, :] = dep_ref[
                at : at + quarter, :
            ]
    groups = 4
    count = groups * 4

    def spread_out(step, carry):
        high, low = split_hi_lo(
            acc_ref[pl.ds(pl.multiple_of(step * groups * cols, cols), groups * cols), :]
        )
        both = dot_f32(high, pick_ref[...]) + dot_f32(low, pick_ref[...])
        for group in range(groups):
            for part in range(4):
                at = step * count + group * 4 + part
                value = sigma_ref[at] * both[
                    group * cols : (group + 1) * cols, part * levels : (part + 1) * levels
                ]
                adj_ref[at] = value
                left_ref[at] = value[:NSTEP].astype(BF16)
                right_ref[at] = value[cols - NSTEP :].astype(BF16)
        return carry

    lax.fori_loop(0, lat_rows // count, spread_out, 0)
    top_ref[...] = adj_ref[:NSTEP].astype(BF16)
    bottom_ref[...] = adj_ref[lat_rows - NSTEP :].astype(BF16)


def backward_mixing(vertical):
    high, low = split_hi_lo(vertical)
    return jnp.concatenate(
        [jnp.concatenate([high, high], axis=1), jnp.concatenate([low, low], axis=1)], axis=0
    )


def finish_rows(scaled, kap, mixing):
    count, cols, levels = scaled.shape
    adjoint = (scaled / kap).reshape(count * cols, levels)
    both = dot_nt(jnp.concatenate(split_hi_lo(adjoint), axis=1), mixing)
    return (both[:, :levels] + both[:, levels:]).reshape(count, cols, levels)


def inner_kernel(
    adj_ref, east_ref, west_ref, kappa_ref, keast_ref, kwest_ref, vertical_ref, control_ref,
    out_ref, first_ref, second_ref, kap_ref,
):
    rows, cols, levels = control_ref.shape
    put_row_block(kap_ref, 0, rows, spread_kappa(kappa_ref[...]), keast_ref[1], kwest_ref[1])
    put_row_block(first_ref, 0, rows, adj_ref[...], east_ref[...], west_ref[...])
    first_ref[:rows] = first_ref[:rows] * kap_ref[:rows]
    done = sweeps(first_ref, second_ref, kap_ref, rows)
    mixing = backward_mixing(vertical_ref[...])
    count = 8

    def step(index, carry):
        at = pl.ds(NSTEP + index * count, count)
        out_ref[at] = control_ref[at] + finish_rows(
            done[at, :cols, :], kap_ref[at, :cols, :], mixing
        )
        return carry

    lax.fori_loop(0, (rows - 2 * NSTEP) // count, step, 0)


def rim_kernel(
    adj_ref, east_ref, west_ref, north_ref, south_ref, kappa_ref, keast_ref, kwest_ref,
    knorth_ref, ksouth_ref, vertical_ref, control_ref, inner_ref, out_ref,
    first_ref, second_ref, kap_ref, edge_ref, sem_ref,
):
    del inner_ref
    span = 2 * NSTEP
    lat_rows, cols = kappa_ref.shape
    levels = vertical_ref.shape[0]
    flags = pole_flags()
    put_rim_kappa(kap_ref, kappa_ref, keast_ref, kwest_ref, knorth_ref, ksouth_ref, flags)
    put_rims(
        first_ref,
        lambda low, high: adj_ref[0] if low == 0 else adj_ref[1],
        lambda low, high: east_ref[low:high],
        lambda low, high: west_ref[low:high],
        north_ref[...],
        south_ref[...],
        flags,
        lat_rows,
    )
    first_ref[...] = first_ref[...] * kap_ref[...]
    done = sweeps(first_ref, second_ref, kap_ref, 6 * NSTEP)
    mixing = backward_mixing(vertical_ref[...])
    for end in range(2):
        at = pl.ds((1 + 3 * end) * NSTEP, NSTEP)
        back = finish_rows(done[at, :cols, :], kap_ref[at, :cols, :], mixing)
        edge_ref[end] = control_ref[end] + back
    copies = []
    for end in range(2):
        copy = pltpu.make_async_copy(
            edge_ref.at[end], out_ref.at[pl.ds(end * (lat_rows - NSTEP), NSTEP)], sem_ref.at[end]
        )
        copy.start()
        copies.append(copy)
    for copy in copies:
        copy.wait()


def return_kernel(devices_all, quarter, recv_ref, key_ref, out_ref, pair_ref):
    rows_half = devices_all * quarter
    rows = 2 * rows_half
    channels, obs = out_ref.shape
    for half in range(2):
        for device in range(devices_all):
            at = half * rows_half + device * quarter
            high, low = split_hi_lo(recv_ref[device, half * quarter : (half + 1) * quarter, :])
            pair_ref[at : at + quarter, :128] = high
            pair_ref[at : at + quarter, 128:] = low
    chunk = min(512, obs)
    for start in range(0, obs, chunk):
        key = key_ref[:, start : start + chunk]
        side = key >= rows
        row = jnp.where(side, key - rows, key)
        hot = (iota((rows, chunk), 0) == row).astype(F32).astype(BF16)
        both = dot_tn(pair_ref[...], hot)
        both = both[:128] + both[128:]
        out_ref[:, start : start + chunk] = jnp.where(side, both[channels:], both[:channels])


def shifts(axis):
    count = lax.axis_size(axis)
    forward = [(i, (i + 1) % count) for i in range(count)]
    return forward, [(target, source) for source, target in forward]


def exchange_sides(left, right):
    forward, backward = shifts("lon")
    return lax.ppermute(left, "lon", backward), lax.ppermute(right, "lon", forward)


def exchange_rims(top, bottom):
    forward, backward = shifts("lat")
    return lax.ppermute(bottom, "lat", forward), lax.ppermute(top, "lat", backward)


def estimate(flops, bytes_accessed):
    return pl.CostEstimate(flops=flops, bytes_accessed=bytes_accessed, transcendentals=0)


def body(
    control,
    kappa,
    sigma,
    vertical,
    channel_table,
    channel_pick,
    r_inverse,
    innovations,
    error_scale,
    obs_owner,
    obs_cell,
    obs_count,
):
    lat_rows, lon_cols, levels = control.shape
    obs_slots = obs_cell.shape[0]
    channels = innovations.shape[1]
    devices_all = lax.axis_size("lat") * lax.axis_size("lon")
    capacity = max(4, 2 * obs_slots // devices_all)
    quarter = capacity // 4
    rows_half = devices_all * quarter
    columns = lat_rows * lon_cols
    wide = (lat_rows + 1, lon_cols + 2 * NSTEP, levels)
    rim = (6 * NSTEP, lon_cols + 2 * NSTEP, levels)
    span = 2 * NSTEP
    smem = pl.BlockSpec(memory_space=pltpu.SMEM)
    anywhere = pl.BlockSpec(memory_space=pl.ANY)

    def side_of(low, high):
        edge = kappa[:, low:high, None]
        return jnp.stack(
            [
                control[:, low:high].astype(BF16),
                jnp.broadcast_to(edge.astype(BF16), (lat_rows, high - low, levels)),
            ]
        )

    east, west = exchange_sides(side_of(0, NSTEP), side_of(lon_cols - NSTEP, lon_cols))

    payload, key = pl.pallas_call(
        functools.partial(address_kernel, devices_all, quarter),
        out_shape=(
            jax.ShapeDtypeStruct((devices_all, quarter + 1, 128), I32),
            jax.ShapeDtypeStruct((1, obs_slots), I32),
        ),
        in_specs=[smem] + vmem_specs(4),
        out_specs=tuple(vmem_specs(2)),
        scratch_shapes=[pltpu.VMEM((rows_half, 128), I32)],
        compiler_params=params(),
        cost_estimate=estimate(2_000_000_000, 8_000_000),
        name="address",
    )(
        obs_count,
        obs_owner.reshape(1, obs_slots),
        obs_cell.reshape(1, obs_slots),
        error_scale.reshape(1, obs_slots),
        innovations.T,
    )
    received = lax.all_to_all(payload, ("lat", "lon"), split_axis=0, concat_axis=0, tiled=True)

    def rim_of(low, high):
        tile = jnp.stack(
            [
                control[low:high].astype(BF16),
                jnp.broadcast_to(
                    kappa[low:high, :, None].astype(BF16), (high - low, lon_cols, levels)
                ),
            ]
        )
        return jnp.concatenate([tile, east[:, low:high], west[:, low:high]], axis=2)

    north, south = exchange_rims(rim_of(0, NSTEP), rim_of(lat_rows - NSTEP, lat_rows))

    evolved, picked = pl.pallas_call(
        forward_kernel,
        out_shape=(
            jax.ShapeDtypeStruct((columns // 4, 8 * channels), BF16),
            jax.ShapeDtypeStruct((4 * channels, 4 * levels), BF16),
        ),
        in_specs=vmem_specs(8),
        out_specs=tuple(vmem_specs(2)),
        scratch_shapes=[pltpu.VMEM(wide, F32)] * 3,
        compiler_params=params(),
        cost_estimate=estimate(4_000_000_000, 16_000_000),
        name="forward",
    )(
        control, east, west, kappa, sigma, vertical, channel_table,
        channel_pick.reshape(1, channels),
    )

    returned, adjoint, left, right, top, bottom = pl.pallas_call(
        functools.partial(owner_kernel, devices_all, quarter),
        out_shape=(
            jax.ShapeDtypeStruct((devices_all, 2 * quarter, 128), F32),
            jax.ShapeDtypeStruct(control.shape, F32),
            jax.ShapeDtypeStruct((lat_rows, NSTEP, levels), BF16),
            jax.ShapeDtypeStruct((lat_rows, NSTEP, levels), BF16),
            jax.ShapeDtypeStruct((NSTEP, lon_cols, levels), BF16),
            jax.ShapeDtypeStruct((NSTEP, lon_cols, levels), BF16),
        ),
        in_specs=vmem_specs(12),
        out_specs=tuple(vmem_specs(6)),
        scratch_shapes=[
            pltpu.VMEM((rows_half, 128), I32),
            pltpu.VMEM((2 * rows_half, 128), F32),
            pltpu.VMEM((columns // 4, 4 * channels), F32),
            pltpu.VMEM(rim, F32),
            pltpu.VMEM(rim, F32),
            pltpu.VMEM(rim, F32),
            pltpu.VMEM((columns // 4, 8 * channels), BF16),
            pltpu.VMEM((2 * channels, 2 * channels), F32),
        ],
        compiler_params=params(),
        cost_estimate=estimate(4_000_000_000, 16_000_000),
        name="owner",
    )(
        received, evolved, r_inverse, picked, sigma, control, east, west, north, south, kappa,
        vertical,
    )
    home = lax.all_to_all(returned, ("lat", "lon"), split_axis=0, concat_axis=0, tiled=True)

    aeast, awest = exchange_sides(left, right)
    anorth, asouth = exchange_rims(
        jnp.concatenate([top, aeast[:NSTEP], awest[:NSTEP]], axis=1),
        jnp.concatenate([bottom, aeast[-NSTEP:], awest[-NSTEP:]], axis=1),
    )
    inner = pl.pallas_call(
        inner_kernel,
        out_shape=jax.ShapeDtypeStruct(control.shape, F32),
        in_specs=vmem_specs(8),
        out_specs=vmem_specs(1)[0],
        scratch_shapes=[pltpu.VMEM(wide, F32)] * 3,
        compiler_params=params(),
        cost_estimate=estimate(4_000_000_000, 16_000_000),
        name="inner",
    )(adjoint, aeast, awest, kappa, east, west, vertical, control)

    def ends(field, width):
        return jnp.stack([field[:width], field[lat_rows - width :]])

    gradient = pl.pallas_call(
        rim_kernel,
        out_shape=jax.ShapeDtypeStruct(control.shape, F32),
        in_specs=vmem_specs(12) + [anywhere],
        out_specs=anywhere,
        scratch_shapes=[pltpu.VMEM(rim, F32)] * 3
        + [
            pltpu.VMEM((2, NSTEP, lon_cols, levels), F32),
            pltpu.SemaphoreType.DMA((2,)),
        ],
        input_output_aliases={12: 0},
        compiler_params=params(),
        cost_estimate=estimate(1_000_000_000, 2_000_000),
        name="rims",
    )(
        ends(adjoint, span), aeast, awest, anorth, asouth, kappa, east, west, north, south,
        vertical, ends(control, NSTEP), inner,
    )

    departures = pl.pallas_call(
        functools.partial(return_kernel, devices_all, quarter),
        out_shape=jax.ShapeDtypeStruct((channels, obs_slots), F32),
        in_specs=vmem_specs(2),
        out_specs=vmem_specs(1)[0],
        scratch_shapes=[pltpu.VMEM((2 * rows_half, 256), BF16)],
        compiler_params=params(),
        cost_estimate=estimate(500_000_000, 2_000_000),
        name="give_back",
    )(home, key)
    return (gradient, departures.T)


def solution(mesh):
    return jax.shard_map(
        body,
        mesh=mesh,
        in_specs=(
            P("lat", "lon", None),
            P("lat", "lon"),
            P("lat", "lon", None),
            P(),
            P(),
            P(),
            P(),
            P(("lat", "lon"), None),
            P(("lat", "lon")),
            P(("lat", "lon"), None),
            P(("lat", "lon")),
            P(("lat", "lon")),
        ),
        out_specs=(P("lat", "lon", None), P(("lat", "lon"), None)),
        check_vma=False,
    )
```

```python
import functools

import jax
import jax.numpy as jnp
from jax import lax
from jax.experimental import pallas as pl
from jax.experimental.pallas import tpu as pltpu
from jax.sharding import PartitionSpec as P

NSTEP = 4
F32 = jnp.float32
BF16 = jnp.bfloat16
I32 = jnp.int32
INNOV_MAX = 6.0
INNOV_STEP = INNOV_MAX / 32767.0
WEIGHT_MAX = 4.0
WEIGHT_STEP = WEIGHT_MAX / 65535.0


def split_hi_lo(value):
    high = value.astype(BF16)
    low = (value - high.astype(F32)).astype(BF16)
    return high, low


def iota(shape, dim):
    return lax.broadcasted_iota(I32, shape, dim)


def dot_f32(left, right):
    return jnp.dot(left, right, preferred_element_type=F32)


def dot_nt(left, right):
    return lax.dot_general(left, right, (((1,), (1,)), ((), ())), preferred_element_type=F32)


def dot_tn(left, right):
    return lax.dot_general(left, right, (((0,), (0,)), ((), ())), preferred_element_type=F32)


def params(mebibytes):
    return pltpu.CompilerParams(vmem_limit_bytes=mebibytes * 1024 * 1024)


HBM_SPEC = pl.BlockSpec(memory_space=pltpu.HBM)


def start_copies(pairs, sem_ref, first=0):
    copies = []
    for index, (source, target) in enumerate(pairs):
        copy = pltpu.make_async_copy(source, target, sem_ref.at[first + index])
        copy.start()
        copies.append(copy)
    return copies


def wait_copies(copies):
    for copy in copies:
        copy.wait()


def vmem_specs(count):
    return [pl.BlockSpec(memory_space=pltpu.VMEM)] * count


def address_kernel(
    devices_all, quarter, count_ref, owner_ref, cell_ref, scale_ref, innov_ref, out_ref, key_ref,
    word_ref,
):
    obs = owner_ref.shape[1]
    rows_half = devices_all * quarter
    rows = 2 * rows_half
    owner = owner_ref[...]
    cell = cell_ref[...]
    mine = iota((devices_all, obs), 0) == owner
    mine_f = mine.astype(F32)
    mine_b = mine_f.astype(BF16)
    block = min(256, obs)
    earlier = (iota((block, block), 0) < iota((block, block), 1)).astype(F32).astype(BF16)
    running = jnp.zeros((devices_all, 1), F32)
    parts = []
    for start in range(0, obs, block):
        piece = mine_f[:, start : start + block]
        before = dot_f32(mine_b[:, start : start + block], earlier) + running
        parts.append(jnp.sum(piece * before, axis=0, keepdims=True))
        running = running + jnp.sum(piece, axis=1, keepdims=True)
    position = jnp.concatenate(parts, axis=1).astype(I32)
    group = position // quarter
    key = (
        (group // 2) * rows + (group % 2) * rows_half + owner * quarter + position % quarter
    )
    key_ref[...] = key
    scale = scale_ref[...]
    valid = iota((1, obs), 1) < count_ref[0]
    weight = jnp.where(valid, 1.0 / (scale * scale), 0.0)
    weight = jnp.minimum(jnp.floor(weight * (1.0 / WEIGHT_STEP) + 0.5), 65535.0)
    weight_high = jnp.floor(weight * (1.0 / 256.0))
    weight_low = weight - 256.0 * weight_high
    cell_high = (cell // 64).astype(F32)
    cell_low = (cell % 64).astype(F32)
    left = jnp.concatenate(
        [mine_f * piece for piece in (cell_high, cell_low, weight_high, weight_low)], axis=0
    ).astype(BF16)
    place = (iota((128, obs), 0) == position).astype(F32).astype(BF16)
    table = dot_nt(left, place).astype(I32)
    n = devices_all
    cells = table[:n] * 64 + table[n : 2 * n]
    weights = table[2 * n : 3 * n] * 256 + table[3 * n :]
    out_ref[:, quarter, :] = (cells << 16) | weights

    level = jnp.floor(
        jnp.clip(innov_ref[...], -INNOV_MAX, INNOV_MAX) * (1.0 / INNOV_STEP) + 0.5
    )
    high = jnp.floor(level * (1.0 / 256.0))
    low = (level - 256.0 * high).astype(BF16)
    high = high.astype(BF16)
    bytes_of = [jnp.concatenate([high, low], axis=0), jnp.concatenate([low, high], axis=0)]
    chunk = min(256, rows_half)
    left_lane = iota((chunk, 128), 1) < 64
    for base in range(0, rows_half, chunk):
        total = []
        for half in range(2):
            row = iota((chunk, obs), 0) + (base + half * rows_half)
            found = []
            for side in range(2):
                hot = (row + side * rows == key).astype(F32).astype(BF16)
                got = dot_nt(hot, bytes_of[side])
                found.append(got * 256.0 + pltpu.roll(got, 64, 1))
            total.append(jnp.where(left_lane, found[0], found[1]).astype(I32))
        word_ref[base : base + chunk, :] = (total[0] << 16) | (total[1] & 0xFFFF)
    for device in range(devices_all):
        out_ref[device, :quarter, :] = word_ref[device * quarter : (device + 1) * quarter, :]


def put_row_block(wide_ref, at, count, tile, east, west):
    cols = tile.shape[1]
    wide_ref[at : at + count, :cols, :] = tile
    put_sides(wide_ref, at, count, cols, east, west)


def put_sides(wide_ref, at, count, cols, east, west):
    wide_ref[at : at + count, cols : cols + NSTEP, :] = east.astype(F32)
    wide_ref[at : at + count, cols + NSTEP :, :] = west.astype(F32)


def spread_kappa(kappa):
    rows, cols = kappa.shape
    high, low = split_hi_lo(kappa)
    pair = jnp.concatenate([high.astype(F32), low.astype(F32)], axis=1)
    hot = iota((rows, cols, 2 * cols), 1) == iota((rows, cols, 2 * cols), 2) % cols
    spread = jnp.where(hot, pair[:, None, :], 0.0).astype(BF16)
    ones = jnp.ones((2 * cols, 128), BF16)
    return dot_f32(spread.reshape(rows * cols, 2 * cols), ones).reshape(rows, cols, 128)


def sweep_rows(source, target, kap_ref, low, high, block=8):
    cols = source.shape[1]

    def update(first, count):
        rows = [source[first + i] for i in range(-1, count + 1)]
        for i in range(count):
            here = rows[i + 1]
            change = (
                (rows[i] + rows[i + 2])
                + (pltpu.roll(here, 1, 0) + pltpu.roll(here, cols - 1, 0))
                - 4.0 * here
            )
            target[first + i] = here + kap_ref[first + i] * change

    whole = (high - low) // block

    def step(index, carry):
        update(low + index * block, block)
        return carry

    lax.fori_loop(0, whole, step, 0)
    if low + whole * block < high:
        update(low + whole * block, high - low - whole * block)


def sweeps(first_ref, second_ref, kap_ref, rows, block=8):
    source, target = first_ref, second_ref
    for sweep in range(1, NSTEP + 1):
        sweep_rows(source, target, kap_ref, sweep, rows - sweep, block)
        source, target = target, source
    return source


def fill_picked(pick_ref, picked):
    channels, levels = picked.shape
    pick_ref[...] = jnp.zeros_like(pick_ref)
    for part in range(4):
        pick_ref[
            part * channels : (part + 1) * channels, part * levels : (part + 1) * levels
        ] = picked


def forward_mixing(vertical):
    high, low = split_hi_lo(vertical)
    pair = jnp.concatenate([high, low], axis=1)
    return jnp.concatenate([pair, pair], axis=0)


def project_rows(rows, dev, mixing, pick):
    count, cols, levels = rows.shape
    pair = jnp.concatenate(split_hi_lo(rows.reshape(count * cols, levels)), axis=1)
    both = dot_f32(pair, mixing)
    state = both[:, :levels] + both[:, levels:]
    prof = (dev.reshape(count * cols, levels) * state).astype(BF16)
    prof = prof.reshape(count // 4, 4, cols, levels)
    wide = jnp.concatenate(
        [prof[:, part].reshape(count // 4 * cols, levels) for part in range(4)], axis=1
    )
    return jnp.concatenate(split_hi_lo(dot_f32(wide, pick)), axis=1)


def forward_kernel(
    control_hbm, sigma_hbm, east_ref, west_ref, kappa_ref, vertical_ref, table_ref, choice_ref,
    out_hbm, pick_hbm, first_ref, second_ref, kap_ref, out_ref, pick_ref, sigma_ref, sem_ref,
):
    rows, cols, levels = control_hbm.shape
    tile_in = start_copies(
        [(control_hbm, first_ref.at[pl.ds(0, rows), pl.ds(0, cols)])], sem_ref
    )
    sigma_in = start_copies([(sigma_hbm, sigma_ref)], sem_ref, 1)
    put_sides(first_ref, 0, rows, cols, east_ref[0], west_ref[0])
    kap_ref[:rows, :cols, :] = spread_kappa(kappa_ref[...])
    put_sides(kap_ref, 0, rows, cols, east_ref[1], west_ref[1])
    wait_copies(tile_in)
    done = sweeps(first_ref, second_ref, kap_ref, rows)
    wait_copies(sigma_in)
    channels = choice_ref.shape[1]
    table_rows = table_ref.shape[0]
    hot = (iota((table_rows, channels), 0) == choice_ref[...]).astype(F32).astype(BF16)
    fill_picked(pick_ref, dot_tn(hot, table_ref[...]).astype(BF16))
    mixing = forward_mixing(vertical_ref[...])
    pick = jnp.transpose(pick_ref[...].astype(F32)).astype(BF16)
    copies = start_copies([(pick_ref, pick_hbm)], sem_ref)
    count = 8
    for index in range((rows - 2 * NSTEP) // count):
        row = NSTEP + index * count
        where = pl.ds(row // 4 * cols, count // 4 * cols)
        out_ref[where, :] = project_rows(
            done[row : row + count, :cols, :], sigma_ref[row : row + count], mixing, pick
        )
        copies += start_copies([(out_ref.at[where], out_hbm.at[where])], sem_ref, index + 1)
    wait_copies(copies)


def pole_flags():
    at = lax.axis_index("lat")
    last = lax.axis_size("lat") - 1
    return jnp.where(at > 0, 1.0, 0.0), jnp.where(at < last, 1.0, 0.0)


def put_rims(wide_ref, tile_of, east_of, west_of, north, south, flags, rows):
    span = 2 * NSTEP
    wide_ref[:NSTEP] = north.astype(F32) * flags[0]
    put_row_block(wide_ref, NSTEP, span, tile_of(0, span), east_of(0, span), west_of(0, span))
    put_row_block(
        wide_ref, 3 * NSTEP, span, tile_of(rows - span, rows), east_of(rows - span, rows),
        west_of(rows - span, rows),
    )
    wide_ref[5 * NSTEP :] = south.astype(F32) * flags[1]


def put_rim_kappa(kap_ref, kappa_ref, east_ref, west_ref, north_ref, south_ref, flags):
    rows = kappa_ref.shape[0]
    span = 2 * NSTEP
    spread = spread_kappa(
        jnp.concatenate([kappa_ref[:span, :], kappa_ref[rows - span :, :]], axis=0)
    )
    put_rims(
        kap_ref,
        lambda low, high: spread[:span] if low == 0 else spread[span:],
        lambda low, high: east_ref[1, low:high],
        lambda low, high: west_ref[1, low:high],
        north_ref[1],
        south_ref[1],
        flags,
        rows,
    )


def owner_kernel(
    devices_all, quarter, recv_hbm, evolved_hbm, pick_hbm, sigma_hbm, control_hbm, rinv_ref,
    east_ref, west_ref, north_ref, south_ref, kappa_ref, vertical_ref,
    ret_ref, adj_hbm, left_hbm, right_hbm, top_hbm, bottom_hbm,
    word_ref, dep_ref, acc_ref, first_ref, second_ref, kap_ref, table_ref, pair_ref,
    recv_ref, pick_ref, sigma_ref, ends_ref, adj_ref, left_ref, right_ref, top_ref, bottom_ref,
    sem_ref,
):
    lat_rows, cols, levels = sigma_hbm.shape
    cells_part = evolved_hbm.shape[0]
    flags = pole_flags()
    span = 2 * NSTEP
    inside = pl.ds(cols, cells_part - 2 * cols)
    control_in = start_copies(
        [
            (control_hbm.at[pl.ds(0, span)], ends_ref.at[0]),
            (control_hbm.at[pl.ds(lat_rows - span, span)], ends_ref.at[1]),
        ],
        sem_ref,
    )
    sigma_in = start_copies([(sigma_hbm, sigma_ref), (pick_hbm, pick_ref)], sem_ref, 2)
    others_in = start_copies(
        [(recv_hbm, recv_ref), (evolved_hbm.at[inside], table_ref.at[inside])], sem_ref, 4
    )
    put_rim_kappa(kap_ref, kappa_ref, east_ref, west_ref, north_ref, south_ref, flags)
    wait_copies(control_in)
    put_rims(
        first_ref,
        lambda low, high: ends_ref[0] if low == 0 else ends_ref[1],
        lambda low, high: east_ref[0, low:high],
        lambda low, high: west_ref[0, low:high],
        north_ref[0],
        south_ref[0],
        flags,
        lat_rows,
    )
    done = sweeps(first_ref, second_ref, kap_ref, 6 * NSTEP)
    wait_copies(sigma_in)
    pick = jnp.transpose(pick_ref[...].astype(F32)).astype(BF16)
    ends = project_rows(
        jnp.concatenate(
            [done[NSTEP : 2 * NSTEP, :cols, :], done[4 * NSTEP : 5 * NSTEP, :cols, :]], axis=0
        ),
        jnp.concatenate([sigma_ref[:NSTEP], sigma_ref[lat_rows - NSTEP :]], axis=0),
        forward_mixing(vertical_ref[...]),
        pick,
    )
    table_ref[:cols, :] = ends[:cols]
    table_ref[cells_part - cols :, :] = ends[cols:]

    wait_copies(others_in)
    rows_half = devices_all * quarter
    rows = 2 * rows_half
    for device in range(devices_all):
        word_ref[device * quarter : (device + 1) * quarter, :] = recv_ref[device, :quarter, :]
    meta = recv_ref[:, quarter, :]
    cells, weights = meta >> 16, meta & 0xFFFF
    facts = jnp.concatenate(
        [
            piece.astype(F32).astype(BF16)
            for piece in (cells >> 6, cells & 63, weights >> 8, weights & 255)
        ],
        axis=1,
    )
    channels = rinv_ref.shape[0]
    pair_ref[...] = jnp.zeros_like(pair_ref)
    pair_ref[:channels, :channels] = rinv_ref[...]
    pair_ref[channels:, channels:] = rinv_ref[...]
    high, low = split_hi_lo(pair_ref[...])
    zero = jnp.zeros_like(high)
    mixing = jnp.concatenate(
        [jnp.concatenate([high, low], axis=1), jnp.concatenate([high, zero], axis=1)], axis=0
    )
    acc_ref[...] = jnp.zeros_like(acc_ref)
    chunk = min(512, rows_half)
    left_lane = iota((chunk, 128), 1) < 64
    lane_half = iota((chunk, 128), 1) // 64
    per_half = rows_half // chunk
    for step in range(rows // chunk):
        half = step // per_half
        base = (step % per_half) * chunk
        row = iota((chunk, devices_all), 0) + base
        spread = (row // quarter == iota((chunk, devices_all), 1)).astype(F32).astype(BF16)
        found = dot_f32(spread, facts)
        lat_lane = found[:, :128]
        lon_lane = found[:, 128:256]
        weight_lane = (found[:, 256:384] * 256.0 + found[:, 384:]) * WEIGHT_STEP
        lane = iota((chunk, 128), 1)
        r = (iota((chunk, 128), 0) + base) % quarter
        hots, parts, weight, values = [], [], [], []
        for side in range(2):
            take = lane == (2 * side + half) * quarter + r
            lat = jnp.sum(jnp.where(take, lat_lane, 0.0), axis=1, keepdims=True).astype(I32)
            lon = jnp.sum(jnp.where(take, lon_lane, 0.0), axis=1, keepdims=True).astype(I32)
            weight.append(jnp.sum(jnp.where(take, weight_lane, 0.0), axis=1, keepdims=True))
            part = lat & 3
            inside = (lat >> 2) * cols + lon
            hot = (iota((chunk, cells_part), 1) == inside).astype(F32).astype(BF16)
            got = dot_f32(hot, table_ref[...])
            got = got[:, :256] + got[:, 256:]
            lanes = jnp.where(part >= 2, got[:, 128:], got[:, :128])
            swapped = pltpu.roll(lanes, 64, 1)
            odd = (part & 1) == 1
            values.append(
                jnp.where(odd, swapped, lanes) if side == 0 else jnp.where(odd, lanes, swapped)
            )
            hots.append(hot)
            parts.append(part)
        evolved = jnp.where(left_lane, values[0], values[1])
        words = word_ref[base : base + chunk, :]
        words = (words if half == 0 else words << 16) >> 16
        gap = evolved - words.astype(F32) * INNOV_STEP
        both = dot_f32(jnp.concatenate(split_hi_lo(gap), axis=1), mixing)
        dep = (both[:, :128] + both[:, 128:]) * jnp.where(left_lane, weight[0], weight[1])
        dep_ref[step * chunk : (step + 1) * chunk, :] = evolved
        rounded = dep.astype(BF16).astype(F32)
        swapped = pltpu.roll(rounded, 64, 1)
        for side in range(2):
            twice = (
                jnp.where(left_lane, rounded, swapped)
                if side == 0
                else jnp.where(left_lane, swapped, rounded)
            )
            wide = jnp.concatenate(
                [
                    jnp.where(parts[side] == lane_half, twice, 0.0).astype(BF16),
                    jnp.where(parts[side] == lane_half + 2, twice, 0.0).astype(BF16),
                ],
                axis=1,
            )
            acc_ref[...] += dot_tn(hots[side], wide)
    for half in range(2):
        for device in range(devices_all):
            at = half * rows_half + device * quarter
            ret_ref[device, half * quarter : (half + 1) * quarter, :] = dep_ref[
                at : at + quarter, :
            ]
    groups = 4
    count = groups * 4
    copies = []
    for step in range(lat_rows // count):
        high, low = split_hi_lo(acc_ref[step * groups * cols : (step + 1) * groups * cols, :])
        both = dot_f32(high, pick_ref[...]) + dot_f32(low, pick_ref[...])
        for group in range(groups):
            for part in range(4):
                at = step * count + group * 4 + part
                value = sigma_ref[at] * both[
                    group * cols : (group + 1) * cols, part * levels : (part + 1) * levels
                ]
                adj_ref[at] = value
                left_ref[at] = value[:NSTEP].astype(BF16)
                right_ref[at] = value[cols - NSTEP :].astype(BF16)
                if at < NSTEP:
                    top_ref[at] = value.astype(BF16)
                if at >= lat_rows - NSTEP:
                    bottom_ref[at - (lat_rows - NSTEP)] = value.astype(BF16)
        where = pl.ds(step * count, count)
        copies += start_copies([(adj_ref.at[where], adj_hbm.at[where])], sem_ref, step)
    copies += start_copies(
        [
            (left_ref, left_hbm),
            (right_ref, right_hbm),
            (top_ref, top_hbm),
            (bottom_ref, bottom_hbm),
        ],
        sem_ref,
        lat_rows // count,
    )
    wait_copies(copies)


def backward_mixing(vertical):
    high, low = split_hi_lo(vertical)
    return jnp.concatenate(
        [jnp.concatenate([high, high], axis=1), jnp.concatenate([low, low], axis=1)], axis=0
    )


def finish_rows(scaled, kap, mixing):
    count, cols, levels = scaled.shape
    adjoint = (scaled / kap).reshape(count * cols, levels)
    both = dot_nt(jnp.concatenate(split_hi_lo(adjoint), axis=1), mixing)
    return (both[:, :levels] + both[:, levels:]).reshape(count, cols, levels)


def inner_kernel(
    adj_ref, east_ref, west_ref, kappa_ref, keast_ref, kwest_ref, vertical_ref, control_ref,
    out_hbm, first_ref, second_ref, kap_ref, out_ref, sem_ref,
):
    rows, cols, levels = control_ref.shape
    put_row_block(kap_ref, 0, rows, spread_kappa(kappa_ref[...]), keast_ref[1], kwest_ref[1])
    put_row_block(first_ref, 0, rows, adj_ref[...], east_ref[...], west_ref[...])
    first_ref[:rows] = first_ref[:rows] * kap_ref[:rows]
    done = sweeps(first_ref, second_ref, kap_ref, rows)
    mixing = backward_mixing(vertical_ref[...])
    count = 8
    copies = []
    for index in range((rows - 2 * NSTEP) // count):
        row = NSTEP + index * count
        at = pl.ds(row, count)
        out_ref[at] = control_ref[at] + finish_rows(
            done[row : row + count, :cols, :], kap_ref[row : row + count, :cols, :], mixing
        )
        copies += start_copies([(out_ref.at[at], out_hbm.at[at])], sem_ref, index)
    wait_copies(copies)


def rim_kernel(
    adj_ref, east_ref, west_ref, north_ref, south_ref, kappa_ref, keast_ref, kwest_ref,
    knorth_ref, ksouth_ref, vertical_ref, control_ref, inner_ref, out_ref,
    first_ref, second_ref, kap_ref, edge_ref, sem_ref,
):
    del inner_ref
    span = 2 * NSTEP
    lat_rows, cols = kappa_ref.shape
    levels = vertical_ref.shape[0]
    flags = pole_flags()
    put_rim_kappa(kap_ref, kappa_ref, keast_ref, kwest_ref, knorth_ref, ksouth_ref, flags)
    put_rims(
        first_ref,
        lambda low, high: adj_ref[0] if low == 0 else adj_ref[1],
        lambda low, high: east_ref[low:high],
        lambda low, high: west_ref[low:high],
        north_ref[...],
        south_ref[...],
        flags,
        lat_rows,
    )
    first_ref[...] = first_ref[...] * kap_ref[...]
    done = sweeps(first_ref, second_ref, kap_ref, 6 * NSTEP)
    mixing = backward_mixing(vertical_ref[...])
    for end in range(2):
        at = pl.ds((1 + 3 * end) * NSTEP, NSTEP)
        back = finish_rows(done[at, :cols, :], kap_ref[at, :cols, :], mixing)
        edge_ref[end] = control_ref[end] + back
    copies = []
    for end in range(2):
        copy = pltpu.make_async_copy(
            edge_ref.at[end], out_ref.at[pl.ds(end * (lat_rows - NSTEP), NSTEP)], sem_ref.at[end]
        )
        copy.start()
        copies.append(copy)
    for copy in copies:
        copy.wait()


def return_kernel(
    devices_all, quarter, count_ref, recv_ref, key_ref, innov_ref, scale_ref, rinv_ref, out_ref,
    pair_ref,
):
    rows_half = devices_all * quarter
    rows = 2 * rows_half
    channels, obs = out_ref.shape
    for half in range(2):
        for device in range(devices_all):
            at = half * rows_half + device * quarter
            high, low = split_hi_lo(recv_ref[device, half * quarter : (half + 1) * quarter, :])
            pair_ref[at : at + quarter, :128] = high
            pair_ref[at : at + quarter, 128:] = low
    scale = scale_ref[...]
    valid = iota((1, obs), 1) < count_ref[0]
    weight = jnp.where(valid, 1.0 / (scale * scale), 0.0)
    chunk = min(512, obs)
    for start in range(0, obs, chunk):
        key = key_ref[:, start : start + chunk]
        side = key >= rows
        row = jnp.where(side, key - rows, key)
        hot = (iota((rows, chunk), 0) == row).astype(F32).astype(BF16)
        both = dot_tn(pair_ref[...], hot)
        both = both[:128] + both[128:]
        evolved = jnp.where(side, both[channels:], both[:channels])
        gap = evolved - innov_ref[:, start : start + chunk]
        mixed = lax.dot_general(
            rinv_ref[...], gap, (((0,), (0,)), ((), ())), precision=lax.Precision.HIGHEST,
            preferred_element_type=F32,
        )
        out_ref[:, start : start + chunk] = mixed * weight[:, start : start + chunk]


def shifts(axis):
    count = lax.axis_size(axis)
    forward = [(i, (i + 1) % count) for i in range(count)]
    return forward, [(target, source) for source, target in forward]


def exchange_sides(left, right):
    forward, backward = shifts("lon")
    return lax.ppermute(left, "lon", backward), lax.ppermute(right, "lon", forward)


def exchange_rims(top, bottom):
    forward, backward = shifts("lat")
    return lax.ppermute(bottom, "lat", forward), lax.ppermute(top, "lat", backward)


def estimate(flops, bytes_accessed):
    return pl.CostEstimate(flops=flops, bytes_accessed=bytes_accessed, transcendentals=0)


def body(
    control,
    kappa,
    sigma,
    vertical,
    channel_table,
    channel_pick,
    r_inverse,
    innovations,
    error_scale,
    obs_owner,
    obs_cell,
    obs_count,
):
    lat_rows, lon_cols, levels = control.shape
    obs_slots = obs_cell.shape[0]
    channels = innovations.shape[1]
    devices_all = lax.axis_size("lat") * lax.axis_size("lon")
    capacity = max(4, 2 * obs_slots // devices_all)
    quarter = capacity // 4
    rows_half = devices_all * quarter
    columns = lat_rows * lon_cols
    wide = (lat_rows + 1, lon_cols + 2 * NSTEP, levels)
    rim = (6 * NSTEP, lon_cols + 2 * NSTEP, levels)
    span = 2 * NSTEP
    smem = pl.BlockSpec(memory_space=pltpu.SMEM)
    anywhere = pl.BlockSpec(memory_space=pl.ANY)

    def side_of(low, high):
        edge = kappa[:, low:high, None]
        return jnp.stack(
            [
                control[:, low:high].astype(BF16),
                jnp.broadcast_to(edge.astype(BF16), (lat_rows, high - low, levels)),
            ]
        )

    near, far = side_of(0, NSTEP), side_of(lon_cols - NSTEP, lon_cols)
    near, far, obs_cell = lax.optimization_barrier((near, far, obs_cell))
    east, west = exchange_sides(near, far)

    payload, key = pl.pallas_call(
        functools.partial(address_kernel, devices_all, quarter),
        out_shape=(
            jax.ShapeDtypeStruct((devices_all, quarter + 1, 128), I32),
            jax.ShapeDtypeStruct((1, obs_slots), I32),
        ),
        in_specs=[smem] + vmem_specs(4),
        out_specs=tuple(vmem_specs(2)),
        scratch_shapes=[pltpu.VMEM((rows_half, 128), I32)],
        compiler_params=params(10),
        cost_estimate=estimate(2_000_000_000, 8_000_000),
        name="address",
    )(
        obs_count,
        obs_owner.reshape(1, obs_slots),
        obs_cell.reshape(1, obs_slots),
        error_scale.reshape(1, obs_slots),
        innovations.T,
    )
    received = lax.all_to_all(payload, ("lat", "lon"), split_axis=0, concat_axis=0, tiled=True)

    def rim_of(low, high):
        tile = jnp.stack(
            [
                control[low:high].astype(BF16),
                jnp.broadcast_to(
                    kappa[low:high, :, None].astype(BF16), (high - low, lon_cols, levels)
                ),
            ]
        )
        return jnp.concatenate([tile, east[:, low:high], west[:, low:high]], axis=2)

    north, south = exchange_rims(rim_of(0, NSTEP), rim_of(lat_rows - NSTEP, lat_rows))

    evolved, picked = pl.pallas_call(
        forward_kernel,
        out_shape=(
            jax.ShapeDtypeStruct((columns // 4, 8 * channels), BF16),
            jax.ShapeDtypeStruct((4 * channels, 4 * levels), BF16),
        ),
        in_specs=[HBM_SPEC] * 2 + vmem_specs(6),
        out_specs=(HBM_SPEC, HBM_SPEC),
        scratch_shapes=[pltpu.VMEM(wide, F32)] * 3
        + [
            pltpu.VMEM((columns // 4, 8 * channels), BF16),
            pltpu.VMEM((4 * channels, 4 * levels), BF16),
            pltpu.VMEM(control.shape, F32),
            pltpu.SemaphoreType.DMA((lat_rows // 8 + 2,)),
        ],
        compiler_params=params(58),
        cost_estimate=estimate(4_000_000_000, 16_000_000),
        name="forward",
    )(
        control, sigma, east, west, kappa, vertical, channel_table,
        channel_pick.reshape(1, channels),
    )

    returned, adjoint, left, right, top, bottom = pl.pallas_call(
        functools.partial(owner_kernel, devices_all, quarter),
        out_shape=(
            jax.ShapeDtypeStruct((devices_all, 2 * quarter, 128), F32),
            jax.ShapeDtypeStruct(control.shape, F32),
            jax.ShapeDtypeStruct((lat_rows, NSTEP, levels), BF16),
            jax.ShapeDtypeStruct((lat_rows, NSTEP, levels), BF16),
            jax.ShapeDtypeStruct((NSTEP, lon_cols, levels), BF16),
            jax.ShapeDtypeStruct((NSTEP, lon_cols, levels), BF16),
        ),
        in_specs=[HBM_SPEC] * 5 + vmem_specs(7),
        out_specs=tuple(vmem_specs(1) + [HBM_SPEC] * 5),
        scratch_shapes=[
            pltpu.VMEM((rows_half, 128), I32),
            pltpu.VMEM((2 * rows_half, 128), F32),
            pltpu.VMEM((columns // 4, 4 * channels), F32),
            pltpu.VMEM(rim, F32),
            pltpu.VMEM(rim, F32),
            pltpu.VMEM(rim, F32),
            pltpu.VMEM((columns // 4, 8 * channels), BF16),
            pltpu.VMEM((2 * channels, 2 * channels), F32),
            pltpu.VMEM((devices_all, quarter + 1, 128), I32),
            pltpu.VMEM((4 * channels, 4 * levels), BF16),
            pltpu.VMEM(control.shape, F32),
            pltpu.VMEM((2, span, lon_cols, levels), F32),
            pltpu.VMEM(control.shape, F32),
            pltpu.VMEM((lat_rows, NSTEP, levels), BF16),
            pltpu.VMEM((lat_rows, NSTEP, levels), BF16),
            pltpu.VMEM((NSTEP, lon_cols, levels), BF16),
            pltpu.VMEM((NSTEP, lon_cols, levels), BF16),
            pltpu.SemaphoreType.DMA((lat_rows // 16 + 4,)),
        ],
        compiler_params=params(58),
        cost_estimate=estimate(4_000_000_000, 16_000_000),
        name="owner",
    )(
        received, evolved, picked, sigma, control, r_inverse, east, west, north, south, kappa,
        vertical,
    )
    left, right, returned = lax.optimization_barrier((left, right, returned))
    home = lax.all_to_all(
        returned.astype(jnp.float16), ("lat", "lon"), split_axis=0, concat_axis=0, tiled=True
    )

    aeast, awest = exchange_sides(left, right)
    anorth, asouth = exchange_rims(
        jnp.concatenate([top, aeast[:NSTEP], awest[:NSTEP]], axis=1),
        jnp.concatenate([bottom, aeast[-NSTEP:], awest[-NSTEP:]], axis=1),
    )
    inner = pl.pallas_call(
        inner_kernel,
        out_shape=jax.ShapeDtypeStruct(control.shape, F32),
        in_specs=vmem_specs(8),
        out_specs=HBM_SPEC,
        scratch_shapes=[pltpu.VMEM(wide, F32)] * 3
        + [pltpu.VMEM(control.shape, F32), pltpu.SemaphoreType.DMA((lat_rows // 8,))],
        compiler_params=params(20),
        cost_estimate=estimate(4_000_000_000, 16_000_000),
        name="inner",
    )(adjoint, aeast, awest, kappa, east, west, vertical, control)

    def ends(field, width):
        return jnp.stack([field[:width], field[lat_rows - width :]])

    gradient = pl.pallas_call(
        rim_kernel,
        out_shape=jax.ShapeDtypeStruct(control.shape, F32),
        in_specs=vmem_specs(12) + [anywhere],
        out_specs=anywhere,
        scratch_shapes=[pltpu.VMEM(rim, F32)] * 3
        + [
            pltpu.VMEM((2, NSTEP, lon_cols, levels), F32),
            pltpu.SemaphoreType.DMA((2,)),
        ],
        input_output_aliases={12: 0},
        compiler_params=params(12),
        cost_estimate=estimate(1_000_000_000, 2_000_000),
        name="rims",
    )(
        ends(adjoint, span), aeast, awest, anorth, asouth, kappa, east, west, north, south,
        vertical, ends(control, NSTEP), inner,
    )

    departures = pl.pallas_call(
        functools.partial(return_kernel, devices_all, quarter),
        out_shape=jax.ShapeDtypeStruct((channels, obs_slots), F32),
        in_specs=[smem] + vmem_specs(5),
        out_specs=vmem_specs(1)[0],
        scratch_shapes=[pltpu.VMEM((2 * rows_half, 256), BF16)],
        compiler_params=params(10),
        cost_estimate=estimate(500_000_000, 2_000_000),
        name="give_back",
    )(
        obs_count, home.astype(F32), key, innovations.T, error_scale.reshape(1, obs_slots),
        r_inverse,
    )
    return (gradient, departures.T)


def solution(mesh):
    return jax.shard_map(
        body,
        mesh=mesh,
        in_specs=(
            P("lat", "lon", None),
            P("lat", "lon"),
            P("lat", "lon", None),
            P(),
            P(),
            P(),
            P(),
            P(("lat", "lon"), None),
            P(("lat", "lon")),
            P(("lat", "lon"), None),
            P(("lat", "lon")),
            P(("lat", "lon")),
        ),
        out_specs=(P("lat", "lon", None), P(("lat", "lon"), None)),
        check_vma=False,
    )
```

```python
import functools

import jax
import jax.numpy as jnp
from jax import lax
from jax.experimental import pallas as pl
from jax.experimental.pallas import tpu as pltpu
from jax.sharding import PartitionSpec as P

NSTEP = 4
F32 = jnp.float32
BF16 = jnp.bfloat16
I32 = jnp.int32
INNOV_MAX = 6.0
INNOV_STEP = INNOV_MAX / 32767.0
WEIGHT_MAX = 4.0
WEIGHT_STEP = WEIGHT_MAX / 65535.0
CODE_FLOOR = -15.0
CODE_STEPS = 1056.0


def split_hi_lo(value):
    high = value.astype(BF16)
    low = (value - high.astype(F32)).astype(BF16)
    return high, low


def encode(value):
    size = jnp.maximum(jnp.abs(value), 2.0**CODE_FLOOR)
    level = (jnp.log2(size) - CODE_FLOOR) * CODE_STEPS + 0.5
    code = jnp.minimum(level, 32767.0).astype(I32)
    return jnp.where(value < 0.0, code + 32768, code)


def decode(code):
    level = code & 32767
    size = jnp.exp2(level.astype(F32) * (1.0 / CODE_STEPS) + CODE_FLOOR)
    size = jnp.where(level == 0, 0.0, size)
    return jnp.where(code >= 32768, -size, size)


def iota(shape, dim):
    return lax.broadcasted_iota(I32, shape, dim)


def dot_f32(left, right):
    return jnp.dot(left, right, preferred_element_type=F32)


def dot_nt(left, right):
    return lax.dot_general(left, right, (((1,), (1,)), ((), ())), preferred_element_type=F32)


def dot_tn(left, right):
    return lax.dot_general(left, right, (((0,), (0,)), ((), ())), preferred_element_type=F32)


def params(mebibytes):
    return pltpu.CompilerParams(vmem_limit_bytes=mebibytes * 1024 * 1024)


HBM_SPEC = pl.BlockSpec(memory_space=pltpu.HBM)


def start_copies(pairs, sem_ref, first=0):
    copies = []
    for index, (source, target) in enumerate(pairs):
        copy = pltpu.make_async_copy(source, target, sem_ref.at[first + index])
        copy.start()
        copies.append(copy)
    return copies


def wait_copies(copies):
    for copy in copies:
        copy.wait()


def vmem_specs(count):
    return [pl.BlockSpec(memory_space=pltpu.VMEM)] * count


def address_kernel(
    devices_all, quarter, count_ref, owner_ref, cell_ref, scale_ref, innov_ref, kappa_ref,
    control_hbm, out_ref, key_ref, top_ref, bottom_ref, word_ref, ends_ref, sem_ref,
):
    grid_rows = control_hbm.shape[0]
    ends_in = start_copies(
        [
            (control_hbm.at[pl.ds(0, NSTEP)], ends_ref.at[0]),
            (control_hbm.at[pl.ds(grid_rows - NSTEP, NSTEP)], ends_ref.at[1]),
        ],
        sem_ref,
    )
    obs = owner_ref.shape[1]
    rows_half = devices_all * quarter
    rows = 2 * rows_half
    owner = owner_ref[...]
    cell = cell_ref[...]
    mine = iota((devices_all, obs), 0) == owner
    mine_f = mine.astype(F32)
    mine_b = mine_f.astype(BF16)
    block = min(256, obs)
    earlier = (iota((block, block), 0) < iota((block, block), 1)).astype(F32).astype(BF16)
    running = jnp.zeros((devices_all, 1), F32)
    parts = []
    for start in range(0, obs, block):
        piece = mine_f[:, start : start + block]
        before = dot_f32(mine_b[:, start : start + block], earlier) + running
        parts.append(jnp.sum(piece * before, axis=0, keepdims=True))
        running = running + jnp.sum(piece, axis=1, keepdims=True)
    position = jnp.concatenate(parts, axis=1).astype(I32)
    group = position // quarter
    key = (
        (group // 2) * rows + (group % 2) * rows_half + owner * quarter + position % quarter
    )
    key_ref[...] = key
    scale = scale_ref[...]
    valid = iota((1, obs), 1) < count_ref[0]
    weight = jnp.where(valid, 1.0 / (scale * scale), 0.0)
    weight = jnp.minimum(jnp.floor(weight * (1.0 / WEIGHT_STEP) + 0.5), 65535.0)
    weight_high = jnp.floor(weight * (1.0 / 256.0))
    weight_low = weight - 256.0 * weight_high
    cell_high = (cell // 64).astype(F32)
    cell_low = (cell % 64).astype(F32)
    left = jnp.concatenate(
        [mine_f * piece for piece in (cell_high, cell_low, weight_high, weight_low)], axis=0
    ).astype(BF16)
    place = (iota((128, obs), 0) == position).astype(F32).astype(BF16)
    table = dot_nt(left, place).astype(I32)
    n = devices_all
    cells = table[:n] * 64 + table[n : 2 * n]
    weights = table[2 * n : 3 * n] * 256 + table[3 * n :]
    meta = (cells << 16) | weights

    level = jnp.floor(
        jnp.clip(innov_ref[...], -INNOV_MAX, INNOV_MAX) * (1.0 / INNOV_STEP) + 0.5
    )
    high = jnp.floor(level * (1.0 / 256.0))
    low = (level - 256.0 * high).astype(BF16)
    high = high.astype(BF16)
    bytes_of = [jnp.concatenate([high, low], axis=0), jnp.concatenate([low, high], axis=0)]
    chunk = min(256, rows_half)
    left_lane = iota((chunk, 128), 1) < 64
    for base in range(0, rows_half, chunk):
        total = []
        for half in range(2):
            row = iota((chunk, obs), 0) + (base + half * rows_half)
            found = []
            for side in range(2):
                hot = (row + side * rows == key).astype(F32).astype(BF16)
                got = dot_nt(hot, bytes_of[side])
                found.append(got * 256.0 + pltpu.roll(got, 64, 1))
            total.append(jnp.where(left_lane, found[0], found[1]).astype(I32))
        word_ref[base : base + chunk, :] = (total[0] << 16) | (total[1] & 0xFFFF)
    for device in range(devices_all):
        at = device * (quarter + 1)
        out_ref[at : at + quarter, :] = word_ref[device * quarter : (device + 1) * quarter, :]
        out_ref[at + quarter : at + quarter + 1, :] = meta[device : device + 1]
    top_ref[1] = spread_kappa(kappa_ref[:NSTEP, :]).astype(BF16)
    bottom_ref[1] = spread_kappa(kappa_ref[grid_rows - NSTEP :, :]).astype(BF16)
    wait_copies(ends_in)
    top_ref[0] = ends_ref[0].astype(BF16)
    bottom_ref[0] = ends_ref[1].astype(BF16)


def put_sides(wide_ref, at, count, cols, east, west):
    wide_ref[at : at + count, cols : cols + NSTEP, :] = east.astype(F32)
    wide_ref[at : at + count, cols + NSTEP :, :] = west.astype(F32)


def spread_kappa(kappa, low=0, high=None):
    rows, cols = kappa.shape
    count = (cols if high is None else high) - low
    top, rest = split_hi_lo(kappa)
    pair = jnp.concatenate([top.astype(F32), rest.astype(F32)], axis=1)
    shape = (rows, count, 2 * cols)
    hot = iota(shape, 1) + low == iota(shape, 2) % cols
    spread = jnp.where(hot, pair[:, None, :], 0.0).astype(BF16)
    ones = jnp.ones((2 * cols, 128), BF16)
    return dot_f32(spread.reshape(rows * count, 2 * cols), ones).reshape(rows, count, 128)


def pack_kernel(control_hbm, kappa_ref, near_ref, far_ref, left_ref, right_ref, sem_ref):
    cols = control_hbm.shape[1]
    copies = start_copies(
        [
            (control_hbm.at[:, pl.ds(0, 8)], left_ref),
            (control_hbm.at[:, pl.ds(cols - 8, 8)], right_ref),
        ],
        sem_ref,
    )
    kappa = kappa_ref[...]
    near_ref[1] = spread_kappa(kappa, 0, 8)[:, :NSTEP].astype(BF16)
    far_ref[1] = spread_kappa(kappa, cols - 8, cols)[:, 8 - NSTEP :].astype(BF16)
    wait_copies(copies)
    near_ref[0] = left_ref[:, :NSTEP].astype(BF16)
    far_ref[0] = right_ref[:, 8 - NSTEP :].astype(BF16)


def sweep_rows(source, target, kap_ref, low, high, block=8):
    cols = source.shape[1]

    def update(first, count):
        rows = [source[first + i] for i in range(-1, count + 1)]
        for i in range(count):
            here = rows[i + 1]
            change = (
                (rows[i] + rows[i + 2])
                + (pltpu.roll(here, 1, 0) + pltpu.roll(here, cols - 1, 0))
                - 4.0 * here
            )
            target[first + i] = here + kap_ref[first + i] * change

    whole = (high - low) // block

    def step(index, carry):
        update(low + index * block, block)
        return carry

    lax.fori_loop(0, whole, step, 0)
    if low + whole * block < high:
        update(low + whole * block, high - low - whole * block)


def sweeps(first_ref, second_ref, kap_ref, rows, block=8):
    source, target = first_ref, second_ref
    for sweep in range(1, NSTEP + 1):
        sweep_rows(source, target, kap_ref, sweep, rows - sweep, block)
        source, target = target, source
    return source


def fill_picked(pick_ref, picked):
    channels, levels = picked.shape
    pick_ref[...] = jnp.zeros_like(pick_ref)
    for part in range(4):
        pick_ref[
            part * channels : (part + 1) * channels, part * levels : (part + 1) * levels
        ] = picked


def forward_mixing(vertical):
    high, low = split_hi_lo(vertical)
    pair = jnp.concatenate([high, low], axis=1)
    return jnp.concatenate([pair, pair], axis=0)


def project_rows(rows, dev, mixing):
    count, cols, levels = rows.shape
    pair = jnp.concatenate(split_hi_lo(rows.reshape(count * cols, levels)), axis=1)
    both = dot_f32(pair, mixing)
    state = both[:, :levels] + both[:, levels:]
    prof = (dev.reshape(count * cols, levels) * state).astype(BF16)
    prof = prof.reshape(count // 4, 4, cols, levels)
    return jnp.concatenate(
        [prof[:, part].reshape(count // 4 * cols, levels) for part in range(4)], axis=1
    )


def forward_kernel(
    control_hbm, sigma_hbm, east_ref, west_ref, kappa_ref, vertical_ref, table_ref, choice_ref,
    out_hbm, pick_hbm, first_ref, second_ref, kap_ref, out_ref, pick_ref, sigma_ref, sem_ref,
):
    rows, cols, levels = control_hbm.shape
    tile_in = start_copies(
        [(control_hbm, first_ref.at[pl.ds(0, rows), pl.ds(0, cols)])], sem_ref
    )
    sigma_in = start_copies([(sigma_hbm, sigma_ref)], sem_ref, 1)
    put_sides(first_ref, 0, rows, cols, east_ref[0], west_ref[0])
    kap_ref[:rows, :cols, :] = spread_kappa(kappa_ref[...])
    put_sides(kap_ref, 0, rows, cols, east_ref[1], west_ref[1])
    wait_copies(tile_in)
    done = sweeps(first_ref, second_ref, kap_ref, rows)
    wait_copies(sigma_in)
    channels = choice_ref.shape[1]
    table_rows = table_ref.shape[0]
    hot = (iota((table_rows, channels), 0) == choice_ref[...]).astype(F32).astype(BF16)
    fill_picked(pick_ref, dot_tn(hot, table_ref[...]).astype(BF16))
    mixing = forward_mixing(vertical_ref[...])
    copies = start_copies([(pick_ref, pick_hbm)], sem_ref)
    count = 8
    for index in range((rows - 2 * NSTEP) // count):
        row = NSTEP + index * count
        where = pl.ds(row // 4 * cols, count // 4 * cols)
        out_ref[where, :] = project_rows(
            done[row : row + count, :cols, :], sigma_ref[row : row + count], mixing
        )
        copies += start_copies([(out_ref.at[where], out_hbm.at[where])], sem_ref, index + 1)
    wait_copies(copies)


def pole_flags():
    at = lax.axis_index("lat")
    last = lax.axis_size("lat") - 1
    return jnp.where(at > 0, 1.0, 0.0), jnp.where(at < last, 1.0, 0.0)


def put_rims(wide_ref, east_of, west_of, north, south, flags, rows, cols):
    span = 2 * NSTEP
    wide_ref[:NSTEP] = north.astype(F32) * flags[0]
    put_sides(wide_ref, NSTEP, span, cols, east_of(0, span), west_of(0, span))
    put_sides(
        wide_ref, NSTEP + span, span, cols, east_of(rows - span, rows), west_of(rows - span, rows)
    )
    wide_ref[NSTEP + 2 * span :] = south.astype(F32) * flags[1]


def rim_tiles(hbm, wide_ref):
    span = 2 * NSTEP
    rows, cols, _ = hbm.shape
    return [
        (hbm.at[pl.ds(0, span)], wide_ref.at[pl.ds(NSTEP, span), pl.ds(0, cols)]),
        (hbm.at[pl.ds(rows - span, span)], wide_ref.at[pl.ds(NSTEP + span, span), pl.ds(0, cols)]),
    ]


def put_rim_kappa(kap_ref, kappa_ref, east_ref, west_ref, north_ref, south_ref, flags):
    rows, cols = kappa_ref.shape
    span = 2 * NSTEP
    kap_ref[NSTEP : NSTEP + 2 * span, :cols, :] = spread_kappa(
        jnp.concatenate([kappa_ref[:span, :], kappa_ref[rows - span :, :]], axis=0)
    )
    put_rims(
        kap_ref,
        lambda low, high: east_ref[1, low:high],
        lambda low, high: west_ref[1, low:high],
        north_ref[1],
        south_ref[1],
        flags,
        rows,
        cols,
    )


def owner_kernel(
    devices_all, quarter, recv_hbm, evolved_hbm, pick_hbm, sigma_hbm, control_hbm, rinv_ref,
    east_ref, west_ref, north_ref, south_ref, kappa_ref, vertical_ref,
    ret_hbm, adj_hbm, left_hbm, right_hbm, top_hbm, bottom_hbm,
    word_ref, dep_ref, acc_ref, first_ref, second_ref, kap_ref, table_ref, pair_ref,
    recv_ref, ret_ref, pick_ref, sigma_ref, adj_ref, left_ref, right_ref, top_ref, bottom_ref,
    sem_ref,
):
    lat_rows, cols, levels = sigma_hbm.shape
    cells_part = evolved_hbm.shape[0]
    flags = pole_flags()
    span = 2 * NSTEP
    inside = pl.ds(cols, cells_part - 2 * cols)
    control_in = start_copies(rim_tiles(control_hbm, first_ref), sem_ref)
    ends_at = (pl.ds(0, NSTEP), pl.ds(lat_rows - NSTEP, NSTEP))
    ends_in = start_copies(
        [(sigma_hbm.at[at], sigma_ref.at[at]) for at in ends_at] + [(pick_hbm, pick_ref)],
        sem_ref,
        2,
    )
    others_in = start_copies(
        [(recv_hbm, recv_ref), (evolved_hbm.at[inside], table_ref.at[inside])], sem_ref, 5
    )
    rest = pl.ds(NSTEP, lat_rows - 2 * NSTEP)
    sigma_in = start_copies([(sigma_hbm.at[rest], sigma_ref.at[rest])], sem_ref, 7)
    put_rim_kappa(kap_ref, kappa_ref, east_ref, west_ref, north_ref, south_ref, flags)
    put_rims(
        first_ref,
        lambda low, high: east_ref[0, low:high],
        lambda low, high: west_ref[0, low:high],
        north_ref[0],
        south_ref[0],
        flags,
        lat_rows,
        cols,
    )
    wait_copies(control_in)
    done = sweeps(first_ref, second_ref, kap_ref, 6 * NSTEP)
    wait_copies(ends_in)
    ends = project_rows(
        jnp.concatenate(
            [done[NSTEP : 2 * NSTEP, :cols, :], done[4 * NSTEP : 5 * NSTEP, :cols, :]], axis=0
        ),
        jnp.concatenate([sigma_ref[:NSTEP], sigma_ref[lat_rows - NSTEP :]], axis=0),
        forward_mixing(vertical_ref[...]),
    )
    table_ref[:cols, :] = ends[:cols]
    table_ref[cells_part - cols :, :] = ends[cols:]

    wait_copies(others_in)
    rows_half = devices_all * quarter
    rows = 2 * rows_half
    metas = []
    for device in range(devices_all):
        at = device * (quarter + 1)
        word_ref[device * quarter : (device + 1) * quarter, :] = recv_ref[at : at + quarter, :]
        metas.append(recv_ref[at + quarter : at + quarter + 1, :])
    meta = jnp.concatenate(metas, axis=0)
    cells, weights = meta >> 16, meta & 0xFFFF
    facts = jnp.concatenate(
        [
            piece.astype(F32).astype(BF16)
            for piece in (cells >> 6, cells & 63, weights >> 8, weights & 255)
        ],
        axis=1,
    )
    channels = rinv_ref.shape[0]
    pair_ref[...] = jnp.zeros_like(pair_ref)
    pair_ref[:channels, :channels] = rinv_ref[...]
    pair_ref[channels:, channels:] = rinv_ref[...]
    high, low = split_hi_lo(pair_ref[...])
    zero = jnp.zeros_like(high)
    mixing = jnp.concatenate(
        [jnp.concatenate([high, low], axis=1), jnp.concatenate([high, zero], axis=1)], axis=0
    )
    pick_pair = jnp.transpose(
        pick_ref[: 2 * channels, : 2 * levels].astype(F32)
    ).astype(BF16)
    acc_ref[...] = jnp.zeros_like(acc_ref)
    chunk = min(512, rows_half)
    left_lane = iota((chunk, 128), 1) < 64
    lane_half = iota((chunk, 128), 1) // 64
    per_half = rows_half // chunk
    for step in range(rows // chunk):
        half = step // per_half
        base = (step % per_half) * chunk
        row = iota((chunk, devices_all), 0) + base
        spread = (row // quarter == iota((chunk, devices_all), 1)).astype(F32).astype(BF16)
        found = dot_f32(spread, facts)
        lat_lane = found[:, :128]
        lon_lane = found[:, 128:256]
        weight_lane = (found[:, 256:384] * 256.0 + found[:, 384:]) * WEIGHT_STEP
        lane = iota((chunk, 128), 1)
        r = (iota((chunk, 128), 0) + base) % quarter
        hots, parts, weight, values = [], [], [], []
        for side in range(2):
            take = lane == (2 * side + half) * quarter + r
            lat = jnp.sum(jnp.where(take, lat_lane, 0.0), axis=1, keepdims=True).astype(I32)
            lon = jnp.sum(jnp.where(take, lon_lane, 0.0), axis=1, keepdims=True).astype(I32)
            weight.append(jnp.sum(jnp.where(take, weight_lane, 0.0), axis=1, keepdims=True))
            part = lat & 3
            inside = (lat >> 2) * cols + lon
            hot = (iota((chunk, cells_part), 1) == inside).astype(F32).astype(BF16)
            got = dot_f32(hot, table_ref[...])
            low_parts = jnp.where(part == 0, got[:, :levels], got[:, levels : 2 * levels])
            high_parts = jnp.where(
                part == 2, got[:, 2 * levels : 3 * levels], got[:, 3 * levels :]
            )
            values.append(jnp.where(part < 2, low_parts, high_parts).astype(BF16))
            hots.append(hot)
            parts.append(part)
        evolved = dot_f32(jnp.concatenate(values, axis=1), pick_pair)
        words = word_ref[base : base + chunk, :]
        words = (words if half == 0 else words << 16) >> 16
        gap = evolved - words.astype(F32) * INNOV_STEP
        both = dot_f32(jnp.concatenate(split_hi_lo(gap), axis=1), mixing)
        dep = (both[:, :128] + both[:, 128:]) * jnp.where(left_lane, weight[0], weight[1])
        dep_ref[step * chunk : (step + 1) * chunk, :] = encode(evolved)
        rounded = dep.astype(BF16).astype(F32)
        swapped = pltpu.roll(rounded, 64, 1)
        for side in range(2):
            twice = (
                jnp.where(left_lane, rounded, swapped)
                if side == 0
                else jnp.where(left_lane, swapped, rounded)
            )
            wide = jnp.concatenate(
                [
                    jnp.where(parts[side] == lane_half, twice, 0.0).astype(BF16),
                    jnp.where(parts[side] == lane_half + 2, twice, 0.0).astype(BF16),
                ],
                axis=1,
            )
            acc_ref[...] += dot_tn(hots[side], wide)
    ret_ref[...] = (dep_ref[:rows_half, :] << 16) | dep_ref[rows_half:, :]
    copies = start_copies([(ret_ref, ret_hbm)], sem_ref)
    wait_copies(sigma_in)
    groups = 4
    count = groups * 4
    for step in range(lat_rows // count):
        high, low = split_hi_lo(acc_ref[step * groups * cols : (step + 1) * groups * cols, :])
        both = dot_f32(high, pick_ref[...]) + dot_f32(low, pick_ref[...])
        for group in range(groups):
            for part in range(4):
                at = step * count + group * 4 + part
                value = sigma_ref[at] * both[
                    group * cols : (group + 1) * cols, part * levels : (part + 1) * levels
                ]
                adj_ref[at] = value
                left_ref[at] = value[:NSTEP].astype(BF16)
                right_ref[at] = value[cols - NSTEP :].astype(BF16)
                if at < NSTEP:
                    top_ref[at] = value.astype(BF16)
                if at >= lat_rows - NSTEP:
                    bottom_ref[at - (lat_rows - NSTEP)] = value.astype(BF16)
        where = pl.ds(step * count, count)
        copies += start_copies([(adj_ref.at[where], adj_hbm.at[where])], sem_ref, step + 1)
    copies += start_copies(
        [
            (left_ref, left_hbm),
            (right_ref, right_hbm),
            (top_ref, top_hbm),
            (bottom_ref, bottom_hbm),
        ],
        sem_ref,
        lat_rows // count + 1,
    )
    wait_copies(copies)


def backward_mixing(vertical):
    high, low = split_hi_lo(vertical)
    return jnp.concatenate(
        [jnp.concatenate([high, high], axis=1), jnp.concatenate([low, low], axis=1)], axis=0
    )


def finish_rows(scaled, kap, mixing):
    count, cols, levels = scaled.shape
    adjoint = (scaled / kap).reshape(count * cols, levels)
    both = dot_nt(jnp.concatenate(split_hi_lo(adjoint), axis=1), mixing)
    return (both[:, :levels] + both[:, levels:]).reshape(count, cols, levels)


def inner_kernel(
    adj_hbm, control_hbm, east_ref, west_ref, kappa_ref, keast_ref, kwest_ref, vertical_ref,
    out_hbm, first_ref, second_ref, kap_ref, out_ref, control_ref, sem_ref,
):
    rows, cols, levels = control_hbm.shape
    tile_in = start_copies([(adj_hbm, first_ref.at[pl.ds(0, rows), pl.ds(0, cols)])], sem_ref)
    control_in = start_copies([(control_hbm, control_ref)], sem_ref, 1)
    kap_ref[:rows, :cols, :] = spread_kappa(kappa_ref[...])
    put_sides(kap_ref, 0, rows, cols, keast_ref[1], kwest_ref[1])
    put_sides(first_ref, 0, rows, cols, east_ref[...], west_ref[...])
    wait_copies(tile_in)
    first_ref[:rows] = first_ref[:rows] * kap_ref[:rows]
    done = sweeps(first_ref, second_ref, kap_ref, rows)
    mixing = backward_mixing(vertical_ref[...])
    wait_copies(control_in)
    count = 8
    copies = []
    for index in range((rows - 2 * NSTEP) // count):
        row = NSTEP + index * count
        at = pl.ds(row, count)
        out_ref[at] = control_ref[at] + finish_rows(
            done[row : row + count, :cols, :], kap_ref[row : row + count, :cols, :], mixing
        )
        copies += start_copies([(out_ref.at[at], out_hbm.at[at])], sem_ref, index)
    wait_copies(copies)


def rim_kernel(
    adj_hbm, control_hbm, east_ref, west_ref, north_ref, south_ref, kappa_ref, keast_ref,
    kwest_ref, knorth_ref, ksouth_ref, vertical_ref, inner_ref, out_ref,
    first_ref, second_ref, kap_ref, edge_ref, control_ref, sem_ref,
):
    del inner_ref
    lat_rows, cols = kappa_ref.shape
    flags = pole_flags()
    tile_in = start_copies(rim_tiles(adj_hbm, first_ref), sem_ref)
    starts = (0, lat_rows - NSTEP)
    control_in = start_copies(
        [(control_hbm.at[pl.ds(at, NSTEP)], control_ref.at[i]) for i, at in enumerate(starts)],
        sem_ref,
        2,
    )
    put_rim_kappa(kap_ref, kappa_ref, keast_ref, kwest_ref, knorth_ref, ksouth_ref, flags)
    put_rims(
        first_ref,
        lambda low, high: east_ref[low:high],
        lambda low, high: west_ref[low:high],
        north_ref[...],
        south_ref[...],
        flags,
        lat_rows,
        cols,
    )
    wait_copies(tile_in)
    first_ref[...] = first_ref[...] * kap_ref[...]
    done = sweeps(first_ref, second_ref, kap_ref, 6 * NSTEP)
    mixing = backward_mixing(vertical_ref[...])
    wait_copies(control_in)
    copies = []
    for end in range(2):
        at = pl.ds((1 + 3 * end) * NSTEP, NSTEP)
        back = finish_rows(done[at, :cols, :], kap_ref[at, :cols, :], mixing)
        edge_ref[end] = control_ref[end] + back
        copies += start_copies(
            [(edge_ref.at[end], out_ref.at[pl.ds(starts[end], NSTEP)])], sem_ref, 4 + end
        )
    wait_copies(copies)


def pass_kernel(array_hbm, first_hbm, second_hbm, out_hbm):
    del array_hbm, first_hbm, second_hbm, out_hbm


def return_kernel(
    devices_all, quarter, count_ref, recv_ref, key_ref, innov_ref, scale_ref, rinv_ref, out_ref,
    pair_ref,
):
    rows_half = devices_all * quarter
    rows = 2 * rows_half
    channels, obs = out_ref.shape
    words = recv_ref[...]
    for half in range(2):
        code = (words >> 16) & 0xFFFF if half == 0 else words & 0xFFFF
        high, low = split_hi_lo(decode(code))
        pair_ref[half * rows_half : (half + 1) * rows_half, :128] = high
        pair_ref[half * rows_half : (half + 1) * rows_half, 128:] = low
    scale = scale_ref[...]
    valid = iota((1, obs), 1) < count_ref[0]
    weight = jnp.where(valid, 1.0 / (scale * scale), 0.0)
    chunk = min(512, obs)
    for start in range(0, obs, chunk):
        key = key_ref[:, start : start + chunk]
        side = key >= rows
        row = jnp.where(side, key - rows, key)
        hot = (iota((rows, chunk), 0) == row).astype(F32).astype(BF16)
        both = dot_tn(pair_ref[...], hot)
        both = both[:128] + both[128:]
        evolved = jnp.where(side, both[channels:], both[:channels])
        gap = evolved - innov_ref[:, start : start + chunk]
        mixed = lax.dot_general(
            rinv_ref[...], gap, (((0,), (0,)), ((), ())), precision=lax.Precision.HIGHEST,
            preferred_element_type=F32,
        )
        out_ref[:, start : start + chunk] = mixed * weight[:, start : start + chunk]


def shifts(axis):
    count = lax.axis_size(axis)
    forward = [(i, (i + 1) % count) for i in range(count)]
    return forward, [(target, source) for source, target in forward]


def exchange_sides(left, right):
    forward, backward = shifts("lon")
    return lax.ppermute(left, "lon", backward), lax.ppermute(right, "lon", forward)


def exchange_rims(top, bottom):
    forward, backward = shifts("lat")
    return lax.ppermute(bottom, "lat", forward), lax.ppermute(top, "lat", backward)


def estimate(flops, bytes_accessed):
    return pl.CostEstimate(flops=flops, bytes_accessed=bytes_accessed, transcendentals=0)


def body(
    control,
    kappa,
    sigma,
    vertical,
    channel_table,
    channel_pick,
    r_inverse,
    innovations,
    error_scale,
    obs_owner,
    obs_cell,
    obs_count,
):
    lat_rows, lon_cols, levels = control.shape
    obs_slots = obs_cell.shape[0]
    channels = innovations.shape[1]
    devices_all = lax.axis_size("lat") * lax.axis_size("lon")
    capacity = max(4, 2 * obs_slots // devices_all)
    quarter = capacity // 4
    rows_half = devices_all * quarter
    columns = lat_rows * lon_cols
    wide = (lat_rows + 1, lon_cols + 2 * NSTEP, levels)
    rim = (6 * NSTEP, lon_cols + 2 * NSTEP, levels)
    smem = pl.BlockSpec(memory_space=pltpu.SMEM)
    anywhere = pl.BlockSpec(memory_space=pl.ANY)

    near, far = pl.pallas_call(
        pack_kernel,
        out_shape=(jax.ShapeDtypeStruct((2, lat_rows, NSTEP, levels), BF16),) * 2,
        in_specs=[HBM_SPEC] + vmem_specs(1),
        out_specs=tuple(vmem_specs(2)),
        scratch_shapes=[
            pltpu.VMEM((lat_rows, 8, levels), F32),
            pltpu.VMEM((lat_rows, 8, levels), F32),
            pltpu.SemaphoreType.DMA((2,)),
        ],
        compiler_params=params(58),
        name="pack",
    )(control, kappa)
    near, far, obs_cell = lax.optimization_barrier((near, far, obs_cell))
    east, west = exchange_sides(near, far)

    payload, key, top, bottom = pl.pallas_call(
        functools.partial(address_kernel, devices_all, quarter),
        out_shape=(
            jax.ShapeDtypeStruct((devices_all * (quarter + 1), 128), I32),
            jax.ShapeDtypeStruct((1, obs_slots), I32),
            jax.ShapeDtypeStruct((2, NSTEP, lon_cols, levels), BF16),
            jax.ShapeDtypeStruct((2, NSTEP, lon_cols, levels), BF16),
        ),
        in_specs=[smem] + vmem_specs(5) + [HBM_SPEC],
        out_specs=tuple(vmem_specs(4)),
        scratch_shapes=[
            pltpu.VMEM((rows_half, 128), I32),
            pltpu.VMEM((2, NSTEP, lon_cols, levels), F32),
            pltpu.SemaphoreType.DMA((2,)),
        ],
        compiler_params=params(10),
        cost_estimate=estimate(2_000_000_000, 8_000_000),
        name="address",
    )(
        obs_count,
        obs_owner.reshape(1, obs_slots),
        obs_cell.reshape(1, obs_slots),
        error_scale.reshape(1, obs_slots),
        innovations.T,
        kappa,
        control,
    )
    received = lax.all_to_all(
        payload.reshape(devices_all, 1, (quarter + 1) * 128),
        ("lat", "lon"),
        split_axis=0,
        concat_axis=0,
        tiled=True,
    ).reshape(payload.shape)

    def with_sides(tile, low, high):
        return jnp.concatenate([tile, east[:, low:high], west[:, low:high]], axis=2)

    north, south = exchange_rims(
        with_sides(top, 0, NSTEP), with_sides(bottom, lat_rows - NSTEP, lat_rows)
    )

    evolved, picked = pl.pallas_call(
        forward_kernel,
        out_shape=(
            jax.ShapeDtypeStruct((columns // 4, 8 * channels), BF16),
            jax.ShapeDtypeStruct((4 * channels, 4 * levels), BF16),
        ),
        in_specs=[HBM_SPEC] * 2 + vmem_specs(6),
        out_specs=(HBM_SPEC, HBM_SPEC),
        scratch_shapes=[pltpu.VMEM(wide, F32)] * 3
        + [
            pltpu.VMEM((columns // 4, 8 * channels), BF16),
            pltpu.VMEM((4 * channels, 4 * levels), BF16),
            pltpu.VMEM(control.shape, F32),
            pltpu.SemaphoreType.DMA((lat_rows // 8 + 2,)),
        ],
        compiler_params=params(58),
        cost_estimate=estimate(4_000_000_000, 16_000_000),
        name="forward",
    )(
        control, sigma, east, west, kappa, vertical, channel_table,
        channel_pick.reshape(1, channels),
    )

    returned, adjoint, left, right, atop, abottom = pl.pallas_call(
        functools.partial(owner_kernel, devices_all, quarter),
        out_shape=(
            jax.ShapeDtypeStruct((rows_half, 128), I32),
            jax.ShapeDtypeStruct(control.shape, F32),
            jax.ShapeDtypeStruct((lat_rows, NSTEP, levels), BF16),
            jax.ShapeDtypeStruct((lat_rows, NSTEP, levels), BF16),
            jax.ShapeDtypeStruct((NSTEP, lon_cols, levels), BF16),
            jax.ShapeDtypeStruct((NSTEP, lon_cols, levels), BF16),
        ),
        in_specs=[HBM_SPEC] * 5 + vmem_specs(7),
        out_specs=(HBM_SPEC,) * 6,
        scratch_shapes=[
            pltpu.VMEM((rows_half, 128), I32),
            pltpu.VMEM((2 * rows_half, 128), I32),
            pltpu.VMEM((columns // 4, 4 * channels), F32),
            pltpu.VMEM(rim, F32),
            pltpu.VMEM(rim, F32),
            pltpu.VMEM(rim, F32),
            pltpu.VMEM((columns // 4, 8 * channels), BF16),
            pltpu.VMEM((2 * channels, 2 * channels), F32),
            pltpu.VMEM((devices_all * (quarter + 1), 128), I32),
            pltpu.VMEM((rows_half, 128), I32),
            pltpu.VMEM((4 * channels, 4 * levels), BF16),
            pltpu.VMEM(control.shape, F32),
            pltpu.VMEM(control.shape, F32),
            pltpu.VMEM((lat_rows, NSTEP, levels), BF16),
            pltpu.VMEM((lat_rows, NSTEP, levels), BF16),
            pltpu.VMEM((NSTEP, lon_cols, levels), BF16),
            pltpu.VMEM((NSTEP, lon_cols, levels), BF16),
            pltpu.SemaphoreType.DMA((max(8, lat_rows // 16 + 5),)),
        ],
        compiler_params=params(58),
        cost_estimate=estimate(4_000_000_000, 16_000_000),
        name="owner",
    )(
        received, evolved, picked, sigma, control, r_inverse, east, west, north, south, kappa,
        vertical,
    )
    returned = pl.pallas_call(
        pass_kernel,
        out_shape=jax.ShapeDtypeStruct(returned.shape, I32),
        in_specs=[anywhere] * 3,
        out_specs=anywhere,
        input_output_aliases={0: 0},
        cost_estimate=estimate(1_000_000, 1_000_000),
        name="pass",
    )(returned, left, right)
    home = lax.all_to_all(
        returned.reshape(devices_all, quarter, 128),
        ("lat", "lon"),
        split_axis=0,
        concat_axis=0,
        tiled=True,
    ).reshape(returned.shape)

    aeast, awest = exchange_sides(left, right)
    anorth, asouth = exchange_rims(
        jnp.concatenate([atop, aeast[:NSTEP], awest[:NSTEP]], axis=1),
        jnp.concatenate([abottom, aeast[-NSTEP:], awest[-NSTEP:]], axis=1),
    )
    inner = pl.pallas_call(
        inner_kernel,
        out_shape=jax.ShapeDtypeStruct(control.shape, F32),
        in_specs=[HBM_SPEC] * 2 + vmem_specs(6),
        out_specs=HBM_SPEC,
        scratch_shapes=[pltpu.VMEM(wide, F32)] * 3
        + [pltpu.VMEM(control.shape, F32)] * 2
        + [pltpu.SemaphoreType.DMA((lat_rows // 8,))],
        compiler_params=params(20),
        cost_estimate=estimate(4_000_000_000, 16_000_000),
        name="inner",
    )(adjoint, control, aeast, awest, kappa, east, west, vertical)

    gradient = pl.pallas_call(
        rim_kernel,
        out_shape=jax.ShapeDtypeStruct(control.shape, F32),
        in_specs=[HBM_SPEC] * 2 + vmem_specs(10) + [anywhere],
        out_specs=anywhere,
        scratch_shapes=[pltpu.VMEM(rim, F32)] * 3
        + [
            pltpu.VMEM((2, NSTEP, lon_cols, levels), F32),
            pltpu.VMEM((2, NSTEP, lon_cols, levels), F32),
            pltpu.SemaphoreType.DMA((6,)),
        ],
        input_output_aliases={12: 0},
        compiler_params=params(12),
        cost_estimate=estimate(1_000_000_000, 2_000_000),
        name="rims",
    )(
        adjoint, control, aeast, awest, anorth, asouth, kappa, east, west, north, south, vertical,
        inner,
    )

    departures = pl.pallas_call(
        functools.partial(return_kernel, devices_all, quarter),
        out_shape=jax.ShapeDtypeStruct((channels, obs_slots), F32),
        in_specs=[smem] + vmem_specs(5),
        out_specs=vmem_specs(1)[0],
        scratch_shapes=[pltpu.VMEM((2 * rows_half, 256), BF16)],
        compiler_params=params(10),
        cost_estimate=estimate(500_000_000, 2_000_000),
        name="give_back",
    )(
        obs_count, home, key, innovations.T, error_scale.reshape(1, obs_slots),
        r_inverse,
    )
    return (gradient, departures.T)


def solution(mesh):
    return jax.shard_map(
        body,
        mesh=mesh,
        in_specs=(
            P("lat", "lon", None),
            P("lat", "lon"),
            P("lat", "lon", None),
            P(),
            P(),
            P(),
            P(),
            P(("lat", "lon"), None),
            P(("lat", "lon")),
            P(("lat", "lon"), None),
            P(("lat", "lon")),
            P(("lat", "lon")),
        ),
        out_specs=(P("lat", "lon", None), P(("lat", "lon"), None)),
        check_vma=False,
    )
```

```python
import functools

import jax
import jax.numpy as jnp
from jax import lax
from jax.experimental import pallas as pl
from jax.experimental.pallas import tpu as pltpu
from jax.sharding import PartitionSpec as P

NSTEP = 4
F32 = jnp.float32
BF16 = jnp.bfloat16
I32 = jnp.int32
INNOV_MAX = 6.0
INNOV_STEP = INNOV_MAX / 32767.0
WEIGHT_MAX = 4.0
WEIGHT_STEP = WEIGHT_MAX / 65535.0
CODE_FLOOR = -15.0
CODE_STEPS = 1056.0


def split_hi_lo(value):
    high = value.astype(BF16)
    low = (value - high.astype(F32)).astype(BF16)
    return high, low


def encode(value):
    size = jnp.maximum(jnp.abs(value), 2.0**CODE_FLOOR)
    level = (jnp.log2(size) - CODE_FLOOR) * CODE_STEPS + 0.5
    code = jnp.minimum(level, 32767.0).astype(I32)
    return jnp.where(value < 0.0, code + 32768, code)


def decode(code):
    level = code & 32767
    size = jnp.exp2(level.astype(F32) * (1.0 / CODE_STEPS) + CODE_FLOOR)
    size = jnp.where(level == 0, 0.0, size)
    return jnp.where(code >= 32768, -size, size)


def iota(shape, dim):
    return lax.broadcasted_iota(I32, shape, dim)


def dot_f32(left, right):
    return jnp.dot(left, right, preferred_element_type=F32)


def dot_nt(left, right):
    return lax.dot_general(left, right, (((1,), (1,)), ((), ())), preferred_element_type=F32)


def dot_tn(left, right):
    return lax.dot_general(left, right, (((0,), (0,)), ((), ())), preferred_element_type=F32)


def params(mebibytes):
    return pltpu.CompilerParams(vmem_limit_bytes=mebibytes * 1024 * 1024)


HBM_SPEC = pl.BlockSpec(memory_space=pltpu.HBM)


def in_hbm(array):
    return pltpu.with_memory_space_constraint(array, pltpu.HBM)


def start_copies(pairs, sem_ref, first=0):
    copies = []
    for index, (source, target) in enumerate(pairs):
        copy = pltpu.make_async_copy(source, target, sem_ref.at[first + index])
        copy.start()
        copies.append(copy)
    return copies


def wait_copies(copies):
    for copy in copies:
        copy.wait()


def vmem_specs(count):
    return [pl.BlockSpec(memory_space=pltpu.VMEM)] * count


def address_kernel(
    devices_all, quarter, count_ref, owner_ref, cell_ref, scale_ref, innov_ref, kappa_ref,
    control_hbm, out_ref, key_ref, top_ref, bottom_ref, word_ref, ends_ref, sem_ref,
):
    grid_rows = control_hbm.shape[0]
    ends_in = start_copies(
        [
            (control_hbm.at[pl.ds(0, NSTEP)], ends_ref.at[0]),
            (control_hbm.at[pl.ds(grid_rows - NSTEP, NSTEP)], ends_ref.at[1]),
        ],
        sem_ref,
    )
    obs = owner_ref.shape[1]
    rows_half = devices_all * quarter
    rows = 2 * rows_half
    owner = owner_ref[...]
    cell = cell_ref[...]
    mine = iota((devices_all, obs), 0) == owner
    mine_f = mine.astype(F32)
    mine_b = mine_f.astype(BF16)
    block = min(256, obs)
    earlier = (iota((block, block), 0) < iota((block, block), 1)).astype(F32).astype(BF16)
    running = jnp.zeros((devices_all, 1), F32)
    parts = []
    for start in range(0, obs, block):
        piece = mine_f[:, start : start + block]
        before = dot_f32(mine_b[:, start : start + block], earlier) + running
        parts.append(jnp.sum(piece * before, axis=0, keepdims=True))
        running = running + jnp.sum(piece, axis=1, keepdims=True)
    position = jnp.concatenate(parts, axis=1).astype(I32)
    group = position // quarter
    key = (
        (group // 2) * rows + (group % 2) * rows_half + owner * quarter + position % quarter
    )
    key_ref[...] = key
    scale = scale_ref[...]
    valid = iota((1, obs), 1) < count_ref[0]
    weight = jnp.where(valid, 1.0 / (scale * scale), 0.0)
    weight = jnp.minimum(jnp.floor(weight * (1.0 / WEIGHT_STEP) + 0.5), 65535.0)
    weight_high = jnp.floor(weight * (1.0 / 256.0))
    weight_low = weight - 256.0 * weight_high
    cell_high = (cell // 64).astype(F32)
    cell_low = (cell % 64).astype(F32)
    left = jnp.concatenate(
        [mine_f * piece for piece in (cell_high, cell_low, weight_high, weight_low)], axis=0
    ).astype(BF16)
    place = (iota((128, obs), 0) == position).astype(F32).astype(BF16)
    table = dot_nt(left, place).astype(I32)
    n = devices_all
    cells = table[:n] * 64 + table[n : 2 * n]
    weights = table[2 * n : 3 * n] * 256 + table[3 * n :]
    meta = (cells << 16) | weights

    level = jnp.floor(
        jnp.clip(innov_ref[...], -INNOV_MAX, INNOV_MAX) * (1.0 / INNOV_STEP) + 0.5
    )
    high = jnp.floor(level * (1.0 / 256.0))
    low = (level - 256.0 * high).astype(BF16)
    high = high.astype(BF16)
    bytes_of = [jnp.concatenate([high, low], axis=0), jnp.concatenate([low, high], axis=0)]
    chunk = min(256, rows_half)
    left_lane = iota((chunk, 128), 1) < 64
    for base in range(0, rows_half, chunk):
        total = []
        for half in range(2):
            row = iota((chunk, obs), 0) + (base + half * rows_half)
            found = []
            for side in range(2):
                hot = (row + side * rows == key).astype(F32).astype(BF16)
                got = dot_nt(hot, bytes_of[side])
                found.append(got * 256.0 + pltpu.roll(got, 64, 1))
            total.append(jnp.where(left_lane, found[0], found[1]).astype(I32))
        word_ref[base : base + chunk, :] = (total[0] << 16) | (total[1] & 0xFFFF)
    for device in range(devices_all):
        at = device * (quarter + 1)
        out_ref[at : at + quarter, :] = word_ref[device * quarter : (device + 1) * quarter, :]
        out_ref[at + quarter : at + quarter + 1, :] = meta[device : device + 1]
    top_ref[1] = spread_kappa(kappa_ref[:NSTEP, :]).astype(BF16)
    bottom_ref[1] = spread_kappa(kappa_ref[grid_rows - NSTEP :, :]).astype(BF16)
    wait_copies(ends_in)
    top_ref[0] = ends_ref[0].astype(BF16)
    bottom_ref[0] = ends_ref[1].astype(BF16)


def put_sides(wide_ref, at, count, cols, east, west):
    wide_ref[at : at + count, cols : cols + NSTEP, :] = east.astype(F32)
    wide_ref[at : at + count, cols + NSTEP :, :] = west.astype(F32)


def spread_kappa(kappa, low=0, high=None):
    rows, cols = kappa.shape
    count = (cols if high is None else high) - low
    top, rest = split_hi_lo(kappa)
    pair = jnp.concatenate([top.astype(F32), rest.astype(F32)], axis=1)
    shape = (rows, count, 2 * cols)
    hot = iota(shape, 1) + low == iota(shape, 2) % cols
    spread = jnp.where(hot, pair[:, None, :], 0.0).astype(BF16)
    ones = jnp.ones((2 * cols, 128), BF16)
    return dot_f32(spread.reshape(rows * count, 2 * cols), ones).reshape(rows, count, 128)


def pack_kernel(
    control_hbm, kappa_hbm, near_ref, far_ref, left_ref, right_ref, kappa_ref, sem_ref
):
    cols = control_hbm.shape[1]
    kappa_in = start_copies([(kappa_hbm, kappa_ref)], sem_ref, 2)
    copies = start_copies(
        [
            (control_hbm.at[:, pl.ds(0, 8)], left_ref),
            (control_hbm.at[:, pl.ds(cols - 8, 8)], right_ref),
        ],
        sem_ref,
    )
    wait_copies(kappa_in)
    kappa = kappa_ref[...]
    near_ref[1] = spread_kappa(kappa, 0, 8)[:, :NSTEP].astype(BF16)
    far_ref[1] = spread_kappa(kappa, cols - 8, cols)[:, 8 - NSTEP :].astype(BF16)
    wait_copies(copies)
    near_ref[0] = left_ref[:, :NSTEP].astype(BF16)
    far_ref[0] = right_ref[:, 8 - NSTEP :].astype(BF16)


def sweep_rows(source, target, kap_ref, low, high, block=8):
    cols = source.shape[1]

    def update(first, count):
        rows = [source[first + i] for i in range(-1, count + 1)]
        for i in range(count):
            here = rows[i + 1]
            change = (
                (rows[i] + rows[i + 2])
                + (pltpu.roll(here, 1, 0) + pltpu.roll(here, cols - 1, 0))
                - 4.0 * here
            )
            target[first + i] = here + kap_ref[first + i] * change

    whole = (high - low) // block

    def step(index, carry):
        update(low + index * block, block)
        return carry

    lax.fori_loop(0, whole, step, 0)
    if low + whole * block < high:
        update(low + whole * block, high - low - whole * block)


def sweeps(first_ref, second_ref, kap_ref, rows, block=8):
    source, target = first_ref, second_ref
    for sweep in range(1, NSTEP + 1):
        sweep_rows(source, target, kap_ref, sweep, rows - sweep, block)
        source, target = target, source
    return source


def fill_picked(pick_ref, picked):
    channels, levels = picked.shape
    pick_ref[...] = jnp.zeros_like(pick_ref)
    for part in range(4):
        pick_ref[
            part * channels : (part + 1) * channels, part * levels : (part + 1) * levels
        ] = picked


def forward_mixing(vertical):
    high, low = split_hi_lo(vertical)
    pair = jnp.concatenate([high, low], axis=1)
    return jnp.concatenate([pair, pair], axis=0)


def project_rows(rows, dev, mixing):
    count, cols, levels = rows.shape
    pair = jnp.concatenate(split_hi_lo(rows.reshape(count * cols, levels)), axis=1)
    both = dot_f32(pair, mixing)
    state = both[:, :levels] + both[:, levels:]
    prof = (dev.reshape(count * cols, levels) * state).astype(BF16)
    prof = prof.reshape(count // 4, 4, cols, levels)
    return jnp.concatenate(
        [prof[:, part].reshape(count // 4 * cols, levels) for part in range(4)], axis=1
    )


def forward_kernel(
    control_hbm, sigma_hbm, east_ref, west_ref, kappa_ref, vertical_ref, table_ref, choice_ref,
    out_ref, pick_ref, first_ref, second_ref, kap_ref, sigma_ref, sem_ref,
):
    rows, cols, levels = control_hbm.shape
    tile_in = start_copies(
        [(control_hbm, first_ref.at[pl.ds(0, rows), pl.ds(0, cols)])], sem_ref
    )
    put_sides(first_ref, 0, rows, cols, east_ref[0], west_ref[0])
    kap_ref[:rows, :cols, :] = spread_kappa(kappa_ref[...])
    put_sides(kap_ref, 0, rows, cols, east_ref[1], west_ref[1])
    wait_copies(tile_in)
    sigma_in = start_copies([(sigma_hbm, sigma_ref)], sem_ref, 1)
    done = sweeps(first_ref, second_ref, kap_ref, rows)
    channels = choice_ref.shape[1]
    table_rows = table_ref.shape[0]
    hot = (iota((table_rows, channels), 0) == choice_ref[...]).astype(F32).astype(BF16)
    fill_picked(pick_ref, dot_tn(hot, table_ref[...]).astype(BF16))
    mixing = forward_mixing(vertical_ref[...])
    wait_copies(sigma_in)
    count = 8
    for index in range((rows - 2 * NSTEP) // count):
        row = NSTEP + index * count
        where = pl.ds(row // 4 * cols, count // 4 * cols)
        out_ref[where, :] = project_rows(
            done[row : row + count, :cols, :], sigma_ref[row : row + count], mixing
        )


def pole_flags():
    at = lax.axis_index("lat")
    last = lax.axis_size("lat") - 1
    return jnp.where(at > 0, 1.0, 0.0), jnp.where(at < last, 1.0, 0.0)


def put_rims(wide_ref, east_of, west_of, north, south, flags, rows, cols):
    span = 2 * NSTEP
    wide_ref[:NSTEP] = north.astype(F32) * flags[0]
    put_sides(wide_ref, NSTEP, span, cols, east_of(0, span), west_of(0, span))
    put_sides(
        wide_ref, NSTEP + span, span, cols, east_of(rows - span, rows), west_of(rows - span, rows)
    )
    wide_ref[NSTEP + 2 * span :] = south.astype(F32) * flags[1]


def rim_tiles(hbm, wide_ref):
    span = 2 * NSTEP
    rows, cols, _ = hbm.shape
    return [
        (hbm.at[pl.ds(0, span)], wide_ref.at[pl.ds(NSTEP, span), pl.ds(0, cols)]),
        (hbm.at[pl.ds(rows - span, span)], wide_ref.at[pl.ds(NSTEP + span, span), pl.ds(0, cols)]),
    ]


def put_rim_kappa(kap_ref, kappa_ref, east_ref, west_ref, north_ref, south_ref, flags):
    rows, cols = kappa_ref.shape
    span = 2 * NSTEP
    kap_ref[NSTEP : NSTEP + 2 * span, :cols, :] = spread_kappa(
        jnp.concatenate([kappa_ref[:span, :], kappa_ref[rows - span :, :]], axis=0)
    )
    put_rims(
        kap_ref,
        lambda low, high: east_ref[1, low:high],
        lambda low, high: west_ref[1, low:high],
        north_ref[1],
        south_ref[1],
        flags,
        rows,
        cols,
    )


def owner_kernel(
    devices_all, quarter, recv_hbm, sigma_hbm, control_hbm, inner_ref, pick_ref, rinv_ref,
    east_ref, west_ref, north_ref, south_ref, kappa_ref, vertical_ref,
    ret_hbm, adj_hbm, left_hbm, right_hbm, top_hbm, bottom_hbm,
    word_ref, dep_ref, acc_ref, first_ref, second_ref, kap_ref, table_ref, pair_ref,
    recv_ref, ret_ref, sigma_ref, adj_ref, left_ref, right_ref, top_ref, bottom_ref,
    sem_ref,
):
    lat_rows, cols, levels = sigma_hbm.shape
    cells_part = inner_ref.shape[0]
    flags = pole_flags()
    span = 2 * NSTEP
    control_in = start_copies(rim_tiles(control_hbm, first_ref), sem_ref)
    others_in = start_copies([(recv_hbm, recv_ref)], sem_ref, 2)
    sigma_in = start_copies([(sigma_hbm, sigma_ref)], sem_ref, 3)
    inside = slice(cols, cells_part - cols)
    table_ref[inside, :] = inner_ref[inside, :]
    put_rim_kappa(kap_ref, kappa_ref, east_ref, west_ref, north_ref, south_ref, flags)
    put_rims(
        first_ref,
        lambda low, high: east_ref[0, low:high],
        lambda low, high: west_ref[0, low:high],
        north_ref[0],
        south_ref[0],
        flags,
        lat_rows,
        cols,
    )
    wait_copies(control_in)
    done = sweeps(first_ref, second_ref, kap_ref, 6 * NSTEP)
    wait_copies(sigma_in)
    ends = project_rows(
        jnp.concatenate(
            [done[NSTEP : 2 * NSTEP, :cols, :], done[4 * NSTEP : 5 * NSTEP, :cols, :]], axis=0
        ),
        jnp.concatenate([sigma_ref[:NSTEP], sigma_ref[lat_rows - NSTEP :]], axis=0),
        forward_mixing(vertical_ref[...]),
    )
    table_ref[:cols, :] = ends[:cols]
    table_ref[cells_part - cols :, :] = ends[cols:]

    wait_copies(others_in)
    rows_half = devices_all * quarter
    rows = 2 * rows_half
    metas = []
    for device in range(devices_all):
        at = device * (quarter + 1)
        word_ref[device * quarter : (device + 1) * quarter, :] = recv_ref[at : at + quarter, :]
        metas.append(recv_ref[at + quarter : at + quarter + 1, :])
    meta = jnp.concatenate(metas, axis=0)
    cells, weights = meta >> 16, meta & 0xFFFF
    facts = jnp.concatenate(
        [
            piece.astype(F32).astype(BF16)
            for piece in (cells >> 6, cells & 63, weights >> 8, weights & 255)
        ],
        axis=1,
    )
    channels = rinv_ref.shape[0]
    pair_ref[...] = jnp.zeros_like(pair_ref)
    pair_ref[:channels, :channels] = rinv_ref[...]
    pair_ref[channels:, channels:] = rinv_ref[...]
    high, low = split_hi_lo(pair_ref[...])
    zero = jnp.zeros_like(high)
    mixing = jnp.concatenate(
        [jnp.concatenate([high, low], axis=1), jnp.concatenate([high, zero], axis=1)], axis=0
    )
    pick_pair = jnp.transpose(
        pick_ref[: 2 * channels, : 2 * levels].astype(F32)
    ).astype(BF16)
    acc_ref[...] = jnp.zeros_like(acc_ref)
    chunk = min(512, rows_half)
    left_lane = iota((chunk, 128), 1) < 64
    lane_half = iota((chunk, 128), 1) // 64
    per_half = rows_half // chunk
    for step in range(rows // chunk):
        half = step // per_half
        base = (step % per_half) * chunk
        row = iota((chunk, devices_all), 0) + base
        spread = (row // quarter == iota((chunk, devices_all), 1)).astype(F32).astype(BF16)
        found = dot_f32(spread, facts)
        lat_lane = found[:, :128]
        lon_lane = found[:, 128:256]
        weight_lane = (found[:, 256:384] * 256.0 + found[:, 384:]) * WEIGHT_STEP
        lane = iota((chunk, 128), 1)
        r = (iota((chunk, 128), 0) + base) % quarter
        hots, parts, weight, values = [], [], [], []
        for side in range(2):
            take = lane == (2 * side + half) * quarter + r
            lat = jnp.sum(jnp.where(take, lat_lane, 0.0), axis=1, keepdims=True).astype(I32)
            lon = jnp.sum(jnp.where(take, lon_lane, 0.0), axis=1, keepdims=True).astype(I32)
            weight.append(jnp.sum(jnp.where(take, weight_lane, 0.0), axis=1, keepdims=True))
            part = lat & 3
            inside = (lat >> 2) * cols + lon
            hot = (iota((chunk, cells_part), 1) == inside).astype(F32).astype(BF16)
            got = dot_f32(hot, table_ref[...])
            low_parts = jnp.where(part == 0, got[:, :levels], got[:, levels : 2 * levels])
            high_parts = jnp.where(
                part == 2, got[:, 2 * levels : 3 * levels], got[:, 3 * levels :]
            )
            values.append(jnp.where(part < 2, low_parts, high_parts).astype(BF16))
            hots.append(hot)
            parts.append(part)
        evolved = dot_f32(jnp.concatenate(values, axis=1), pick_pair)
        words = word_ref[base : base + chunk, :]
        words = (words if half == 0 else words << 16) >> 16
        gap = evolved - words.astype(F32) * INNOV_STEP
        both = dot_f32(jnp.concatenate(split_hi_lo(gap), axis=1), mixing)
        dep = (both[:, :128] + both[:, 128:]) * jnp.where(left_lane, weight[0], weight[1])
        dep_ref[step * chunk : (step + 1) * chunk, :] = encode(evolved)
        rounded = dep.astype(BF16).astype(F32)
        swapped = pltpu.roll(rounded, 64, 1)
        for side in range(2):
            twice = (
                jnp.where(left_lane, rounded, swapped)
                if side == 0
                else jnp.where(left_lane, swapped, rounded)
            )
            wide = jnp.concatenate(
                [
                    jnp.where(parts[side] == lane_half, twice, 0.0).astype(BF16),
                    jnp.where(parts[side] == lane_half + 2, twice, 0.0).astype(BF16),
                ],
                axis=1,
            )
            acc_ref[...] += dot_tn(hots[side], wide)
    ret_ref[...] = (dep_ref[:rows_half, :] << 16) | dep_ref[rows_half:, :]
    copies = start_copies([(ret_ref, ret_hbm)], sem_ref)
    groups = 4
    count = groups * 4
    for step in range(lat_rows // count):
        high, low = split_hi_lo(acc_ref[step * groups * cols : (step + 1) * groups * cols, :])
        both = dot_f32(high, pick_ref[...]) + dot_f32(low, pick_ref[...])
        for group in range(groups):
            for part in range(4):
                at = step * count + group * 4 + part
                value = sigma_ref[at] * both[
                    group * cols : (group + 1) * cols, part * levels : (part + 1) * levels
                ]
                adj_ref[at] = value
                left_ref[at] = value[:NSTEP].astype(BF16)
                right_ref[at] = value[cols - NSTEP :].astype(BF16)
                if at < NSTEP:
                    top_ref[at] = value.astype(BF16)
                if at >= lat_rows - NSTEP:
                    bottom_ref[at - (lat_rows - NSTEP)] = value.astype(BF16)
        where = pl.ds(step * count, count)
        copies += start_copies([(adj_ref.at[where], adj_hbm.at[where])], sem_ref, step + 1)
    copies += start_copies(
        [
            (left_ref, left_hbm),
            (right_ref, right_hbm),
            (top_ref, top_hbm),
            (bottom_ref, bottom_hbm),
        ],
        sem_ref,
        lat_rows // count + 1,
    )
    wait_copies(copies)


def backward_mixing(vertical):
    high, low = split_hi_lo(vertical)
    return jnp.concatenate(
        [jnp.concatenate([high, high], axis=1), jnp.concatenate([low, low], axis=1)], axis=0
    )


def finish_rows(scaled, kap, mixing):
    count, cols, levels = scaled.shape
    adjoint = (scaled / kap).reshape(count * cols, levels)
    both = dot_nt(jnp.concatenate(split_hi_lo(adjoint), axis=1), mixing)
    return (both[:, :levels] + both[:, levels:]).reshape(count, cols, levels)


def inner_kernel(
    adj_hbm, control_hbm, east_ref, west_ref, kappa_ref, keast_ref, kwest_ref, vertical_ref,
    out_hbm, rim_ref, rim_kap_ref, rim_control_ref, first_ref, second_ref, kap_ref, out_ref,
    control_ref, sem_ref,
):
    rows, cols, levels = control_hbm.shape
    tile_in = start_copies([(adj_hbm, first_ref.at[pl.ds(0, rows), pl.ds(0, cols)])], sem_ref)
    kap_ref[:rows, :cols, :] = spread_kappa(kappa_ref[...])
    put_sides(kap_ref, 0, rows, cols, keast_ref[1], kwest_ref[1])
    put_sides(first_ref, 0, rows, cols, east_ref[...], west_ref[...])
    wait_copies(tile_in)
    control_in = start_copies([(control_hbm, control_ref)], sem_ref, 1)
    first_ref[:rows] = first_ref[:rows] * kap_ref[:rows]
    span = 2 * NSTEP
    for end, low in enumerate((0, rows - span)):
        rim_ref[end * span : (end + 1) * span] = first_ref[low : low + span]
        rim_kap_ref[end * span : (end + 1) * span] = kap_ref[low : low + span]
    done = sweeps(first_ref, second_ref, kap_ref, rows)
    mixing = backward_mixing(vertical_ref[...])
    wait_copies(control_in)
    rim_control_ref[0] = control_ref[:NSTEP]
    rim_control_ref[1] = control_ref[rows - NSTEP :]
    count = 8
    copies = []
    for index in range((rows - 2 * NSTEP) // count):
        row = NSTEP + index * count
        at = pl.ds(row, count)
        out_ref[at] = control_ref[at] + finish_rows(
            done[row : row + count, :cols, :], kap_ref[row : row + count, :cols, :], mixing
        )
        copies += start_copies([(out_ref.at[at], out_hbm.at[at])], sem_ref, index)
    wait_copies(copies)


def rim_kernel(
    rim_ref, rim_kap_ref, control_ref, north_ref, south_ref, knorth_ref, ksouth_ref, vertical_ref,
    inner_ref, out_ref, first_ref, second_ref, kap_ref, edge_ref, sem_ref,
):
    del inner_ref
    lat_rows = out_ref.shape[0]
    cols = out_ref.shape[1]
    north_on, south_on = pole_flags()
    tiles = slice(NSTEP, 5 * NSTEP)
    kap_ref[:NSTEP] = knorth_ref[1].astype(F32) * north_on
    kap_ref[tiles] = rim_kap_ref[...]
    kap_ref[5 * NSTEP :] = ksouth_ref[1].astype(F32) * south_on
    first_ref[:NSTEP] = north_ref[...].astype(F32) * kap_ref[:NSTEP]
    first_ref[tiles] = rim_ref[...]
    first_ref[5 * NSTEP :] = south_ref[...].astype(F32) * kap_ref[5 * NSTEP :]
    done = sweeps(first_ref, second_ref, kap_ref, 6 * NSTEP)
    mixing = backward_mixing(vertical_ref[...])
    copies = []
    for end in range(2):
        at = pl.ds((1 + 3 * end) * NSTEP, NSTEP)
        back = finish_rows(done[at, :cols, :], kap_ref[at, :cols, :], mixing)
        edge_ref[end] = control_ref[end] + back
        copies += start_copies(
            [(edge_ref.at[end], out_ref.at[pl.ds(end * (lat_rows - NSTEP), NSTEP)])], sem_ref, end
        )
    wait_copies(copies)


def pass_kernel(array_hbm, first_hbm, second_hbm, out_hbm):
    del array_hbm, first_hbm, second_hbm, out_hbm


def return_kernel(
    devices_all, quarter, count_ref, recv_ref, key_ref, innov_ref, scale_ref, rinv_ref, out_ref,
    pair_ref,
):
    rows_half = devices_all * quarter
    rows = 2 * rows_half
    channels, obs = out_ref.shape
    words = recv_ref[...]
    for half in range(2):
        code = (words >> 16) & 0xFFFF if half == 0 else words & 0xFFFF
        high, low = split_hi_lo(decode(code))
        pair_ref[half * rows_half : (half + 1) * rows_half, :128] = high
        pair_ref[half * rows_half : (half + 1) * rows_half, 128:] = low
    scale = scale_ref[...]
    valid = iota((1, obs), 1) < count_ref[0]
    weight = jnp.where(valid, 1.0 / (scale * scale), 0.0)
    chunk = min(512, obs)
    for start in range(0, obs, chunk):
        key = key_ref[:, start : start + chunk]
        side = key >= rows
        row = jnp.where(side, key - rows, key)
        hot = (iota((rows, chunk), 0) == row).astype(F32).astype(BF16)
        both = dot_tn(pair_ref[...], hot)
        both = both[:128] + both[128:]
        evolved = jnp.where(side, both[channels:], both[:channels])
        gap = evolved - innov_ref[:, start : start + chunk]
        mixed = lax.dot_general(
            rinv_ref[...], gap, (((0,), (0,)), ((), ())), precision=lax.Precision.HIGHEST,
            preferred_element_type=F32,
        )
        out_ref[:, start : start + chunk] = mixed * weight[:, start : start + chunk]


def shifts(axis):
    count = lax.axis_size(axis)
    forward = [(i, (i + 1) % count) for i in range(count)]
    return forward, [(target, source) for source, target in forward]


def exchange_sides(left, right):
    forward, backward = shifts("lon")
    return lax.ppermute(left, "lon", backward), lax.ppermute(right, "lon", forward)


def exchange_rims(top, bottom):
    forward, backward = shifts("lat")
    return lax.ppermute(bottom, "lat", forward), lax.ppermute(top, "lat", backward)


def estimate(flops, bytes_accessed):
    return pl.CostEstimate(flops=flops, bytes_accessed=bytes_accessed, transcendentals=0)


def body(
    control,
    kappa,
    sigma,
    vertical,
    channel_table,
    channel_pick,
    r_inverse,
    innovations,
    error_scale,
    obs_owner,
    obs_cell,
    obs_count,
):
    lat_rows, lon_cols, levels = control.shape
    obs_slots = obs_cell.shape[0]
    channels = innovations.shape[1]
    devices_all = lax.axis_size("lat") * lax.axis_size("lon")
    capacity = max(4, 2 * obs_slots // devices_all)
    quarter = capacity // 4
    rows_half = devices_all * quarter
    columns = lat_rows * lon_cols
    wide = (lat_rows + 1, lon_cols + 2 * NSTEP, levels)
    rim = (6 * NSTEP, lon_cols + 2 * NSTEP, levels)
    smem = pl.BlockSpec(memory_space=pltpu.SMEM)
    anywhere = pl.BlockSpec(memory_space=pl.ANY)

    control, sigma = in_hbm(control), in_hbm(sigma)
    near, far = pl.pallas_call(
        pack_kernel,
        out_shape=(jax.ShapeDtypeStruct((2, lat_rows, NSTEP, levels), BF16),) * 2,
        in_specs=[HBM_SPEC] * 2,
        out_specs=tuple(vmem_specs(2)),
        scratch_shapes=[
            pltpu.VMEM((lat_rows, 8, levels), F32),
            pltpu.VMEM((lat_rows, 8, levels), F32),
            pltpu.VMEM(kappa.shape, F32),
            pltpu.SemaphoreType.DMA((3,)),
        ],
        compiler_params=params(6),
        name="pack",
    )(control, in_hbm(kappa))
    near, far, obs_cell = lax.optimization_barrier((near, far, obs_cell))
    east, west = exchange_sides(near, far)

    payload, key, top, bottom = pl.pallas_call(
        functools.partial(address_kernel, devices_all, quarter),
        out_shape=(
            jax.ShapeDtypeStruct((devices_all * (quarter + 1), 128), I32),
            jax.ShapeDtypeStruct((1, obs_slots), I32),
            jax.ShapeDtypeStruct((2, NSTEP, lon_cols, levels), BF16),
            jax.ShapeDtypeStruct((2, NSTEP, lon_cols, levels), BF16),
        ),
        in_specs=[smem] + vmem_specs(5) + [HBM_SPEC],
        out_specs=tuple(vmem_specs(4)),
        scratch_shapes=[
            pltpu.VMEM((rows_half, 128), I32),
            pltpu.VMEM((2, NSTEP, lon_cols, levels), F32),
            pltpu.SemaphoreType.DMA((2,)),
        ],
        compiler_params=params(10),
        cost_estimate=estimate(2_000_000_000, 8_000_000),
        name="address",
    )(
        obs_count,
        obs_owner.reshape(1, obs_slots),
        obs_cell.reshape(1, obs_slots),
        error_scale.reshape(1, obs_slots),
        innovations.T,
        kappa,
        control,
    )
    received = lax.all_to_all(
        payload.reshape(devices_all, 1, (quarter + 1) * 128),
        ("lat", "lon"),
        split_axis=0,
        concat_axis=0,
        tiled=True,
    ).reshape(payload.shape)

    def with_sides(tile, low, high):
        return jnp.concatenate([tile, east[:, low:high], west[:, low:high]], axis=2)

    north, south = exchange_rims(
        with_sides(top, 0, NSTEP), with_sides(bottom, lat_rows - NSTEP, lat_rows)
    )

    evolved, picked = pl.pallas_call(
        forward_kernel,
        out_shape=(
            pltpu.VMEM((columns // 4, 8 * channels), BF16),
            pltpu.VMEM((4 * channels, 4 * levels), BF16),
        ),
        in_specs=[HBM_SPEC] * 2 + vmem_specs(6),
        out_specs=tuple(vmem_specs(2)),
        scratch_shapes=[pltpu.VMEM(wide, F32)] * 3
        + [pltpu.VMEM(control.shape, F32), pltpu.SemaphoreType.DMA((2,))],
        compiler_params=params(24),
        cost_estimate=estimate(4_000_000_000, 16_000_000),
        name="forward",
    )(
        control, sigma, east, west, kappa, vertical, channel_table,
        channel_pick.reshape(1, channels),
    )

    returned, adjoint, left, right, atop, abottom = pl.pallas_call(
        functools.partial(owner_kernel, devices_all, quarter),
        out_shape=(
            pltpu.HBM((rows_half, 128), I32),
            pltpu.HBM(control.shape, F32),
            pltpu.HBM((lat_rows, NSTEP, levels), BF16),
            pltpu.HBM((lat_rows, NSTEP, levels), BF16),
            jax.ShapeDtypeStruct((NSTEP, lon_cols, levels), BF16),
            jax.ShapeDtypeStruct((NSTEP, lon_cols, levels), BF16),
        ),
        in_specs=[HBM_SPEC] * 3 + vmem_specs(9),
        out_specs=(HBM_SPEC,) * 6,
        scratch_shapes=[
            pltpu.VMEM((rows_half, 128), I32),
            pltpu.VMEM((2 * rows_half, 128), I32),
            pltpu.VMEM((columns // 4, 4 * channels), F32),
            pltpu.VMEM(rim, F32),
            pltpu.VMEM(rim, F32),
            pltpu.VMEM(rim, F32),
            pltpu.VMEM((columns // 4, 8 * channels), BF16),
            pltpu.VMEM((2 * channels, 2 * channels), F32),
            pltpu.VMEM((devices_all * (quarter + 1), 128), I32),
            pltpu.VMEM((rows_half, 128), I32),
            pltpu.VMEM(control.shape, F32),
            pltpu.VMEM(control.shape, F32),
            pltpu.VMEM((lat_rows, NSTEP, levels), BF16),
            pltpu.VMEM((lat_rows, NSTEP, levels), BF16),
            pltpu.VMEM((NSTEP, lon_cols, levels), BF16),
            pltpu.VMEM((NSTEP, lon_cols, levels), BF16),
            pltpu.SemaphoreType.DMA((max(8, lat_rows // 16 + 5),)),
        ],
        compiler_params=params(28),
        cost_estimate=estimate(4_000_000_000, 16_000_000),
        name="owner",
    )(
        received, sigma, control, evolved, picked, r_inverse, east, west, north, south, kappa,
        vertical,
    )
    returned = pl.pallas_call(
        pass_kernel,
        out_shape=pltpu.HBM(returned.shape, I32),
        in_specs=[HBM_SPEC] * 3,
        out_specs=HBM_SPEC,
        input_output_aliases={0: 0},
        cost_estimate=estimate(1_000_000, 1_000_000),
        name="pass",
    )(in_hbm(returned), in_hbm(left), in_hbm(right))
    home = lax.all_to_all(
        returned.reshape(devices_all, quarter, 128),
        ("lat", "lon"),
        split_axis=0,
        concat_axis=0,
        tiled=True,
    ).reshape(returned.shape)

    aeast, awest = exchange_sides(left, right)
    anorth, asouth = exchange_rims(
        jnp.concatenate([atop, aeast[:NSTEP], awest[:NSTEP]], axis=1),
        jnp.concatenate([abottom, aeast[-NSTEP:], awest[-NSTEP:]], axis=1),
    )
    rim_tile = (4 * NSTEP, lon_cols + 2 * NSTEP, levels)
    inner, rim_scaled, rim_kappa, rim_control = pl.pallas_call(
        inner_kernel,
        out_shape=(
            pltpu.HBM(control.shape, F32),
            pltpu.VMEM(rim_tile, F32),
            pltpu.VMEM(rim_tile, F32),
            pltpu.VMEM((2, NSTEP, lon_cols, levels), F32),
        ),
        in_specs=[HBM_SPEC] * 2 + vmem_specs(6),
        out_specs=(HBM_SPEC,) + tuple(vmem_specs(3)),
        scratch_shapes=[pltpu.VMEM(wide, F32)] * 3
        + [pltpu.VMEM(control.shape, F32)] * 2
        + [pltpu.SemaphoreType.DMA((lat_rows // 8,))],
        compiler_params=params(24),
        cost_estimate=estimate(4_000_000_000, 16_000_000),
        name="inner",
    )(in_hbm(adjoint), control, aeast, awest, kappa, east, west, vertical)

    gradient = pl.pallas_call(
        rim_kernel,
        out_shape=jax.ShapeDtypeStruct(control.shape, F32),
        in_specs=vmem_specs(8) + [anywhere],
        out_specs=anywhere,
        scratch_shapes=[pltpu.VMEM(rim, F32)] * 3
        + [
            pltpu.VMEM((2, NSTEP, lon_cols, levels), F32),
            pltpu.SemaphoreType.DMA((2,)),
        ],
        input_output_aliases={8: 0},
        compiler_params=params(12),
        cost_estimate=estimate(1_000_000_000, 2_000_000),
        name="rims",
    )(
        rim_scaled, rim_kappa, rim_control, anorth, asouth, north, south, vertical, inner,
    )

    departures = pl.pallas_call(
        functools.partial(return_kernel, devices_all, quarter),
        out_shape=jax.ShapeDtypeStruct((channels, obs_slots), F32),
        in_specs=[smem] + vmem_specs(5),
        out_specs=vmem_specs(1)[0],
        scratch_shapes=[pltpu.VMEM((2 * rows_half, 256), BF16)],
        compiler_params=params(10),
        cost_estimate=estimate(500_000_000, 2_000_000),
        name="give_back",
    )(
        obs_count, home, key, innovations.T, error_scale.reshape(1, obs_slots),
        r_inverse,
    )
    return (gradient, departures.T)


def solution(mesh):
    return jax.shard_map(
        body,
        mesh=mesh,
        in_specs=(
            P("lat", "lon", None),
            P("lat", "lon"),
            P("lat", "lon", None),
            P(),
            P(),
            P(),
            P(),
            P(("lat", "lon"), None),
            P(("lat", "lon")),
            P(("lat", "lon"), None),
            P(("lat", "lon")),
            P(("lat", "lon")),
        ),
        out_specs=(P("lat", "lon", None), P(("lat", "lon"), None)),
        check_vma=False,
    )
```

```python
import functools

import jax
import jax.numpy as jnp
from jax import lax
from jax.experimental import pallas as pl
from jax.experimental.pallas import tpu as pltpu
from jax.sharding import PartitionSpec as P

NSTEP = 4
F32 = jnp.float32
BF16 = jnp.bfloat16
I32 = jnp.int32
INNOV_MAX = 6.0
INNOV_STEP = INNOV_MAX / 32767.0
WEIGHT_MAX = 4.0
WEIGHT_STEP = WEIGHT_MAX / 65535.0
CODE_FLOOR = -15.0
CODE_STEPS = 1056.0


def split_hi_lo(value):
    high = value.astype(BF16)
    low = (value - high.astype(F32)).astype(BF16)
    return high, low


def encode(value):
    size = jnp.maximum(jnp.abs(value), 2.0**CODE_FLOOR)
    level = (jnp.log2(size) - CODE_FLOOR) * CODE_STEPS + 0.5
    code = jnp.minimum(level, 32767.0).astype(I32)
    return jnp.where(value < 0.0, code + 32768, code)


def decode(code):
    level = code & 32767
    size = jnp.exp2(level.astype(F32) * (1.0 / CODE_STEPS) + CODE_FLOOR)
    size = jnp.where(level == 0, 0.0, size)
    return jnp.where(code >= 32768, -size, size)


def iota(shape, dim):
    return lax.broadcasted_iota(I32, shape, dim)


def dot_f32(left, right):
    return jnp.dot(left, right, preferred_element_type=F32)


def dot_nt(left, right):
    return lax.dot_general(left, right, (((1,), (1,)), ((), ())), preferred_element_type=F32)


def dot_tn(left, right):
    return lax.dot_general(left, right, (((0,), (0,)), ((), ())), preferred_element_type=F32)


def params(mebibytes):
    return pltpu.CompilerParams(vmem_limit_bytes=mebibytes * 1024 * 1024)


HBM_SPEC = pl.BlockSpec(memory_space=pltpu.HBM)


def in_hbm(array):
    return pltpu.with_memory_space_constraint(array, pltpu.HBM)


def start_copies(pairs, sem_ref, first=0):
    copies = []
    for index, (source, target) in enumerate(pairs):
        copy = pltpu.make_async_copy(source, target, sem_ref.at[first + index])
        copy.start()
        copies.append(copy)
    return copies


def wait_copies(copies):
    for copy in copies:
        copy.wait()


def vmem_specs(count):
    return [pl.BlockSpec(memory_space=pltpu.VMEM)] * count


def address_kernel(
    devices_all, quarter, count_ref, owner_ref, cell_ref, scale_ref, innov_ref, kappa_ref,
    control_hbm, out_ref, key_ref, top_ref, bottom_ref, word_ref, ends_ref, sem_ref,
):
    grid_rows = control_hbm.shape[0]
    ends_in = start_copies(
        [
            (control_hbm.at[pl.ds(0, NSTEP)], ends_ref.at[0]),
            (control_hbm.at[pl.ds(grid_rows - NSTEP, NSTEP)], ends_ref.at[1]),
        ],
        sem_ref,
    )
    obs = owner_ref.shape[1]
    rows_half = devices_all * quarter
    rows = 2 * rows_half
    owner = owner_ref[...]
    cell = cell_ref[...]
    mine = iota((devices_all, obs), 0) == owner
    mine_f = mine.astype(F32)
    mine_b = mine_f.astype(BF16)
    block = min(256, obs)
    earlier = (iota((block, block), 0) < iota((block, block), 1)).astype(F32).astype(BF16)
    running = jnp.zeros((devices_all, 1), F32)
    parts = []
    for start in range(0, obs, block):
        piece = mine_f[:, start : start + block]
        before = dot_f32(mine_b[:, start : start + block], earlier) + running
        parts.append(jnp.sum(piece * before, axis=0, keepdims=True))
        running = running + jnp.sum(piece, axis=1, keepdims=True)
    position = jnp.concatenate(parts, axis=1).astype(I32)
    group = position // quarter
    key = (
        (group // 2) * rows + (group % 2) * rows_half + owner * quarter + position % quarter
    )
    key_ref[...] = key
    scale = scale_ref[...]
    valid = iota((1, obs), 1) < count_ref[0]
    weight = jnp.where(valid, 1.0 / (scale * scale), 0.0)
    weight = jnp.minimum(jnp.floor(weight * (1.0 / WEIGHT_STEP) + 0.5), 65535.0)
    weight_high = jnp.floor(weight * (1.0 / 256.0))
    weight_low = weight - 256.0 * weight_high
    cell_high = (cell // 64).astype(F32)
    cell_low = (cell % 64).astype(F32)
    left = jnp.concatenate(
        [mine_f * piece for piece in (cell_high, cell_low, weight_high, weight_low)], axis=0
    ).astype(BF16)
    place = (iota((128, obs), 0) == position).astype(F32).astype(BF16)
    table = dot_nt(left, place).astype(I32)
    n = devices_all
    cells = table[:n] * 64 + table[n : 2 * n]
    weights = table[2 * n : 3 * n] * 256 + table[3 * n :]
    meta = (cells << 16) | weights

    level = jnp.floor(
        jnp.clip(innov_ref[...], -INNOV_MAX, INNOV_MAX) * (1.0 / INNOV_STEP) + 0.5
    )
    high = jnp.floor(level * (1.0 / 256.0))
    low = (level - 256.0 * high).astype(BF16)
    high = high.astype(BF16)
    bytes_of = [jnp.concatenate([high, low], axis=0), jnp.concatenate([low, high], axis=0)]
    chunk = min(256, rows_half)
    left_lane = iota((chunk, 128), 1) < 64
    for base in range(0, rows_half, chunk):
        total = []
        for half in range(2):
            row = iota((chunk, obs), 0) + (base + half * rows_half)
            found = []
            for side in range(2):
                hot = (row + side * rows == key).astype(F32).astype(BF16)
                got = dot_nt(hot, bytes_of[side])
                found.append(got * 256.0 + pltpu.roll(got, 64, 1))
            total.append(jnp.where(left_lane, found[0], found[1]).astype(I32))
        word_ref[base : base + chunk, :] = (total[0] << 16) | (total[1] & 0xFFFF)
    for device in range(devices_all):
        at = device * (quarter + 1)
        out_ref[at : at + quarter, :] = word_ref[device * quarter : (device + 1) * quarter, :]
        out_ref[at + quarter : at + quarter + 1, :] = meta[device : device + 1]
    top_ref[1] = spread_kappa(kappa_ref[:NSTEP, :]).astype(BF16)
    bottom_ref[1] = spread_kappa(kappa_ref[grid_rows - NSTEP :, :]).astype(BF16)
    wait_copies(ends_in)
    top_ref[0] = ends_ref[0].astype(BF16)
    bottom_ref[0] = ends_ref[1].astype(BF16)


def put_sides(wide_ref, at, count, cols, east, west):
    wide_ref[at : at + count, cols : cols + NSTEP, :] = east.astype(F32)
    wide_ref[at : at + count, cols + NSTEP :, :] = west.astype(F32)


def spread_kappa(kappa, low=0, high=None):
    rows, cols = kappa.shape
    count = (cols if high is None else high) - low
    top, rest = split_hi_lo(kappa)
    pair = jnp.concatenate([top.astype(F32), rest.astype(F32)], axis=1)
    shape = (rows, count, 2 * cols)
    hot = iota(shape, 1) + low == iota(shape, 2) % cols
    spread = jnp.where(hot, pair[:, None, :], 0.0).astype(BF16)
    ones = jnp.ones((2 * cols, 128), BF16)
    return dot_f32(spread.reshape(rows * count, 2 * cols), ones).reshape(rows, count, 128)


def pack_kernel(
    control_hbm, kappa_hbm, near_ref, far_ref, left_ref, right_ref, kappa_ref, sem_ref
):
    cols = control_hbm.shape[1]
    kappa_in = start_copies([(kappa_hbm, kappa_ref)], sem_ref, 2)
    copies = start_copies(
        [
            (control_hbm.at[:, pl.ds(0, 8)], left_ref),
            (control_hbm.at[:, pl.ds(cols - 8, 8)], right_ref),
        ],
        sem_ref,
    )
    wait_copies(kappa_in)
    kappa = kappa_ref[...]
    near_ref[1] = spread_kappa(kappa, 0, 8)[:, :NSTEP].astype(BF16)
    far_ref[1] = spread_kappa(kappa, cols - 8, cols)[:, 8 - NSTEP :].astype(BF16)
    wait_copies(copies)
    near_ref[0] = left_ref[:, :NSTEP].astype(BF16)
    far_ref[0] = right_ref[:, 8 - NSTEP :].astype(BF16)


def sweep_rows(source, target, kap_ref, low, high, block=8):
    cols = source.shape[1]

    def update(first, count):
        rows = [source[first + i] for i in range(-1, count + 1)]
        for i in range(count):
            here = rows[i + 1]
            change = (
                (rows[i] + rows[i + 2])
                + (pltpu.roll(here, 1, 0) + pltpu.roll(here, cols - 1, 0))
                - 4.0 * here
            )
            target[first + i] = here + kap_ref[first + i] * change

    whole = (high - low) // block

    def step(index, carry):
        update(low + index * block, block)
        return carry

    lax.fori_loop(0, whole, step, 0)
    if low + whole * block < high:
        update(low + whole * block, high - low - whole * block)


def sweeps(first_ref, second_ref, kap_ref, rows, block=8):
    source, target = first_ref, second_ref
    for sweep in range(1, NSTEP + 1):
        sweep_rows(source, target, kap_ref, sweep, rows - sweep, block)
        source, target = target, source
    return source


def fill_picked(pick_ref, picked):
    channels, levels = picked.shape
    pick_ref[...] = jnp.zeros_like(pick_ref)
    for part in range(4):
        pick_ref[
            part * channels : (part + 1) * channels, part * levels : (part + 1) * levels
        ] = picked


def forward_mixing(vertical):
    high, low = split_hi_lo(vertical)
    pair = jnp.concatenate([high, low], axis=1)
    return jnp.concatenate([pair, pair], axis=0)


def project_rows(rows, dev, mixing):
    count, cols, levels = rows.shape
    pair = jnp.concatenate(split_hi_lo(rows.reshape(count * cols, levels)), axis=1)
    both = dot_f32(pair, mixing)
    state = both[:, :levels] + both[:, levels:]
    prof = (dev.reshape(count * cols, levels) * state).astype(BF16)
    prof = prof.reshape(count // 4, 4, cols, levels)
    return jnp.concatenate(
        [prof[:, part].reshape(count // 4 * cols, levels) for part in range(4)], axis=1
    )


def forward_kernel(
    control_hbm, sigma_hbm, east_ref, west_ref, kappa_ref, vertical_ref, table_ref, choice_ref,
    out_ref, pick_ref, rim_ref, rim_kap_ref, rim_sigma_ref, first_ref, second_ref, kap_ref,
    sigma_ref, sem_ref,
):
    rows, cols, levels = control_hbm.shape
    tile_in = start_copies(
        [(control_hbm, first_ref.at[pl.ds(0, rows), pl.ds(0, cols)])], sem_ref
    )
    put_sides(first_ref, 0, rows, cols, east_ref[0], west_ref[0])
    kap_ref[:rows, :cols, :] = spread_kappa(kappa_ref[...])
    put_sides(kap_ref, 0, rows, cols, east_ref[1], west_ref[1])
    wait_copies(tile_in)
    sigma_in = start_copies([(sigma_hbm, sigma_ref)], sem_ref, 1)
    keep_rims(rim_ref, first_ref, rows)
    keep_rims(rim_kap_ref, kap_ref, rows)
    done = sweeps(first_ref, second_ref, kap_ref, rows)
    channels = choice_ref.shape[1]
    table_rows = table_ref.shape[0]
    hot = (iota((table_rows, channels), 0) == choice_ref[...]).astype(F32).astype(BF16)
    fill_picked(pick_ref, dot_tn(hot, table_ref[...]).astype(BF16))
    mixing = forward_mixing(vertical_ref[...])
    wait_copies(sigma_in)
    rim_sigma_ref[0] = sigma_ref[:NSTEP]
    rim_sigma_ref[1] = sigma_ref[rows - NSTEP :]
    count = 8
    for index in range((rows - 2 * NSTEP) // count):
        row = NSTEP + index * count
        where = pl.ds(row // 4 * cols, count // 4 * cols)
        out_ref[where, :] = project_rows(
            done[row : row + count, :cols, :], sigma_ref[row : row + count], mixing
        )


def keep_rims(rim_ref, wide_ref, rows):
    span = 2 * NSTEP
    for end, low in enumerate((0, rows - span)):
        rim_ref[end * span : (end + 1) * span] = wide_ref[low : low + span]


def pole_flags():
    at = lax.axis_index("lat")
    last = lax.axis_size("lat") - 1
    return jnp.where(at > 0, 1.0, 0.0), jnp.where(at < last, 1.0, 0.0)


def put_rims(wide_ref, rim_ref, north, south):
    wide_ref[:NSTEP] = north
    wide_ref[NSTEP : 5 * NSTEP] = rim_ref[...]
    wide_ref[5 * NSTEP :] = south


def ends_kernel(
    rim_ref, rim_kap_ref, sigma_ref, north_ref, south_ref, vertical_ref, out_ref,
    first_ref, second_ref, kap_ref,
):
    cols = sigma_ref.shape[2]
    north_on, south_on = pole_flags()
    put_rims(
        kap_ref, rim_kap_ref, north_ref[1].astype(F32) * north_on,
        south_ref[1].astype(F32) * south_on,
    )
    put_rims(
        first_ref, rim_ref, north_ref[0].astype(F32) * north_on,
        south_ref[0].astype(F32) * south_on,
    )
    done = sweeps(first_ref, second_ref, kap_ref, 6 * NSTEP)
    mixing = forward_mixing(vertical_ref[...])
    for end in range(2):
        at = slice((1 + 3 * end) * NSTEP, (2 + 3 * end) * NSTEP)
        out_ref[end] = project_rows(done[at, :cols, :], sigma_ref[end], mixing)


def owner_kernel(
    devices_all, quarter, recv_hbm, sigma_hbm, inner_ref, ends_ref, pick_ref, rinv_ref,
    ret_hbm, adj_hbm, left_hbm, right_hbm, top_hbm, bottom_hbm,
    word_ref, dep_ref, acc_ref, table_ref, pair_ref,
    recv_ref, ret_ref, sigma_ref, adj_ref, left_ref, right_ref, top_ref, bottom_ref,
    sem_ref,
):
    lat_rows, cols, levels = sigma_hbm.shape
    cells_part = inner_ref.shape[0]
    others_in = start_copies([(recv_hbm, recv_ref)], sem_ref)
    sigma_in = start_copies([(sigma_hbm, sigma_ref)], sem_ref, 1)
    table_ref[:cols, :] = ends_ref[0]
    table_ref[cols : cells_part - cols, :] = inner_ref[cols : cells_part - cols, :]
    table_ref[cells_part - cols :, :] = ends_ref[1]
    wait_copies(others_in)
    rows_half = devices_all * quarter
    rows = 2 * rows_half
    metas = []
    for device in range(devices_all):
        at = device * (quarter + 1)
        word_ref[device * quarter : (device + 1) * quarter, :] = recv_ref[at : at + quarter, :]
        metas.append(recv_ref[at + quarter : at + quarter + 1, :])
    meta = jnp.concatenate(metas, axis=0)
    cells, weights = meta >> 16, meta & 0xFFFF
    facts = jnp.concatenate(
        [
            piece.astype(F32).astype(BF16)
            for piece in (cells >> 6, cells & 63, weights >> 8, weights & 255)
        ],
        axis=1,
    )
    channels = rinv_ref.shape[0]
    pair_ref[...] = jnp.zeros_like(pair_ref)
    pair_ref[:channels, :channels] = rinv_ref[...]
    pair_ref[channels:, channels:] = rinv_ref[...]
    high, low = split_hi_lo(pair_ref[...])
    zero = jnp.zeros_like(high)
    mixing = jnp.concatenate(
        [jnp.concatenate([high, low], axis=1), jnp.concatenate([high, zero], axis=1)], axis=0
    )
    pick_pair = jnp.transpose(
        pick_ref[: 2 * channels, : 2 * levels].astype(F32)
    ).astype(BF16)
    acc_ref[...] = jnp.zeros_like(acc_ref)
    chunk = min(512, rows_half)
    left_lane = iota((chunk, 128), 1) < 64
    lane_half = iota((chunk, 128), 1) // 64
    per_half = rows_half // chunk
    for step in range(rows // chunk):
        half = step // per_half
        base = (step % per_half) * chunk
        row = iota((chunk, devices_all), 0) + base
        spread = (row // quarter == iota((chunk, devices_all), 1)).astype(F32).astype(BF16)
        found = dot_f32(spread, facts)
        lat_lane = found[:, :128]
        lon_lane = found[:, 128:256]
        weight_lane = (found[:, 256:384] * 256.0 + found[:, 384:]) * WEIGHT_STEP
        lane = iota((chunk, 128), 1)
        r = (iota((chunk, 128), 0) + base) % quarter
        hots, parts, weight, values = [], [], [], []
        for side in range(2):
            take = lane == (2 * side + half) * quarter + r
            lat = jnp.sum(jnp.where(take, lat_lane, 0.0), axis=1, keepdims=True).astype(I32)
            lon = jnp.sum(jnp.where(take, lon_lane, 0.0), axis=1, keepdims=True).astype(I32)
            weight.append(jnp.sum(jnp.where(take, weight_lane, 0.0), axis=1, keepdims=True))
            part = lat & 3
            inside = (lat >> 2) * cols + lon
            hot = (iota((chunk, cells_part), 1) == inside).astype(F32).astype(BF16)
            got = dot_f32(hot, table_ref[...])
            low_parts = jnp.where(part == 0, got[:, :levels], got[:, levels : 2 * levels])
            high_parts = jnp.where(
                part == 2, got[:, 2 * levels : 3 * levels], got[:, 3 * levels :]
            )
            values.append(jnp.where(part < 2, low_parts, high_parts).astype(BF16))
            hots.append(hot)
            parts.append(part)
        evolved = dot_f32(jnp.concatenate(values, axis=1), pick_pair)
        words = word_ref[base : base + chunk, :]
        words = (words if half == 0 else words << 16) >> 16
        gap = evolved - words.astype(F32) * INNOV_STEP
        both = dot_f32(jnp.concatenate(split_hi_lo(gap), axis=1), mixing)
        dep = (both[:, :128] + both[:, 128:]) * jnp.where(left_lane, weight[0], weight[1])
        dep_ref[step * chunk : (step + 1) * chunk, :] = encode(evolved)
        rounded = dep.astype(BF16).astype(F32)
        swapped = pltpu.roll(rounded, 64, 1)
        for side in range(2):
            twice = (
                jnp.where(left_lane, rounded, swapped)
                if side == 0
                else jnp.where(left_lane, swapped, rounded)
            )
            wide = jnp.concatenate(
                [
                    jnp.where(parts[side] == lane_half, twice, 0.0).astype(BF16),
                    jnp.where(parts[side] == lane_half + 2, twice, 0.0).astype(BF16),
                ],
                axis=1,
            )
            acc_ref[...] += dot_tn(hots[side], wide)
    ret_ref[...] = (dep_ref[:rows_half, :] << 16) | dep_ref[rows_half:, :]
    copies = start_copies([(ret_ref, ret_hbm)], sem_ref)
    wait_copies(sigma_in)
    groups = 4
    count = groups * 4
    for step in range(lat_rows // count):
        high, low = split_hi_lo(acc_ref[step * groups * cols : (step + 1) * groups * cols, :])
        both = dot_f32(high, pick_ref[...]) + dot_f32(low, pick_ref[...])
        for group in range(groups):
            for part in range(4):
                at = step * count + group * 4 + part
                value = sigma_ref[at] * both[
                    group * cols : (group + 1) * cols, part * levels : (part + 1) * levels
                ]
                adj_ref[at] = value
                left_ref[at] = value[:NSTEP].astype(BF16)
                right_ref[at] = value[cols - NSTEP :].astype(BF16)
                if at < NSTEP:
                    top_ref[at] = value.astype(BF16)
                if at >= lat_rows - NSTEP:
                    bottom_ref[at - (lat_rows - NSTEP)] = value.astype(BF16)
        where = pl.ds(step * count, count)
        copies += start_copies([(adj_ref.at[where], adj_hbm.at[where])], sem_ref, step + 1)
    copies += start_copies(
        [
            (left_ref, left_hbm),
            (right_ref, right_hbm),
            (top_ref, top_hbm),
            (bottom_ref, bottom_hbm),
        ],
        sem_ref,
        lat_rows // count + 1,
    )
    wait_copies(copies)


def backward_mixing(vertical):
    high, low = split_hi_lo(vertical)
    return jnp.concatenate(
        [jnp.concatenate([high, high], axis=1), jnp.concatenate([low, low], axis=1)], axis=0
    )


def finish_rows(scaled, kap, mixing):
    count, cols, levels = scaled.shape
    adjoint = (scaled / kap).reshape(count * cols, levels)
    both = dot_nt(jnp.concatenate(split_hi_lo(adjoint), axis=1), mixing)
    return (both[:, :levels] + both[:, levels:]).reshape(count, cols, levels)


def inner_kernel(
    adj_hbm, control_hbm, east_ref, west_ref, kappa_ref, keast_ref, kwest_ref, vertical_ref,
    out_hbm, rim_ref, rim_kap_ref, rim_control_ref, first_ref, second_ref, kap_ref, out_ref,
    control_ref, sem_ref,
):
    rows, cols, levels = control_hbm.shape
    tile_in = start_copies([(adj_hbm, first_ref.at[pl.ds(0, rows), pl.ds(0, cols)])], sem_ref)
    kap_ref[:rows, :cols, :] = spread_kappa(kappa_ref[...])
    put_sides(kap_ref, 0, rows, cols, keast_ref[1], kwest_ref[1])
    put_sides(first_ref, 0, rows, cols, east_ref[...], west_ref[...])
    wait_copies(tile_in)
    control_in = start_copies([(control_hbm, control_ref)], sem_ref, 1)
    first_ref[:rows] = first_ref[:rows] * kap_ref[:rows]
    keep_rims(rim_ref, first_ref, rows)
    keep_rims(rim_kap_ref, kap_ref, rows)
    done = sweeps(first_ref, second_ref, kap_ref, rows)
    mixing = backward_mixing(vertical_ref[...])
    wait_copies(control_in)
    rim_control_ref[0] = control_ref[:NSTEP]
    rim_control_ref[1] = control_ref[rows - NSTEP :]
    count = 8
    copies = []
    for index in range((rows - 2 * NSTEP) // count):
        row = NSTEP + index * count
        at = pl.ds(row, count)
        out_ref[at] = control_ref[at] + finish_rows(
            done[row : row + count, :cols, :], kap_ref[row : row + count, :cols, :], mixing
        )
        copies += start_copies([(out_ref.at[at], out_hbm.at[at])], sem_ref, index)
    wait_copies(copies)


def rim_kernel(
    rim_ref, rim_kap_ref, control_ref, north_ref, south_ref, knorth_ref, ksouth_ref, vertical_ref,
    inner_ref, out_ref, first_ref, second_ref, kap_ref, edge_ref, sem_ref,
):
    del inner_ref
    lat_rows = out_ref.shape[0]
    cols = out_ref.shape[1]
    north_on, south_on = pole_flags()
    put_rims(
        kap_ref, rim_kap_ref, knorth_ref[1].astype(F32) * north_on,
        ksouth_ref[1].astype(F32) * south_on,
    )
    put_rims(
        first_ref, rim_ref, north_ref[...].astype(F32) * kap_ref[:NSTEP],
        south_ref[...].astype(F32) * kap_ref[5 * NSTEP :],
    )
    done = sweeps(first_ref, second_ref, kap_ref, 6 * NSTEP)
    mixing = backward_mixing(vertical_ref[...])
    copies = []
    for end in range(2):
        at = pl.ds((1 + 3 * end) * NSTEP, NSTEP)
        back = finish_rows(done[at, :cols, :], kap_ref[at, :cols, :], mixing)
        edge_ref[end] = control_ref[end] + back
        copies += start_copies(
            [(edge_ref.at[end], out_ref.at[pl.ds(end * (lat_rows - NSTEP), NSTEP)])], sem_ref, end
        )
    wait_copies(copies)


def pass_kernel(array_hbm, first_hbm, second_hbm, out_hbm):
    del array_hbm, first_hbm, second_hbm, out_hbm


def return_kernel(
    devices_all, quarter, count_ref, recv_ref, key_ref, innov_ref, scale_ref, rinv_ref, out_ref,
    pair_ref,
):
    rows_half = devices_all * quarter
    rows = 2 * rows_half
    channels, obs = out_ref.shape
    words = recv_ref[...]
    for half in range(2):
        code = (words >> 16) & 0xFFFF if half == 0 else words & 0xFFFF
        high, low = split_hi_lo(decode(code))
        pair_ref[half * rows_half : (half + 1) * rows_half, :128] = high
        pair_ref[half * rows_half : (half + 1) * rows_half, 128:] = low
    scale = scale_ref[...]
    valid = iota((1, obs), 1) < count_ref[0]
    weight = jnp.where(valid, 1.0 / (scale * scale), 0.0)
    chunk = min(512, obs)
    for start in range(0, obs, chunk):
        key = key_ref[:, start : start + chunk]
        side = key >= rows
        row = jnp.where(side, key - rows, key)
        hot = (iota((rows, chunk), 0) == row).astype(F32).astype(BF16)
        both = dot_tn(pair_ref[...], hot)
        both = both[:128] + both[128:]
        evolved = jnp.where(side, both[channels:], both[:channels])
        gap = evolved - innov_ref[:, start : start + chunk]
        mixed = lax.dot_general(
            rinv_ref[...], gap, (((0,), (0,)), ((), ())), precision=lax.Precision.HIGHEST,
            preferred_element_type=F32,
        )
        out_ref[:, start : start + chunk] = mixed * weight[:, start : start + chunk]


def shifts(axis):
    count = lax.axis_size(axis)
    forward = [(i, (i + 1) % count) for i in range(count)]
    return forward, [(target, source) for source, target in forward]


def exchange_sides(left, right):
    forward, backward = shifts("lon")
    return lax.ppermute(left, "lon", backward), lax.ppermute(right, "lon", forward)


def exchange_rims(top, bottom):
    forward, backward = shifts("lat")
    return lax.ppermute(bottom, "lat", forward), lax.ppermute(top, "lat", backward)


def estimate(flops, bytes_accessed):
    return pl.CostEstimate(flops=flops, bytes_accessed=bytes_accessed, transcendentals=0)


def body(
    control,
    kappa,
    sigma,
    vertical,
    channel_table,
    channel_pick,
    r_inverse,
    innovations,
    error_scale,
    obs_owner,
    obs_cell,
    obs_count,
):
    lat_rows, lon_cols, levels = control.shape
    obs_slots = obs_cell.shape[0]
    channels = innovations.shape[1]
    devices_all = lax.axis_size("lat") * lax.axis_size("lon")
    capacity = max(4, 2 * obs_slots // devices_all)
    quarter = capacity // 4
    rows_half = devices_all * quarter
    columns = lat_rows * lon_cols
    wide = (lat_rows + 1, lon_cols + 2 * NSTEP, levels)
    rim_tile = (4 * NSTEP, lon_cols + 2 * NSTEP, levels)
    rim = (6 * NSTEP, lon_cols + 2 * NSTEP, levels)
    smem = pl.BlockSpec(memory_space=pltpu.SMEM)
    anywhere = pl.BlockSpec(memory_space=pl.ANY)

    control, sigma = in_hbm(control), in_hbm(sigma)
    near, far = pl.pallas_call(
        pack_kernel,
        out_shape=(jax.ShapeDtypeStruct((2, lat_rows, NSTEP, levels), BF16),) * 2,
        in_specs=[HBM_SPEC] * 2,
        out_specs=tuple(vmem_specs(2)),
        scratch_shapes=[
            pltpu.VMEM((lat_rows, 8, levels), F32),
            pltpu.VMEM((lat_rows, 8, levels), F32),
            pltpu.VMEM(kappa.shape, F32),
            pltpu.SemaphoreType.DMA((3,)),
        ],
        compiler_params=params(6),
        name="pack",
    )(control, in_hbm(kappa))
    near, far, obs_cell = lax.optimization_barrier((near, far, obs_cell))
    east, west = exchange_sides(near, far)

    payload, key, top, bottom = pl.pallas_call(
        functools.partial(address_kernel, devices_all, quarter),
        out_shape=(
            jax.ShapeDtypeStruct((devices_all * (quarter + 1), 128), I32),
            jax.ShapeDtypeStruct((1, obs_slots), I32),
            jax.ShapeDtypeStruct((2, NSTEP, lon_cols, levels), BF16),
            jax.ShapeDtypeStruct((2, NSTEP, lon_cols, levels), BF16),
        ),
        in_specs=[smem] + vmem_specs(5) + [HBM_SPEC],
        out_specs=tuple(vmem_specs(4)),
        scratch_shapes=[
            pltpu.VMEM((rows_half, 128), I32),
            pltpu.VMEM((2, NSTEP, lon_cols, levels), F32),
            pltpu.SemaphoreType.DMA((2,)),
        ],
        compiler_params=params(10),
        cost_estimate=estimate(2_000_000_000, 8_000_000),
        name="address",
    )(
        obs_count,
        obs_owner.reshape(1, obs_slots),
        obs_cell.reshape(1, obs_slots),
        error_scale.reshape(1, obs_slots),
        innovations.T,
        kappa,
        control,
    )
    received = lax.all_to_all(
        payload.reshape(devices_all, 1, (quarter + 1) * 128),
        ("lat", "lon"),
        split_axis=0,
        concat_axis=0,
        tiled=True,
    ).reshape(payload.shape)

    def with_sides(tile, low, high):
        return jnp.concatenate([tile, east[:, low:high], west[:, low:high]], axis=2)

    north, south = exchange_rims(
        with_sides(top, 0, NSTEP), with_sides(bottom, lat_rows - NSTEP, lat_rows)
    )

    evolved, picked, rim_state, rim_kappa, rim_sigma = pl.pallas_call(
        forward_kernel,
        out_shape=(
            pltpu.VMEM((columns // 4, 8 * channels), BF16),
            pltpu.VMEM((4 * channels, 4 * levels), BF16),
            pltpu.VMEM(rim_tile, F32),
            pltpu.VMEM(rim_tile, F32),
            pltpu.VMEM((2, NSTEP, lon_cols, levels), F32),
        ),
        in_specs=[HBM_SPEC] * 2 + vmem_specs(6),
        out_specs=tuple(vmem_specs(5)),
        scratch_shapes=[pltpu.VMEM(wide, F32)] * 3
        + [pltpu.VMEM(control.shape, F32), pltpu.SemaphoreType.DMA((2,))],
        compiler_params=params(24),
        cost_estimate=estimate(4_000_000_000, 16_000_000),
        name="forward",
    )(
        control, sigma, east, west, kappa, vertical, channel_table,
        channel_pick.reshape(1, channels),
    )

    ends = pl.pallas_call(
        ends_kernel,
        out_shape=pltpu.VMEM((2, lon_cols, 8 * channels), BF16),
        in_specs=vmem_specs(6),
        out_specs=vmem_specs(1)[0],
        scratch_shapes=[pltpu.VMEM(rim, F32)] * 3,
        compiler_params=params(12),
        cost_estimate=estimate(1_000_000_000, 2_000_000),
        name="ends",
    )(rim_state, rim_kappa, rim_sigma, north, south, vertical)

    returned, adjoint, left, right, atop, abottom = pl.pallas_call(
        functools.partial(owner_kernel, devices_all, quarter),
        out_shape=(
            pltpu.HBM((rows_half, 128), I32),
            pltpu.HBM(control.shape, F32),
            pltpu.HBM((lat_rows, NSTEP, levels), BF16),
            pltpu.HBM((lat_rows, NSTEP, levels), BF16),
            jax.ShapeDtypeStruct((NSTEP, lon_cols, levels), BF16),
            jax.ShapeDtypeStruct((NSTEP, lon_cols, levels), BF16),
        ),
        in_specs=[HBM_SPEC] * 2 + vmem_specs(4),
        out_specs=(HBM_SPEC,) * 6,
        scratch_shapes=[
            pltpu.VMEM((rows_half, 128), I32),
            pltpu.VMEM((2 * rows_half, 128), I32),
            pltpu.VMEM((columns // 4, 4 * channels), F32),
            pltpu.VMEM((columns // 4, 8 * channels), BF16),
            pltpu.VMEM((2 * channels, 2 * channels), F32),
            pltpu.VMEM((devices_all * (quarter + 1), 128), I32),
            pltpu.VMEM((rows_half, 128), I32),
            pltpu.VMEM(control.shape, F32),
            pltpu.VMEM(control.shape, F32),
            pltpu.VMEM((lat_rows, NSTEP, levels), BF16),
            pltpu.VMEM((lat_rows, NSTEP, levels), BF16),
            pltpu.VMEM((NSTEP, lon_cols, levels), BF16),
            pltpu.VMEM((NSTEP, lon_cols, levels), BF16),
            pltpu.SemaphoreType.DMA((max(8, lat_rows // 16 + 5),)),
        ],
        compiler_params=params(28),
        cost_estimate=estimate(4_000_000_000, 16_000_000),
        name="owner",
    )(received, sigma, evolved, ends, picked, r_inverse)
    returned = pl.pallas_call(
        pass_kernel,
        out_shape=pltpu.HBM(returned.shape, I32),
        in_specs=[HBM_SPEC] * 3,
        out_specs=HBM_SPEC,
        input_output_aliases={0: 0},
        cost_estimate=estimate(1_000_000, 1_000_000),
        name="pass",
    )(in_hbm(returned), in_hbm(left), in_hbm(right))
    home = lax.all_to_all(
        returned.reshape(devices_all, quarter, 128),
        ("lat", "lon"),
        split_axis=0,
        concat_axis=0,
        tiled=True,
    ).reshape(returned.shape)

    aeast, awest = exchange_sides(left, right)
    anorth, asouth = exchange_rims(
        jnp.concatenate([atop, aeast[:NSTEP], awest[:NSTEP]], axis=1),
        jnp.concatenate([abottom, aeast[-NSTEP:], awest[-NSTEP:]], axis=1),
    )
    inner, rim_scaled, rim_kappa, rim_control = pl.pallas_call(
        inner_kernel,
        out_shape=(
            pltpu.HBM(control.shape, F32),
            pltpu.VMEM(rim_tile, F32),
            pltpu.VMEM(rim_tile, F32),
            pltpu.VMEM((2, NSTEP, lon_cols, levels), F32),
        ),
        in_specs=[HBM_SPEC] * 2 + vmem_specs(6),
        out_specs=(HBM_SPEC,) + tuple(vmem_specs(3)),
        scratch_shapes=[pltpu.VMEM(wide, F32)] * 3
        + [pltpu.VMEM(control.shape, F32)] * 2
        + [pltpu.SemaphoreType.DMA((lat_rows // 8,))],
        compiler_params=params(24),
        cost_estimate=estimate(4_000_000_000, 16_000_000),
        name="inner",
    )(in_hbm(adjoint), control, aeast, awest, kappa, east, west, vertical)

    gradient = pl.pallas_call(
        rim_kernel,
        out_shape=jax.ShapeDtypeStruct(control.shape, F32),
        in_specs=vmem_specs(8) + [anywhere],
        out_specs=anywhere,
        scratch_shapes=[pltpu.VMEM(rim, F32)] * 3
        + [
            pltpu.VMEM((2, NSTEP, lon_cols, levels), F32),
            pltpu.SemaphoreType.DMA((2,)),
        ],
        input_output_aliases={8: 0},
        compiler_params=params(12),
        cost_estimate=estimate(1_000_000_000, 2_000_000),
        name="rims",
    )(
        rim_scaled, rim_kappa, rim_control, anorth, asouth, north, south, vertical, inner,
    )

    departures = pl.pallas_call(
        functools.partial(return_kernel, devices_all, quarter),
        out_shape=jax.ShapeDtypeStruct((channels, obs_slots), F32),
        in_specs=[smem] + vmem_specs(5),
        out_specs=vmem_specs(1)[0],
        scratch_shapes=[pltpu.VMEM((2 * rows_half, 256), BF16)],
        compiler_params=params(10),
        cost_estimate=estimate(500_000_000, 2_000_000),
        name="give_back",
    )(
        obs_count, home, key, innovations.T, error_scale.reshape(1, obs_slots),
        r_inverse,
    )
    return (gradient, departures.T)


def solution(mesh):
    return jax.shard_map(
        body,
        mesh=mesh,
        in_specs=(
            P("lat", "lon", None),
            P("lat", "lon"),
            P("lat", "lon", None),
            P(),
            P(),
            P(),
            P(),
            P(("lat", "lon"), None),
            P(("lat", "lon")),
            P(("lat", "lon"), None),
            P(("lat", "lon")),
            P(("lat", "lon")),
        ),
        out_specs=(P("lat", "lon", None), P(("lat", "lon"), None)),
        check_vma=False,
    )
```

```python
import functools

import jax
import jax.numpy as jnp
from jax import lax
from jax.experimental import pallas as pl
from jax.experimental.pallas import tpu as pltpu
from jax.sharding import PartitionSpec as P

NSTEP = 4
F32 = jnp.float32
BF16 = jnp.bfloat16
I32 = jnp.int32
INNOV_MAX = 6.0
INNOV_STEP = INNOV_MAX / 32767.0
WEIGHT_MAX = 4.0
WEIGHT_STEP = WEIGHT_MAX / 65535.0
CODE_FLOOR = -15.0
CODE_STEPS = 1056.0


def split_hi_lo(value):
    high = value.astype(BF16)
    low = (value - high.astype(F32)).astype(BF16)
    return high, low


def encode(value):
    size = jnp.maximum(jnp.abs(value), 2.0**CODE_FLOOR)
    level = (jnp.log2(size) - CODE_FLOOR) * CODE_STEPS + 0.5
    code = jnp.minimum(level, 32767.0).astype(I32)
    return jnp.where(value < 0.0, code + 32768, code)


def decode(code):
    level = code & 32767
    size = jnp.exp2(level.astype(F32) * (1.0 / CODE_STEPS) + CODE_FLOOR)
    size = jnp.where(level == 0, 0.0, size)
    return jnp.where(code >= 32768, -size, size)


def iota(shape, dim):
    return lax.broadcasted_iota(I32, shape, dim)


def dot_f32(left, right):
    return jnp.dot(left, right, preferred_element_type=F32)


def dot_nt(left, right):
    return lax.dot_general(left, right, (((1,), (1,)), ((), ())), preferred_element_type=F32)


def dot_tn(left, right):
    return lax.dot_general(left, right, (((0,), (0,)), ((), ())), preferred_element_type=F32)


def params(mebibytes):
    return pltpu.CompilerParams(vmem_limit_bytes=mebibytes * 1024 * 1024)


HBM_SPEC = pl.BlockSpec(memory_space=pltpu.HBM)


def in_hbm(array):
    return pltpu.with_memory_space_constraint(array, pltpu.HBM)


def start_copies(pairs, sem_ref, first=0):
    copies = []
    for index, (source, target) in enumerate(pairs):
        copy = pltpu.make_async_copy(source, target, sem_ref.at[first + index])
        copy.start()
        copies.append(copy)
    return copies


def wait_copies(copies):
    for copy in copies:
        copy.wait()


def vmem_specs(count):
    return [pl.BlockSpec(memory_space=pltpu.VMEM)] * count


def address_kernel(
    devices_all, quarter, count_ref, owner_ref, cell_ref, scale_ref, innov_ref, kappa_ref,
    control_hbm, out_ref, key_ref, top_ref, bottom_ref, word_ref, ends_ref, sem_ref,
):
    grid_rows = control_hbm.shape[0]
    ends_in = start_copies(
        [
            (control_hbm.at[pl.ds(0, NSTEP)], ends_ref.at[0]),
            (control_hbm.at[pl.ds(grid_rows - NSTEP, NSTEP)], ends_ref.at[1]),
        ],
        sem_ref,
    )
    obs = owner_ref.shape[1]
    rows_half = devices_all * quarter
    rows = 2 * rows_half
    owner = owner_ref[...]
    cell = cell_ref[...]
    mine = iota((devices_all, obs), 0) == owner
    mine_f = mine.astype(F32)
    mine_b = mine_f.astype(BF16)
    block = min(256, obs)
    earlier = (iota((block, block), 0) < iota((block, block), 1)).astype(F32).astype(BF16)
    running = jnp.zeros((devices_all, 1), F32)
    parts = []
    for start in range(0, obs, block):
        piece = mine_f[:, start : start + block]
        before = dot_f32(mine_b[:, start : start + block], earlier) + running
        parts.append(jnp.sum(piece * before, axis=0, keepdims=True))
        running = running + jnp.sum(piece, axis=1, keepdims=True)
    position = jnp.concatenate(parts, axis=1).astype(I32)
    group = position // quarter
    key = (
        (group // 2) * rows + (group % 2) * rows_half + owner * quarter + position % quarter
    )
    key_ref[...] = key
    scale = scale_ref[...]
    valid = iota((1, obs), 1) < count_ref[0]
    weight = jnp.where(valid, 1.0 / (scale * scale), 0.0)
    weight = jnp.minimum(jnp.floor(weight * (1.0 / WEIGHT_STEP) + 0.5), 65535.0)
    weight_high = jnp.floor(weight * (1.0 / 256.0))
    weight_low = weight - 256.0 * weight_high
    cell_high = (cell // 64).astype(F32)
    cell_low = (cell % 64).astype(F32)
    left = jnp.concatenate(
        [mine_f * piece for piece in (cell_high, cell_low, weight_high, weight_low)], axis=0
    ).astype(BF16)
    place = (iota((128, obs), 0) == position).astype(F32).astype(BF16)
    table = dot_nt(left, place).astype(I32)
    n = devices_all
    cells = table[:n] * 64 + table[n : 2 * n]
    weights = table[2 * n : 3 * n] * 256 + table[3 * n :]
    meta = (cells << 16) | weights

    level = jnp.floor(
        jnp.clip(innov_ref[...], -INNOV_MAX, INNOV_MAX) * (1.0 / INNOV_STEP) + 0.5
    )
    high = jnp.floor(level * (1.0 / 256.0))
    low = (level - 256.0 * high).astype(BF16)
    high = high.astype(BF16)
    bytes_of = [jnp.concatenate([high, low], axis=0), jnp.concatenate([low, high], axis=0)]
    chunk = min(256, rows_half)
    left_lane = iota((chunk, 128), 1) < 64
    for base in range(0, rows_half, chunk):
        total = []
        for half in range(2):
            row = iota((chunk, obs), 0) + (base + half * rows_half)
            found = []
            for side in range(2):
                hot = (row + side * rows == key).astype(F32).astype(BF16)
                got = dot_nt(hot, bytes_of[side])
                found.append(got * 256.0 + pltpu.roll(got, 64, 1))
            total.append(jnp.where(left_lane, found[0], found[1]).astype(I32))
        word_ref[base : base + chunk, :] = (total[0] << 16) | (total[1] & 0xFFFF)
    for device in range(devices_all):
        at = device * (quarter + 1)
        out_ref[at : at + quarter, :] = word_ref[device * quarter : (device + 1) * quarter, :]
        out_ref[at + quarter : at + quarter + 1, :] = meta[device : device + 1]
    top_ref[1] = spread_kappa(kappa_ref[:NSTEP, :]).astype(BF16)
    bottom_ref[1] = spread_kappa(kappa_ref[grid_rows - NSTEP :, :]).astype(BF16)
    wait_copies(ends_in)
    top_ref[0] = ends_ref[0].astype(BF16)
    bottom_ref[0] = ends_ref[1].astype(BF16)


LEAD = 16


def tile_of(cols):
    return slice(LEAD, LEAD + cols)


def put_sides(wide_ref, at, count, cols, east, west):
    wide_ref[at : at + count, LEAD + cols : LEAD + cols + NSTEP, :] = east.astype(F32)
    wide_ref[at : at + count, LEAD - NSTEP : LEAD, :] = west.astype(F32)


def spread_kappa(kappa, low=0, high=None):
    rows, cols = kappa.shape
    count = (cols if high is None else high) - low
    top, rest = split_hi_lo(kappa)
    pair = jnp.concatenate([top.astype(F32), rest.astype(F32)], axis=1)
    shape = (rows, count, 2 * cols)
    hot = iota(shape, 1) + low == iota(shape, 2) % cols
    spread = jnp.where(hot, pair[:, None, :], 0.0).astype(BF16)
    ones = jnp.ones((2 * cols, 128), BF16)
    return dot_f32(spread.reshape(rows * count, 2 * cols), ones).reshape(rows, count, 128)


def pack_kernel(
    control_hbm, kappa_hbm, near_ref, far_ref, left_ref, right_ref, kappa_ref, sem_ref
):
    cols = control_hbm.shape[1]
    kappa_in = start_copies([(kappa_hbm, kappa_ref)], sem_ref, 2)
    copies = start_copies(
        [
            (control_hbm.at[:, pl.ds(0, 8)], left_ref),
            (control_hbm.at[:, pl.ds(cols - 8, 8)], right_ref),
        ],
        sem_ref,
    )
    wait_copies(kappa_in)
    kappa = kappa_ref[...]
    near_ref[1] = spread_kappa(kappa, 0, 8)[:, :NSTEP].astype(BF16)
    far_ref[1] = spread_kappa(kappa, cols - 8, cols)[:, 8 - NSTEP :].astype(BF16)
    wait_copies(copies)
    near_ref[0] = left_ref[:, :NSTEP].astype(BF16)
    far_ref[0] = right_ref[:, 8 - NSTEP :].astype(BF16)


def sweep_rows(source, target, kap_ref, low, high, block=8):
    width = source.shape[1]
    here_at = slice(8, width - 8)

    def update(first, count):
        rows = [source[first + i, here_at, :] for i in range(-1, count + 1)]
        for i in range(count):
            here = rows[i + 1]
            change = (
                (rows[i] + rows[i + 2])
                + (source[first + i, 7 : width - 9, :] + source[first + i, 9 : width - 7, :])
                - 4.0 * here
            )
            target[first + i, here_at, :] = here + kap_ref[first + i, here_at, :] * change

    whole = (high - low) // block

    def step(index, carry):
        update(low + index * block, block)
        return carry

    lax.fori_loop(0, whole, step, 0)
    if low + whole * block < high:
        update(low + whole * block, high - low - whole * block)


def sweeps(first_ref, second_ref, kap_ref, rows, block=8):
    source, target = first_ref, second_ref
    for sweep in range(1, NSTEP + 1):
        sweep_rows(source, target, kap_ref, sweep, rows - sweep, block)
        source, target = target, source
    return source


def fill_picked(pick_ref, picked):
    channels, levels = picked.shape
    pick_ref[...] = jnp.zeros_like(pick_ref)
    for part in range(4):
        pick_ref[
            part * channels : (part + 1) * channels, part * levels : (part + 1) * levels
        ] = picked


def forward_mixing(vertical):
    high, low = split_hi_lo(vertical)
    pair = jnp.concatenate([high, low], axis=1)
    return jnp.concatenate([pair, pair], axis=0)


def project_rows(rows, dev, mixing):
    count, cols, levels = rows.shape
    pair = jnp.concatenate(split_hi_lo(rows.reshape(count * cols, levels)), axis=1)
    both = dot_f32(pair, mixing)
    state = both[:, :levels] + both[:, levels:]
    prof = (dev.reshape(count * cols, levels) * state).astype(BF16)
    prof = prof.reshape(count // 4, 4, cols, levels)
    return jnp.concatenate(
        [prof[:, part].reshape(count // 4 * cols, levels) for part in range(4)], axis=1
    )


def forward_kernel(
    control_hbm, sigma_hbm, east_ref, west_ref, kappa_ref, vertical_ref, table_ref, choice_ref,
    out_ref, pick_ref, rim_ref, rim_kap_ref, rim_sigma_ref, first_ref, second_ref, kap_ref,
    sigma_ref, sem_ref,
):
    rows, cols, levels = control_hbm.shape
    tile_in = start_copies(
        [(control_hbm, first_ref.at[pl.ds(0, rows), pl.ds(LEAD, cols)])], sem_ref
    )
    put_sides(first_ref, 0, rows, cols, east_ref[0], west_ref[0])
    kap_ref[:rows, tile_of(cols), :] = spread_kappa(kappa_ref[...])
    put_sides(kap_ref, 0, rows, cols, east_ref[1], west_ref[1])
    wait_copies(tile_in)
    sigma_in = start_copies([(sigma_hbm, sigma_ref)], sem_ref, 1)
    keep_rims(rim_ref, first_ref, rows)
    keep_rims(rim_kap_ref, kap_ref, rows)
    done = sweeps(first_ref, second_ref, kap_ref, rows)
    channels = choice_ref.shape[1]
    table_rows = table_ref.shape[0]
    hot = (iota((table_rows, channels), 0) == choice_ref[...]).astype(F32).astype(BF16)
    fill_picked(pick_ref, dot_tn(hot, table_ref[...]).astype(BF16))
    mixing = forward_mixing(vertical_ref[...])
    wait_copies(sigma_in)
    rim_sigma_ref[0] = sigma_ref[:NSTEP]
    rim_sigma_ref[1] = sigma_ref[rows - NSTEP :]
    count = 8
    for index in range((rows - 2 * NSTEP) // count):
        row = NSTEP + index * count
        where = pl.ds(row // 4 * cols, count // 4 * cols)
        out_ref[where, :] = project_rows(
            done[row : row + count, tile_of(cols), :], sigma_ref[row : row + count], mixing
        )


def keep_rims(rim_ref, wide_ref, rows):
    span = 2 * NSTEP
    for end, low in enumerate((0, rows - span)):
        rim_ref[end * span : (end + 1) * span] = wide_ref[low : low + span]


def pole_flags():
    at = lax.axis_index("lat")
    last = lax.axis_size("lat") - 1
    return jnp.where(at > 0, 1.0, 0.0), jnp.where(at < last, 1.0, 0.0)


def put_rims(wide_ref, rim_ref, north, south, cols):
    wide_ref[NSTEP : 5 * NSTEP] = rim_ref[...]
    for at, rim in ((0, north), (5 * NSTEP, south)):
        wide_ref[at : at + NSTEP, tile_of(cols), :] = rim[:, :cols]
        put_sides(
            wide_ref, at, NSTEP, cols, rim[:, cols : cols + NSTEP], rim[:, cols + NSTEP :]
        )


def ends_kernel(
    rim_ref, rim_kap_ref, sigma_ref, north_ref, south_ref, vertical_ref, out_ref,
    first_ref, second_ref, kap_ref,
):
    cols = sigma_ref.shape[2]
    north_on, south_on = pole_flags()
    put_rims(
        kap_ref, rim_kap_ref, north_ref[1].astype(F32) * north_on,
        south_ref[1].astype(F32) * south_on, cols,
    )
    put_rims(
        first_ref, rim_ref, north_ref[0].astype(F32) * north_on,
        south_ref[0].astype(F32) * south_on, cols,
    )
    done = sweeps(first_ref, second_ref, kap_ref, 6 * NSTEP)
    mixing = forward_mixing(vertical_ref[...])
    for end in range(2):
        at = slice((1 + 3 * end) * NSTEP, (2 + 3 * end) * NSTEP)
        out_ref[end] = project_rows(done[at, tile_of(cols), :], sigma_ref[end], mixing)


def owner_kernel(
    devices_all, quarter, recv_hbm, sigma_hbm, inner_ref, ends_ref, pick_ref, rinv_ref,
    ret_hbm, adj_hbm, left_hbm, right_hbm, top_hbm, bottom_hbm,
    word_ref, dep_ref, acc_ref, table_ref, pair_ref,
    recv_ref, ret_ref, sigma_ref, adj_ref, left_ref, right_ref, top_ref, bottom_ref,
    sem_ref,
):
    lat_rows, cols, levels = sigma_hbm.shape
    cells_part = inner_ref.shape[0]
    others_in = start_copies([(recv_hbm, recv_ref)], sem_ref)
    sigma_in = start_copies([(sigma_hbm, sigma_ref)], sem_ref, 1)
    table_ref[:cols, :] = ends_ref[0]
    table_ref[cols : cells_part - cols, :] = inner_ref[cols : cells_part - cols, :]
    table_ref[cells_part - cols :, :] = ends_ref[1]
    wait_copies(others_in)
    rows_half = devices_all * quarter
    rows = 2 * rows_half
    metas = []
    for device in range(devices_all):
        at = device * (quarter + 1)
        word_ref[device * quarter : (device + 1) * quarter, :] = recv_ref[at : at + quarter, :]
        metas.append(recv_ref[at + quarter : at + quarter + 1, :])
    meta = jnp.concatenate(metas, axis=0)
    cells, weights = meta >> 16, meta & 0xFFFF
    facts = jnp.concatenate(
        [
            piece.astype(F32).astype(BF16)
            for piece in (cells >> 6, cells & 63, weights >> 8, weights & 255)
        ],
        axis=1,
    )
    channels = rinv_ref.shape[0]
    pair_ref[...] = jnp.zeros_like(pair_ref)
    pair_ref[:channels, :channels] = rinv_ref[...]
    pair_ref[channels:, channels:] = rinv_ref[...]
    high, low = split_hi_lo(pair_ref[...])
    zero = jnp.zeros_like(high)
    mixing = jnp.concatenate(
        [jnp.concatenate([high, low], axis=1), jnp.concatenate([high, zero], axis=1)], axis=0
    )
    pick_pair = jnp.transpose(
        pick_ref[: 2 * channels, : 2 * levels].astype(F32)
    ).astype(BF16)
    acc_ref[...] = jnp.zeros_like(acc_ref)
    chunk = min(512, rows_half)
    left_lane = iota((chunk, 128), 1) < 64
    lane_half = iota((chunk, 128), 1) // 64
    per_half = rows_half // chunk
    for step in range(rows // chunk):
        half = step // per_half
        base = (step % per_half) * chunk
        row = iota((chunk, devices_all), 0) + base
        spread = (row // quarter == iota((chunk, devices_all), 1)).astype(F32).astype(BF16)
        found = dot_f32(spread, facts)
        lat_lane = found[:, :128]
        lon_lane = found[:, 128:256]
        weight_lane = (found[:, 256:384] * 256.0 + found[:, 384:]) * WEIGHT_STEP
        lane = iota((chunk, 128), 1)
        r = (iota((chunk, 128), 0) + base) % quarter
        hots, parts, weight, values = [], [], [], []
        for side in range(2):
            take = lane == (2 * side + half) * quarter + r
            lat = jnp.sum(jnp.where(take, lat_lane, 0.0), axis=1, keepdims=True).astype(I32)
            lon = jnp.sum(jnp.where(take, lon_lane, 0.0), axis=1, keepdims=True).astype(I32)
            weight.append(jnp.sum(jnp.where(take, weight_lane, 0.0), axis=1, keepdims=True))
            part = lat & 3
            inside = (lat >> 2) * cols + lon
            hot = (iota((chunk, cells_part), 1) == inside).astype(F32).astype(BF16)
            got = dot_f32(hot, table_ref[...])
            low_parts = jnp.where(part == 0, got[:, :levels], got[:, levels : 2 * levels])
            high_parts = jnp.where(
                part == 2, got[:, 2 * levels : 3 * levels], got[:, 3 * levels :]
            )
            values.append(jnp.where(part < 2, low_parts, high_parts).astype(BF16))
            hots.append(hot)
            parts.append(part)
        evolved = dot_f32(jnp.concatenate(values, axis=1), pick_pair)
        words = word_ref[base : base + chunk, :]
        words = (words if half == 0 else words << 16) >> 16
        gap = evolved - words.astype(F32) * INNOV_STEP
        both = dot_f32(jnp.concatenate(split_hi_lo(gap), axis=1), mixing)
        dep = (both[:, :128] + both[:, 128:]) * jnp.where(left_lane, weight[0], weight[1])
        dep_ref[step * chunk : (step + 1) * chunk, :] = encode(evolved)
        rounded = dep.astype(BF16).astype(F32)
        swapped = pltpu.roll(rounded, 64, 1)
        for side in range(2):
            twice = (
                jnp.where(left_lane, rounded, swapped)
                if side == 0
                else jnp.where(left_lane, swapped, rounded)
            )
            wide = jnp.concatenate(
                [
                    jnp.where(parts[side] == lane_half, twice, 0.0).astype(BF16),
                    jnp.where(parts[side] == lane_half + 2, twice, 0.0).astype(BF16),
                ],
                axis=1,
            )
            acc_ref[...] += dot_tn(hots[side], wide)
    ret_ref[...] = (dep_ref[:rows_half, :] << 16) | dep_ref[rows_half:, :]
    copies = start_copies([(ret_ref, ret_hbm)], sem_ref)
    wait_copies(sigma_in)
    groups = 4
    count = groups * 4
    for step in range(lat_rows // count):
        high, low = split_hi_lo(acc_ref[step * groups * cols : (step + 1) * groups * cols, :])
        both = dot_f32(high, pick_ref[...]) + dot_f32(low, pick_ref[...])
        for group in range(groups):
            for part in range(4):
                at = step * count + group * 4 + part
                value = sigma_ref[at] * both[
                    group * cols : (group + 1) * cols, part * levels : (part + 1) * levels
                ]
                adj_ref[at] = value
                left_ref[at] = value[:NSTEP].astype(BF16)
                right_ref[at] = value[cols - NSTEP :].astype(BF16)
                if at < NSTEP:
                    top_ref[at] = value.astype(BF16)
                if at >= lat_rows - NSTEP:
                    bottom_ref[at - (lat_rows - NSTEP)] = value.astype(BF16)
        where = pl.ds(step * count, count)
        copies += start_copies([(adj_ref.at[where], adj_hbm.at[where])], sem_ref, step + 1)
    copies += start_copies(
        [
            (left_ref, left_hbm),
            (right_ref, right_hbm),
            (top_ref, top_hbm),
            (bottom_ref, bottom_hbm),
        ],
        sem_ref,
        lat_rows // count + 1,
    )
    wait_copies(copies)


def backward_mixing(vertical):
    high, low = split_hi_lo(vertical)
    return jnp.concatenate(
        [jnp.concatenate([high, high], axis=1), jnp.concatenate([low, low], axis=1)], axis=0
    )


def finish_rows(scaled, kap, mixing):
    count, cols, levels = scaled.shape
    adjoint = (scaled / kap).reshape(count * cols, levels)
    both = dot_nt(jnp.concatenate(split_hi_lo(adjoint), axis=1), mixing)
    return (both[:, :levels] + both[:, levels:]).reshape(count, cols, levels)


def inner_kernel(
    adj_hbm, control_hbm, east_ref, west_ref, kappa_ref, keast_ref, kwest_ref, vertical_ref,
    out_hbm, rim_ref, rim_kap_ref, rim_control_ref, first_ref, second_ref, kap_ref, out_ref,
    control_ref, sem_ref,
):
    rows, cols, levels = control_hbm.shape
    tile_in = start_copies([(adj_hbm, first_ref.at[pl.ds(0, rows), pl.ds(LEAD, cols)])], sem_ref)
    kap_ref[:rows, tile_of(cols), :] = spread_kappa(kappa_ref[...])
    put_sides(kap_ref, 0, rows, cols, keast_ref[1], kwest_ref[1])
    put_sides(first_ref, 0, rows, cols, east_ref[...], west_ref[...])
    wait_copies(tile_in)
    control_in = start_copies([(control_hbm, control_ref)], sem_ref, 1)
    first_ref[:rows] = first_ref[:rows] * kap_ref[:rows]
    keep_rims(rim_ref, first_ref, rows)
    keep_rims(rim_kap_ref, kap_ref, rows)
    done = sweeps(first_ref, second_ref, kap_ref, rows)
    mixing = backward_mixing(vertical_ref[...])
    wait_copies(control_in)
    rim_control_ref[0] = control_ref[:NSTEP]
    rim_control_ref[1] = control_ref[rows - NSTEP :]
    count = 8
    copies = []
    for index in range((rows - 2 * NSTEP) // count):
        row = NSTEP + index * count
        at = pl.ds(row, count)
        out_ref[at] = control_ref[at] + finish_rows(
            done[row : row + count, tile_of(cols), :], kap_ref[row : row + count, tile_of(cols), :], mixing
        )
        copies += start_copies([(out_ref.at[at], out_hbm.at[at])], sem_ref, index)
    wait_copies(copies)


def rim_kernel(
    rim_ref, rim_kap_ref, control_ref, north_ref, south_ref, knorth_ref, ksouth_ref, vertical_ref,
    inner_ref, out_ref, first_ref, second_ref, kap_ref, edge_ref, sem_ref,
):
    del inner_ref
    lat_rows = out_ref.shape[0]
    cols = out_ref.shape[1]
    north_on, south_on = pole_flags()
    put_rims(
        kap_ref, rim_kap_ref, knorth_ref[1].astype(F32) * north_on,
        ksouth_ref[1].astype(F32) * south_on, cols,
    )
    put_rims(
        first_ref, rim_ref, north_ref[...].astype(F32), south_ref[...].astype(F32), cols
    )
    for at in (0, 5 * NSTEP):
        first_ref[at : at + NSTEP] = first_ref[at : at + NSTEP] * kap_ref[at : at + NSTEP]
    done = sweeps(first_ref, second_ref, kap_ref, 6 * NSTEP)
    mixing = backward_mixing(vertical_ref[...])
    copies = []
    for end in range(2):
        at = pl.ds((1 + 3 * end) * NSTEP, NSTEP)
        back = finish_rows(done[at, tile_of(cols), :], kap_ref[at, tile_of(cols), :], mixing)
        edge_ref[end] = control_ref[end] + back
        copies += start_copies(
            [(edge_ref.at[end], out_ref.at[pl.ds(end * (lat_rows - NSTEP), NSTEP)])], sem_ref, end
        )
    wait_copies(copies)


def pass_kernel(array_hbm, first_hbm, second_hbm, out_hbm):
    del array_hbm, first_hbm, second_hbm, out_hbm


def return_kernel(
    devices_all, quarter, count_ref, recv_ref, key_ref, innov_ref, scale_ref, rinv_ref, out_ref,
    pair_ref,
):
    rows_half = devices_all * quarter
    rows = 2 * rows_half
    channels, obs = out_ref.shape
    words = recv_ref[...]
    for half in range(2):
        code = (words >> 16) & 0xFFFF if half == 0 else words & 0xFFFF
        high, low = split_hi_lo(decode(code))
        pair_ref[half * rows_half : (half + 1) * rows_half, :128] = high
        pair_ref[half * rows_half : (half + 1) * rows_half, 128:] = low
    scale = scale_ref[...]
    valid = iota((1, obs), 1) < count_ref[0]
    weight = jnp.where(valid, 1.0 / (scale * scale), 0.0)
    chunk = min(512, obs)
    for start in range(0, obs, chunk):
        key = key_ref[:, start : start + chunk]
        side = key >= rows
        row = jnp.where(side, key - rows, key)
        hot = (iota((rows, chunk), 0) == row).astype(F32).astype(BF16)
        both = dot_tn(pair_ref[...], hot)
        both = both[:128] + both[128:]
        evolved = jnp.where(side, both[channels:], both[:channels])
        gap = evolved - innov_ref[:, start : start + chunk]
        mixed = lax.dot_general(
            rinv_ref[...], gap, (((0,), (0,)), ((), ())), precision=lax.Precision.HIGHEST,
            preferred_element_type=F32,
        )
        out_ref[:, start : start + chunk] = mixed * weight[:, start : start + chunk]


def shifts(axis):
    count = lax.axis_size(axis)
    forward = [(i, (i + 1) % count) for i in range(count)]
    return forward, [(target, source) for source, target in forward]


def exchange_sides(left, right):
    forward, backward = shifts("lon")
    return lax.ppermute(left, "lon", backward), lax.ppermute(right, "lon", forward)


def exchange_rims(top, bottom):
    forward, backward = shifts("lat")
    return lax.ppermute(bottom, "lat", forward), lax.ppermute(top, "lat", backward)


def estimate(flops, bytes_accessed):
    return pl.CostEstimate(flops=flops, bytes_accessed=bytes_accessed, transcendentals=0)


def body(
    control,
    kappa,
    sigma,
    vertical,
    channel_table,
    channel_pick,
    r_inverse,
    innovations,
    error_scale,
    obs_owner,
    obs_cell,
    obs_count,
):
    lat_rows, lon_cols, levels = control.shape
    obs_slots = obs_cell.shape[0]
    channels = innovations.shape[1]
    devices_all = lax.axis_size("lat") * lax.axis_size("lon")
    capacity = max(4, 2 * obs_slots // devices_all)
    quarter = capacity // 4
    rows_half = devices_all * quarter
    columns = lat_rows * lon_cols
    wide = (lat_rows + 1, lon_cols + 2 * LEAD, levels)
    rim_tile = (4 * NSTEP, lon_cols + 2 * LEAD, levels)
    rim = (6 * NSTEP, lon_cols + 2 * LEAD, levels)
    smem = pl.BlockSpec(memory_space=pltpu.SMEM)
    anywhere = pl.BlockSpec(memory_space=pl.ANY)

    control, sigma = in_hbm(control), in_hbm(sigma)
    near, far = pl.pallas_call(
        pack_kernel,
        out_shape=(jax.ShapeDtypeStruct((2, lat_rows, NSTEP, levels), BF16),) * 2,
        in_specs=[HBM_SPEC] * 2,
        out_specs=tuple(vmem_specs(2)),
        scratch_shapes=[
            pltpu.VMEM((lat_rows, 8, levels), F32),
            pltpu.VMEM((lat_rows, 8, levels), F32),
            pltpu.VMEM(kappa.shape, F32),
            pltpu.SemaphoreType.DMA((3,)),
        ],
        compiler_params=params(6),
        name="pack",
    )(control, in_hbm(kappa))
    near, far, obs_cell = lax.optimization_barrier((near, far, obs_cell))
    east, west = exchange_sides(near, far)

    payload, key, top, bottom = pl.pallas_call(
        functools.partial(address_kernel, devices_all, quarter),
        out_shape=(
            jax.ShapeDtypeStruct((devices_all * (quarter + 1), 128), I32),
            jax.ShapeDtypeStruct((1, obs_slots), I32),
            jax.ShapeDtypeStruct((2, NSTEP, lon_cols, levels), BF16),
            jax.ShapeDtypeStruct((2, NSTEP, lon_cols, levels), BF16),
        ),
        in_specs=[smem] + vmem_specs(5) + [HBM_SPEC],
        out_specs=tuple(vmem_specs(4)),
        scratch_shapes=[
            pltpu.VMEM((rows_half, 128), I32),
            pltpu.VMEM((2, NSTEP, lon_cols, levels), F32),
            pltpu.SemaphoreType.DMA((2,)),
        ],
        compiler_params=params(10),
        cost_estimate=estimate(2_000_000_000, 8_000_000),
        name="address",
    )(
        obs_count,
        obs_owner.reshape(1, obs_slots),
        obs_cell.reshape(1, obs_slots),
        error_scale.reshape(1, obs_slots),
        innovations.T,
        kappa,
        control,
    )
    received = lax.all_to_all(
        payload.reshape(devices_all, 1, (quarter + 1) * 128),
        ("lat", "lon"),
        split_axis=0,
        concat_axis=0,
        tiled=True,
    ).reshape(payload.shape)

    def with_sides(tile, low, high):
        return jnp.concatenate([tile, east[:, low:high], west[:, low:high]], axis=2)

    north, south = exchange_rims(
        with_sides(top, 0, NSTEP), with_sides(bottom, lat_rows - NSTEP, lat_rows)
    )

    evolved, picked, rim_state, rim_kappa, rim_sigma = pl.pallas_call(
        forward_kernel,
        out_shape=(
            pltpu.VMEM((columns // 4, 8 * channels), BF16),
            pltpu.VMEM((4 * channels, 4 * levels), BF16),
            pltpu.VMEM(rim_tile, F32),
            pltpu.VMEM(rim_tile, F32),
            pltpu.VMEM((2, NSTEP, lon_cols, levels), F32),
        ),
        in_specs=[HBM_SPEC] * 2 + vmem_specs(6),
        out_specs=tuple(vmem_specs(5)),
        scratch_shapes=[pltpu.VMEM(wide, F32)] * 3
        + [pltpu.VMEM(control.shape, F32), pltpu.SemaphoreType.DMA((2,))],
        compiler_params=params(24),
        cost_estimate=estimate(4_000_000_000, 16_000_000),
        name="forward",
    )(
        control, sigma, east, west, kappa, vertical, channel_table,
        channel_pick.reshape(1, channels),
    )

    ends = pl.pallas_call(
        ends_kernel,
        out_shape=pltpu.VMEM((2, lon_cols, 8 * channels), BF16),
        in_specs=vmem_specs(6),
        out_specs=vmem_specs(1)[0],
        scratch_shapes=[pltpu.VMEM(rim, F32)] * 3,
        compiler_params=params(12),
        cost_estimate=estimate(1_000_000_000, 2_000_000),
        name="ends",
    )(rim_state, rim_kappa, rim_sigma, north, south, vertical)

    returned, adjoint, left, right, atop, abottom = pl.pallas_call(
        functools.partial(owner_kernel, devices_all, quarter),
        out_shape=(
            pltpu.HBM((rows_half, 128), I32),
            pltpu.HBM(control.shape, F32),
            pltpu.HBM((lat_rows, NSTEP, levels), BF16),
            pltpu.HBM((lat_rows, NSTEP, levels), BF16),
            jax.ShapeDtypeStruct((NSTEP, lon_cols, levels), BF16),
            jax.ShapeDtypeStruct((NSTEP, lon_cols, levels), BF16),
        ),
        in_specs=[HBM_SPEC] * 2 + vmem_specs(4),
        out_specs=(HBM_SPEC,) * 6,
        scratch_shapes=[
            pltpu.VMEM((rows_half, 128), I32),
            pltpu.VMEM((2 * rows_half, 128), I32),
            pltpu.VMEM((columns // 4, 4 * channels), F32),
            pltpu.VMEM((columns // 4, 8 * channels), BF16),
            pltpu.VMEM((2 * channels, 2 * channels), F32),
            pltpu.VMEM((devices_all * (quarter + 1), 128), I32),
            pltpu.VMEM((rows_half, 128), I32),
            pltpu.VMEM(control.shape, F32),
            pltpu.VMEM(control.shape, F32),
            pltpu.VMEM((lat_rows, NSTEP, levels), BF16),
            pltpu.VMEM((lat_rows, NSTEP, levels), BF16),
            pltpu.VMEM((NSTEP, lon_cols, levels), BF16),
            pltpu.VMEM((NSTEP, lon_cols, levels), BF16),
            pltpu.SemaphoreType.DMA((max(8, lat_rows // 16 + 5),)),
        ],
        compiler_params=params(28),
        cost_estimate=estimate(4_000_000_000, 16_000_000),
        name="owner",
    )(received, sigma, evolved, ends, picked, r_inverse)
    returned = pl.pallas_call(
        pass_kernel,
        out_shape=pltpu.HBM(returned.shape, I32),
        in_specs=[HBM_SPEC] * 3,
        out_specs=HBM_SPEC,
        input_output_aliases={0: 0},
        cost_estimate=estimate(1_000_000, 1_000_000),
        name="pass",
    )(in_hbm(returned), in_hbm(left), in_hbm(right))
    home = lax.all_to_all(
        returned.reshape(devices_all, quarter, 128),
        ("lat", "lon"),
        split_axis=0,
        concat_axis=0,
        tiled=True,
    ).reshape(returned.shape)

    aeast, awest = exchange_sides(left, right)
    anorth, asouth = exchange_rims(
        jnp.concatenate([atop, aeast[:NSTEP], awest[:NSTEP]], axis=1),
        jnp.concatenate([abottom, aeast[-NSTEP:], awest[-NSTEP:]], axis=1),
    )
    inner, rim_scaled, rim_kappa, rim_control = pl.pallas_call(
        inner_kernel,
        out_shape=(
            pltpu.HBM(control.shape, F32),
            pltpu.VMEM(rim_tile, F32),
            pltpu.VMEM(rim_tile, F32),
            pltpu.VMEM((2, NSTEP, lon_cols, levels), F32),
        ),
        in_specs=[HBM_SPEC] * 2 + vmem_specs(6),
        out_specs=(HBM_SPEC,) + tuple(vmem_specs(3)),
        scratch_shapes=[pltpu.VMEM(wide, F32)] * 3
        + [pltpu.VMEM(control.shape, F32)] * 2
        + [pltpu.SemaphoreType.DMA((lat_rows // 8,))],
        compiler_params=params(24),
        cost_estimate=estimate(4_000_000_000, 16_000_000),
        name="inner",
    )(in_hbm(adjoint), control, aeast, awest, kappa, east, west, vertical)

    gradient = pl.pallas_call(
        rim_kernel,
        out_shape=jax.ShapeDtypeStruct(control.shape, F32),
        in_specs=vmem_specs(8) + [anywhere],
        out_specs=anywhere,
        scratch_shapes=[pltpu.VMEM(rim, F32)] * 3
        + [
            pltpu.VMEM((2, NSTEP, lon_cols, levels), F32),
            pltpu.SemaphoreType.DMA((2,)),
        ],
        input_output_aliases={8: 0},
        compiler_params=params(12),
        cost_estimate=estimate(1_000_000_000, 2_000_000),
        name="rims",
    )(
        rim_scaled, rim_kappa, rim_control, anorth, asouth, north, south, vertical, inner,
    )

    departures = pl.pallas_call(
        functools.partial(return_kernel, devices_all, quarter),
        out_shape=jax.ShapeDtypeStruct((channels, obs_slots), F32),
        in_specs=[smem] + vmem_specs(5),
        out_specs=vmem_specs(1)[0],
        scratch_shapes=[pltpu.VMEM((2 * rows_half, 256), BF16)],
        compiler_params=params(10),
        cost_estimate=estimate(500_000_000, 2_000_000),
        name="give_back",
    )(
        obs_count, home, key, innovations.T, error_scale.reshape(1, obs_slots),
        r_inverse,
    )
    return (gradient, departures.T)


def solution(mesh):
    return jax.shard_map(
        body,
        mesh=mesh,
        in_specs=(
            P("lat", "lon", None),
            P("lat", "lon"),
            P("lat", "lon", None),
            P(),
            P(),
            P(),
            P(),
            P(("lat", "lon"), None),
            P(("lat", "lon")),
            P(("lat", "lon"), None),
            P(("lat", "lon")),
            P(("lat", "lon")),
        ),
        out_specs=(P("lat", "lon", None), P(("lat", "lon"), None)),
        check_vma=False,
    )
```

```python
import functools

import jax
import jax.numpy as jnp
from jax import lax
from jax.experimental import pallas as pl
from jax.experimental.pallas import tpu as pltpu
from jax.sharding import PartitionSpec as P

NSTEP = 4
F32 = jnp.float32
BF16 = jnp.bfloat16
I32 = jnp.int32
INNOV_MAX = 6.0
INNOV_STEP = INNOV_MAX / 32767.0
WEIGHT_MAX = 4.0
WEIGHT_STEP = WEIGHT_MAX / 65535.0
CODE_FLOOR = -15.0
CODE_STEPS = 1056.0


def split_hi_lo(value):
    high = value.astype(BF16)
    low = (value - high.astype(F32)).astype(BF16)
    return high, low


def encode(value):
    size = jnp.maximum(jnp.abs(value), 2.0**CODE_FLOOR)
    level = (jnp.log2(size) - CODE_FLOOR) * CODE_STEPS + 0.5
    code = jnp.minimum(level, 32767.0).astype(I32)
    return jnp.where(value < 0.0, code + 32768, code)


def decode(code):
    level = code & 32767
    size = jnp.exp2(level.astype(F32) * (1.0 / CODE_STEPS) + CODE_FLOOR)
    size = jnp.where(level == 0, 0.0, size)
    return jnp.where(code >= 32768, -size, size)


def iota(shape, dim):
    return lax.broadcasted_iota(I32, shape, dim)


def dot_f32(left, right):
    return jnp.dot(left, right, preferred_element_type=F32)


def dot_nt(left, right):
    return lax.dot_general(left, right, (((1,), (1,)), ((), ())), preferred_element_type=F32)


def dot_tn(left, right):
    return lax.dot_general(left, right, (((0,), (0,)), ((), ())), preferred_element_type=F32)


def params(mebibytes):
    return pltpu.CompilerParams(vmem_limit_bytes=mebibytes * 1024 * 1024)


HBM_SPEC = pl.BlockSpec(memory_space=pltpu.HBM)


def in_hbm(array):
    return pltpu.with_memory_space_constraint(array, pltpu.HBM)


def start_copies(pairs, sem_ref, first=0):
    copies = []
    for index, (source, target) in enumerate(pairs):
        copy = pltpu.make_async_copy(source, target, sem_ref.at[first + index])
        copy.start()
        copies.append(copy)
    return copies


def wait_copies(copies):
    for copy in copies:
        copy.wait()


def vmem_specs(count):
    return [pl.BlockSpec(memory_space=pltpu.VMEM)] * count


def address_kernel(
    devices_all, quarter, owner_ref, cell_ref, weight_ref, innov_ref, kappa_ref,
    control_hbm, out_ref, key_ref, top_ref, bottom_ref, word_ref, ends_ref, sem_ref,
):
    grid_rows = control_hbm.shape[0]
    ends_in = start_copies(
        [
            (control_hbm.at[pl.ds(0, NSTEP)], ends_ref.at[0]),
            (control_hbm.at[pl.ds(grid_rows - NSTEP, NSTEP)], ends_ref.at[1]),
        ],
        sem_ref,
    )
    obs = owner_ref.shape[1]
    rows_half = devices_all * quarter
    rows = 2 * rows_half
    owner = owner_ref[...]
    cell = cell_ref[...]
    mine = iota((devices_all, obs), 0) == owner
    mine_f = mine.astype(F32)
    mine_b = mine_f.astype(BF16)
    block = min(256, obs)
    earlier = (iota((block, block), 0) < iota((block, block), 1)).astype(F32).astype(BF16)
    running = jnp.zeros((devices_all, 1), F32)
    parts = []
    for start in range(0, obs, block):
        piece = mine_f[:, start : start + block]
        before = dot_f32(mine_b[:, start : start + block], earlier) + running
        parts.append(jnp.sum(piece * before, axis=0, keepdims=True))
        running = running + jnp.sum(piece, axis=1, keepdims=True)
    position = jnp.concatenate(parts, axis=1).astype(I32)
    group = position // quarter
    key = (
        (group // 2) * rows + (group % 2) * rows_half + owner * quarter + position % quarter
    )
    key_ref[...] = key
    weight = jnp.minimum(jnp.floor(weight_ref[...] * (1.0 / WEIGHT_STEP) + 0.5), 65535.0)
    weight_high = jnp.floor(weight * (1.0 / 256.0))
    weight_low = weight - 256.0 * weight_high
    cell_high = (cell // 64).astype(F32)
    cell_low = (cell % 64).astype(F32)
    left = jnp.concatenate(
        [mine_f * piece for piece in (cell_high, cell_low, weight_high, weight_low)], axis=0
    ).astype(BF16)
    place = (iota((128, obs), 0) == position).astype(F32).astype(BF16)
    table = dot_nt(left, place).astype(I32)
    n = devices_all
    cells = table[:n] * 64 + table[n : 2 * n]
    weights = table[2 * n : 3 * n] * 256 + table[3 * n :]
    meta = (cells << 16) | weights

    level = jnp.floor(
        jnp.clip(innov_ref[...], -INNOV_MAX, INNOV_MAX) * (1.0 / INNOV_STEP) + 0.5
    )
    high = jnp.floor(level * (1.0 / 256.0))
    low = (level - 256.0 * high).astype(BF16)
    high = high.astype(BF16)
    bytes_of = [jnp.concatenate([high, low], axis=0), jnp.concatenate([low, high], axis=0)]
    chunk = min(256, rows_half)
    left_lane = iota((chunk, 128), 1) < 64
    for base in range(0, rows_half, chunk):
        total = []
        for half in range(2):
            row = iota((chunk, obs), 0) + (base + half * rows_half)
            found = []
            for side in range(2):
                hot = (row + side * rows == key).astype(F32).astype(BF16)
                got = dot_nt(hot, bytes_of[side])
                found.append(got * 256.0 + pltpu.roll(got, 64, 1))
            total.append(jnp.where(left_lane, found[0], found[1]).astype(I32))
        word_ref[base : base + chunk, :] = (total[0] << 16) | (total[1] & 0xFFFF)
    for device in range(devices_all):
        at = device * (quarter + 1)
        out_ref[at : at + quarter, :] = word_ref[device * quarter : (device + 1) * quarter, :]
        out_ref[at + quarter : at + quarter + 1, :] = meta[device : device + 1]
    top_ref[1] = spread_kappa(kappa_ref[:NSTEP, :]).astype(BF16)
    bottom_ref[1] = spread_kappa(kappa_ref[grid_rows - NSTEP :, :]).astype(BF16)
    wait_copies(ends_in)
    top_ref[0] = ends_ref[0].astype(BF16)
    bottom_ref[0] = ends_ref[1].astype(BF16)


LEAD = 16


def tile_of(cols):
    return slice(LEAD, LEAD + cols)


def put_sides(wide_ref, at, count, cols, east, west):
    wide_ref[at : at + count, LEAD + cols : LEAD + cols + NSTEP, :] = east.astype(F32)
    wide_ref[at : at + count, LEAD - NSTEP : LEAD, :] = west.astype(F32)


def spread_kappa(kappa, low=0, high=None):
    rows, cols = kappa.shape
    count = (cols if high is None else high) - low
    top, rest = split_hi_lo(kappa)
    pair = jnp.concatenate([top.astype(F32), rest.astype(F32)], axis=1)
    shape = (rows, count, 2 * cols)
    hot = iota(shape, 1) + low == iota(shape, 2) % cols
    spread = jnp.where(hot, pair[:, None, :], 0.0).astype(BF16)
    ones = jnp.ones((2 * cols, 128), BF16)
    return dot_f32(spread.reshape(rows * count, 2 * cols), ones).reshape(rows, count, 128)


def pack_kernel(
    control_hbm, kappa_hbm, near_ref, far_ref, left_ref, right_ref, kappa_ref, sem_ref
):
    cols = control_hbm.shape[1]
    kappa_in = start_copies([(kappa_hbm, kappa_ref)], sem_ref, 2)
    copies = start_copies(
        [
            (control_hbm.at[:, pl.ds(0, 8)], left_ref),
            (control_hbm.at[:, pl.ds(cols - 8, 8)], right_ref),
        ],
        sem_ref,
    )
    wait_copies(kappa_in)
    kappa = kappa_ref[...]
    near_ref[1] = spread_kappa(kappa, 0, 8)[:, :NSTEP].astype(BF16)
    far_ref[1] = spread_kappa(kappa, cols - 8, cols)[:, 8 - NSTEP :].astype(BF16)
    wait_copies(copies)
    near_ref[0] = left_ref[:, :NSTEP].astype(BF16)
    far_ref[0] = right_ref[:, 8 - NSTEP :].astype(BF16)


def sweep_rows(source, target, kap_ref, low, high, block=8):
    width = source.shape[1]
    here_at = slice(8, width - 8)

    def update(first, count):
        rows = [source[first + i, here_at, :] for i in range(-1, count + 1)]
        for i in range(count):
            here = rows[i + 1]
            change = (
                (rows[i] + rows[i + 2])
                + (source[first + i, 7 : width - 9, :] + source[first + i, 9 : width - 7, :])
                - 4.0 * here
            )
            target[first + i, here_at, :] = here + kap_ref[first + i, here_at, :] * change

    whole = (high - low) // block

    def step(index, carry):
        update(low + index * block, block)
        return carry

    lax.fori_loop(0, whole, step, 0)
    if low + whole * block < high:
        update(low + whole * block, high - low - whole * block)


def sweeps(first_ref, second_ref, kap_ref, rows, block=8):
    source, target = first_ref, second_ref
    for sweep in range(1, NSTEP + 1):
        sweep_rows(source, target, kap_ref, sweep, rows - sweep, block)
        source, target = target, source
    return source


def fill_picked(pick_ref, picked):
    channels, levels = picked.shape
    pick_ref[...] = jnp.zeros_like(pick_ref)
    for part in range(4):
        pick_ref[
            part * channels : (part + 1) * channels, part * levels : (part + 1) * levels
        ] = picked


def forward_mixing(vertical):
    high, low = split_hi_lo(vertical)
    pair = jnp.concatenate([high, low], axis=1)
    return jnp.concatenate([pair, pair], axis=0)


def project_rows(rows, dev, mixing):
    count, cols, levels = rows.shape
    pair = jnp.concatenate(split_hi_lo(rows.reshape(count * cols, levels)), axis=1)
    both = dot_f32(pair, mixing)
    state = both[:, :levels] + both[:, levels:]
    prof = (dev.reshape(count * cols, levels) * state).astype(BF16)
    prof = prof.reshape(count // 4, 4, cols, levels)
    return jnp.concatenate(
        [prof[:, part].reshape(count // 4 * cols, levels) for part in range(4)], axis=1
    )


def forward_kernel(
    control_hbm, sigma_hbm, east_ref, west_ref, kappa_ref, vertical_ref, table_ref, choice_ref,
    out_ref, pick_ref, rim_ref, rim_kap_ref, rim_sigma_ref, first_ref, second_ref, kap_ref,
    sigma_ref, sem_ref,
):
    rows, cols, levels = control_hbm.shape
    tile_in = start_copies(
        [(control_hbm, first_ref.at[pl.ds(0, rows), pl.ds(LEAD, cols)])], sem_ref
    )
    put_sides(first_ref, 0, rows, cols, east_ref[0], west_ref[0])
    kap_ref[:rows, tile_of(cols), :] = spread_kappa(kappa_ref[...])
    put_sides(kap_ref, 0, rows, cols, east_ref[1], west_ref[1])
    wait_copies(tile_in)
    sigma_in = start_copies([(sigma_hbm, sigma_ref)], sem_ref, 1)
    keep_rims(rim_ref, first_ref, rows)
    keep_rims(rim_kap_ref, kap_ref, rows)
    done = sweeps(first_ref, second_ref, kap_ref, rows)
    channels = choice_ref.shape[1]
    table_rows = table_ref.shape[0]
    hot = (iota((table_rows, channels), 0) == choice_ref[...]).astype(F32).astype(BF16)
    fill_picked(pick_ref, dot_tn(hot, table_ref[...]).astype(BF16))
    mixing = forward_mixing(vertical_ref[...])
    wait_copies(sigma_in)
    rim_sigma_ref[0] = sigma_ref[:NSTEP]
    rim_sigma_ref[1] = sigma_ref[rows - NSTEP :]
    count = 8
    for index in range((rows - 2 * NSTEP) // count):
        row = NSTEP + index * count
        where = pl.ds(row // 4 * cols, count // 4 * cols)
        out_ref[where, :] = project_rows(
            done[row : row + count, tile_of(cols), :], sigma_ref[row : row + count], mixing
        )


def keep_rims(rim_ref, wide_ref, rows):
    span = 2 * NSTEP
    for end, low in enumerate((0, rows - span)):
        rim_ref[end * span : (end + 1) * span] = wide_ref[low : low + span]


def pole_flags():
    at = lax.axis_index("lat")
    last = lax.axis_size("lat") - 1
    return jnp.where(at > 0, 1.0, 0.0), jnp.where(at < last, 1.0, 0.0)


def put_rims(wide_ref, rim_ref, north, south, cols):
    wide_ref[NSTEP : 5 * NSTEP] = rim_ref[...]
    for at, rim in ((0, north), (5 * NSTEP, south)):
        wide_ref[at : at + NSTEP, tile_of(cols), :] = rim[:, :cols]
        put_sides(
            wide_ref, at, NSTEP, cols, rim[:, cols : cols + NSTEP], rim[:, cols + NSTEP :]
        )


def ends_kernel(
    rim_ref, rim_kap_ref, sigma_ref, north_ref, south_ref, vertical_ref, out_ref,
    first_ref, second_ref, kap_ref,
):
    cols = sigma_ref.shape[2]
    north_on, south_on = pole_flags()
    put_rims(
        kap_ref, rim_kap_ref, north_ref[1].astype(F32) * north_on,
        south_ref[1].astype(F32) * south_on, cols,
    )
    put_rims(
        first_ref, rim_ref, north_ref[0].astype(F32) * north_on,
        south_ref[0].astype(F32) * south_on, cols,
    )
    done = sweeps(first_ref, second_ref, kap_ref, 6 * NSTEP)
    mixing = forward_mixing(vertical_ref[...])
    for end in range(2):
        at = slice((1 + 3 * end) * NSTEP, (2 + 3 * end) * NSTEP)
        out_ref[end] = project_rows(done[at, tile_of(cols), :], sigma_ref[end], mixing)


def owner_kernel(
    devices_all, quarter, recv_hbm, sigma_hbm, inner_ref, ends_ref, pick_ref, rinv_ref,
    ret_hbm, adj_hbm, left_hbm, right_hbm, top_hbm, bottom_hbm,
    word_ref, dep_ref, acc_ref, table_ref, pair_ref,
    recv_ref, ret_ref, sigma_ref, adj_ref, left_ref, right_ref, top_ref, bottom_ref,
    sem_ref,
):
    lat_rows, cols, levels = sigma_hbm.shape
    cells_part = inner_ref.shape[0]
    others_in = start_copies([(recv_hbm, recv_ref)], sem_ref)
    sigma_in = start_copies([(sigma_hbm, sigma_ref)], sem_ref, 1)
    table_ref[:cols, :] = ends_ref[0]
    table_ref[cols : cells_part - cols, :] = inner_ref[cols : cells_part - cols, :]
    table_ref[cells_part - cols :, :] = ends_ref[1]
    wait_copies(others_in)
    rows_half = devices_all * quarter
    rows = 2 * rows_half
    metas = []
    for device in range(devices_all):
        at = device * (quarter + 1)
        word_ref[device * quarter : (device + 1) * quarter, :] = recv_ref[at : at + quarter, :]
        metas.append(recv_ref[at + quarter : at + quarter + 1, :])
    meta = jnp.concatenate(metas, axis=0)
    cells, weights = meta >> 16, meta & 0xFFFF
    facts = jnp.concatenate(
        [
            piece.astype(F32).astype(BF16)
            for piece in (cells >> 6, cells & 63, weights >> 8, weights & 255)
        ],
        axis=1,
    )
    channels = rinv_ref.shape[0]
    pair_ref[...] = jnp.zeros_like(pair_ref)
    pair_ref[:channels, :channels] = rinv_ref[...]
    pair_ref[channels:, channels:] = rinv_ref[...]
    high, low = split_hi_lo(pair_ref[...])
    zero = jnp.zeros_like(high)
    mixing = jnp.concatenate(
        [jnp.concatenate([high, low], axis=1), jnp.concatenate([high, zero], axis=1)], axis=0
    )
    pick_pair = jnp.transpose(
        pick_ref[: 2 * channels, : 2 * levels].astype(F32)
    ).astype(BF16)
    all_hots, all_wides = [], []
    chunk = min(512, rows_half)
    left_lane = iota((chunk, 128), 1) < 64
    lane_half = iota((chunk, 128), 1) // 64
    zero_hot = jnp.zeros((chunk, 128), BF16)
    per_half = rows_half // chunk
    for step in range(rows // chunk):
        half = step // per_half
        base = (step % per_half) * chunk
        row = iota((chunk, devices_all), 0) + base
        spread = (row // quarter == iota((chunk, devices_all), 1)).astype(F32).astype(BF16)
        found = dot_f32(spread, facts)
        lat_lane = found[:, :128]
        lon_lane = found[:, 128:256]
        weight_lane = (found[:, 256:384] * 256.0 + found[:, 384:]) * WEIGHT_STEP
        lane = iota((chunk, 128), 1)
        r = (iota((chunk, 128), 0) + base) % quarter
        hots, parts, weight, values = [], [], [], []
        for side in range(2):
            take = lane == (2 * side + half) * quarter + r
            lat = jnp.sum(jnp.where(take, lat_lane, 0.0), axis=1, keepdims=True).astype(I32)
            lon = jnp.sum(jnp.where(take, lon_lane, 0.0), axis=1, keepdims=True).astype(I32)
            weight.append(jnp.sum(jnp.where(take, weight_lane, 0.0), axis=1, keepdims=True))
            part = lat & 3
            lon_hot = (lane % cols == lon).astype(F32).astype(BF16)
            band = jnp.broadcast_to((lat >> 2).astype(F32), (chunk, 128)).astype(BF16)
            hot = jnp.concatenate(
                [
                    jnp.where(
                        band == (lane // cols + first).astype(F32).astype(BF16), lon_hot, zero_hot
                    )
                    for first in range(0, lat_rows // 4, 128 // cols)
                ],
                axis=1,
            )
            got = dot_f32(hot, table_ref[...])
            low_parts = jnp.where(part == 0, got[:, :levels], got[:, levels : 2 * levels])
            high_parts = jnp.where(
                part == 2, got[:, 2 * levels : 3 * levels], got[:, 3 * levels :]
            )
            values.append(jnp.where(part < 2, low_parts, high_parts).astype(BF16))
            hots.append(hot)
            parts.append(part)
        evolved = dot_f32(jnp.concatenate(values, axis=1), pick_pair)
        words = word_ref[base : base + chunk, :]
        words = (words if half == 0 else words << 16) >> 16
        gap = evolved - words.astype(F32) * INNOV_STEP
        both = dot_f32(jnp.concatenate(split_hi_lo(gap), axis=1), mixing)
        dep = (both[:, :128] + both[:, 128:]) * jnp.where(left_lane, weight[0], weight[1])
        dep_ref[step * chunk : (step + 1) * chunk, :] = encode(evolved)
        rounded = dep.astype(BF16).astype(F32)
        swapped = pltpu.roll(rounded, 64, 1)
        for side in range(2):
            twice = (
                jnp.where(left_lane, rounded, swapped)
                if side == 0
                else jnp.where(left_lane, swapped, rounded)
            )
            wide = jnp.concatenate(
                [
                    jnp.where(parts[side] == lane_half, twice, 0.0).astype(BF16),
                    jnp.where(parts[side] == lane_half + 2, twice, 0.0).astype(BF16),
                ],
                axis=1,
            )
            all_hots.append(hots[side])
            all_wides.append(wide)
    acc_ref[...] = dot_tn(
        jnp.concatenate(all_hots, axis=0), jnp.concatenate(all_wides, axis=0)
    )
    ret_ref[...] = (dep_ref[:rows_half, :] << 16) | dep_ref[rows_half:, :]
    copies = start_copies([(ret_ref, ret_hbm)], sem_ref)
    wait_copies(sigma_in)
    groups = 4
    count = groups * 4
    for step in range(lat_rows // count):
        high, low = split_hi_lo(acc_ref[step * groups * cols : (step + 1) * groups * cols, :])
        both = dot_f32(high, pick_ref[...]) + dot_f32(low, pick_ref[...])
        for group in range(groups):
            for part in range(4):
                at = step * count + group * 4 + part
                value = sigma_ref[at] * both[
                    group * cols : (group + 1) * cols, part * levels : (part + 1) * levels
                ]
                adj_ref[at] = value
                left_ref[at] = value[:NSTEP].astype(BF16)
                right_ref[at] = value[cols - NSTEP :].astype(BF16)
                if at < NSTEP:
                    top_ref[at] = value.astype(BF16)
                if at >= lat_rows - NSTEP:
                    bottom_ref[at - (lat_rows - NSTEP)] = value.astype(BF16)
        where = pl.ds(step * count, count)
        copies += start_copies([(adj_ref.at[where], adj_hbm.at[where])], sem_ref, step + 1)
    copies += start_copies(
        [
            (left_ref, left_hbm),
            (right_ref, right_hbm),
            (top_ref, top_hbm),
            (bottom_ref, bottom_hbm),
        ],
        sem_ref,
        lat_rows // count + 1,
    )
    wait_copies(copies)


def backward_mixing(vertical):
    high, low = split_hi_lo(vertical)
    return jnp.concatenate(
        [jnp.concatenate([high, high], axis=1), jnp.concatenate([low, low], axis=1)], axis=0
    )


def finish_rows(scaled, kap, mixing):
    count, cols, levels = scaled.shape
    adjoint = (scaled / kap).reshape(count * cols, levels)
    both = dot_nt(jnp.concatenate(split_hi_lo(adjoint), axis=1), mixing)
    return (both[:, :levels] + both[:, levels:]).reshape(count, cols, levels)


def inner_kernel(
    adj_hbm, control_hbm, east_ref, west_ref, kappa_ref, keast_ref, kwest_ref, vertical_ref,
    out_hbm, rim_ref, rim_kap_ref, rim_control_ref, first_ref, second_ref, kap_ref, out_ref,
    control_ref, sem_ref,
):
    rows, cols, levels = control_hbm.shape
    tile_in = start_copies([(adj_hbm, first_ref.at[pl.ds(0, rows), pl.ds(LEAD, cols)])], sem_ref)
    kap_ref[:rows, tile_of(cols), :] = spread_kappa(kappa_ref[...])
    put_sides(kap_ref, 0, rows, cols, keast_ref[1], kwest_ref[1])
    put_sides(first_ref, 0, rows, cols, east_ref[...], west_ref[...])
    wait_copies(tile_in)
    control_in = start_copies([(control_hbm, control_ref)], sem_ref, 1)
    first_ref[:rows] = first_ref[:rows] * kap_ref[:rows]
    keep_rims(rim_ref, first_ref, rows)
    keep_rims(rim_kap_ref, kap_ref, rows)
    done = sweeps(first_ref, second_ref, kap_ref, rows)
    mixing = backward_mixing(vertical_ref[...])
    wait_copies(control_in)
    rim_control_ref[0] = control_ref[:NSTEP]
    rim_control_ref[1] = control_ref[rows - NSTEP :]
    count = 8
    copies = []
    for index in range((rows - 2 * NSTEP) // count):
        row = NSTEP + index * count
        at = pl.ds(row, count)
        out_ref[at] = control_ref[at] + finish_rows(
            done[row : row + count, tile_of(cols), :], kap_ref[row : row + count, tile_of(cols), :], mixing
        )
        copies += start_copies([(out_ref.at[at], out_hbm.at[at])], sem_ref, index)
    wait_copies(copies)


def rim_kernel(
    rim_ref, rim_kap_ref, control_ref, north_ref, south_ref, knorth_ref, ksouth_ref, vertical_ref,
    inner_ref, out_ref, first_ref, second_ref, kap_ref, edge_ref, sem_ref,
):
    del inner_ref
    lat_rows = out_ref.shape[0]
    cols = out_ref.shape[1]
    north_on, south_on = pole_flags()
    put_rims(
        kap_ref, rim_kap_ref, knorth_ref[1].astype(F32) * north_on,
        ksouth_ref[1].astype(F32) * south_on, cols,
    )
    put_rims(
        first_ref, rim_ref, north_ref[...].astype(F32), south_ref[...].astype(F32), cols
    )
    for at in (0, 5 * NSTEP):
        first_ref[at : at + NSTEP] = first_ref[at : at + NSTEP] * kap_ref[at : at + NSTEP]
    done = sweeps(first_ref, second_ref, kap_ref, 6 * NSTEP)
    mixing = backward_mixing(vertical_ref[...])
    copies = []
    for end in range(2):
        at = pl.ds((1 + 3 * end) * NSTEP, NSTEP)
        back = finish_rows(done[at, tile_of(cols), :], kap_ref[at, tile_of(cols), :], mixing)
        edge_ref[end] = control_ref[end] + back
        copies += start_copies(
            [(edge_ref.at[end], out_ref.at[pl.ds(end * (lat_rows - NSTEP), NSTEP)])], sem_ref, end
        )
    wait_copies(copies)


def pass_kernel(array_hbm, first_hbm, second_hbm, out_hbm):
    del array_hbm, first_hbm, second_hbm, out_hbm


def return_kernel(
    devices_all, quarter, recv_ref, key_ref, innov_ref, weight_ref, rinv_ref, out_ref,
    pair_ref,
):
    rows_half = devices_all * quarter
    rows = 2 * rows_half
    channels, obs = out_ref.shape
    words = recv_ref[...]
    for half in range(2):
        code = (words >> 16) & 0xFFFF if half == 0 else words & 0xFFFF
        high, low = split_hi_lo(decode(code))
        pair_ref[half * rows_half : (half + 1) * rows_half, :128] = high
        pair_ref[half * rows_half : (half + 1) * rows_half, 128:] = low
    weight = weight_ref[...]
    chunk = min(512, obs)
    for start in range(0, obs, chunk):
        key = key_ref[:, start : start + chunk]
        side = key >= rows
        row = jnp.where(side, key - rows, key)
        hot = (iota((rows, chunk), 0) == row).astype(F32).astype(BF16)
        both = dot_tn(pair_ref[...], hot)
        both = both[:128] + both[128:]
        evolved = jnp.where(side, both[channels:], both[:channels])
        gap = evolved - innov_ref[:, start : start + chunk]
        mixed = lax.dot_general(
            rinv_ref[...], gap, (((0,), (0,)), ((), ())), precision=lax.Precision.HIGHEST,
            preferred_element_type=F32,
        )
        out_ref[:, start : start + chunk] = mixed * weight[:, start : start + chunk]


def shifts(axis):
    count = lax.axis_size(axis)
    forward = [(i, (i + 1) % count) for i in range(count)]
    return forward, [(target, source) for source, target in forward]


def exchange_sides(left, right):
    forward, backward = shifts("lon")
    return lax.ppermute(left, "lon", backward), lax.ppermute(right, "lon", forward)


def exchange_rims(top, bottom):
    forward, backward = shifts("lat")
    return lax.ppermute(bottom, "lat", forward), lax.ppermute(top, "lat", backward)


def estimate(flops, bytes_accessed):
    return pl.CostEstimate(flops=flops, bytes_accessed=bytes_accessed, transcendentals=0)


def body(
    control,
    kappa,
    sigma,
    vertical,
    channel_table,
    channel_pick,
    r_inverse,
    innovations,
    error_scale,
    obs_owner,
    obs_cell,
    obs_count,
):
    lat_rows, lon_cols, levels = control.shape
    obs_slots = obs_cell.shape[0]
    channels = innovations.shape[1]
    devices_all = lax.axis_size("lat") * lax.axis_size("lon")
    capacity = max(4, 2 * obs_slots // devices_all)
    quarter = capacity // 4
    rows_half = devices_all * quarter
    columns = lat_rows * lon_cols
    wide = (lat_rows + 1, lon_cols + 2 * LEAD, levels)
    rim_tile = (4 * NSTEP, lon_cols + 2 * LEAD, levels)
    rim = (6 * NSTEP, lon_cols + 2 * LEAD, levels)
    anywhere = pl.BlockSpec(memory_space=pl.ANY)

    control, sigma = in_hbm(control), in_hbm(sigma)
    near, far = pl.pallas_call(
        pack_kernel,
        out_shape=(jax.ShapeDtypeStruct((2, lat_rows, NSTEP, levels), BF16),) * 2,
        in_specs=[HBM_SPEC] * 2,
        out_specs=tuple(vmem_specs(2)),
        scratch_shapes=[
            pltpu.VMEM((lat_rows, 8, levels), F32),
            pltpu.VMEM((lat_rows, 8, levels), F32),
            pltpu.VMEM(kappa.shape, F32),
            pltpu.SemaphoreType.DMA((3,)),
        ],
        compiler_params=params(6),
        name="pack",
    )(control, in_hbm(kappa))
    valid = jnp.arange(obs_slots, dtype=I32) < obs_count[0]
    weight = jnp.where(valid, 1.0 / (error_scale * error_scale), F32(0.0))
    weight = weight.reshape(1, obs_slots)
    near, far, obs_cell = lax.optimization_barrier((near, far, obs_cell))
    east, west = exchange_sides(near, far)

    payload, key, top, bottom = pl.pallas_call(
        functools.partial(address_kernel, devices_all, quarter),
        out_shape=(
            jax.ShapeDtypeStruct((devices_all * (quarter + 1), 128), I32),
            jax.ShapeDtypeStruct((1, obs_slots), I32),
            jax.ShapeDtypeStruct((2, NSTEP, lon_cols, levels), BF16),
            jax.ShapeDtypeStruct((2, NSTEP, lon_cols, levels), BF16),
        ),
        in_specs=vmem_specs(5) + [HBM_SPEC],
        out_specs=tuple(vmem_specs(4)),
        scratch_shapes=[
            pltpu.VMEM((rows_half, 128), I32),
            pltpu.VMEM((2, NSTEP, lon_cols, levels), F32),
            pltpu.SemaphoreType.DMA((2,)),
        ],
        compiler_params=params(10),
        cost_estimate=estimate(2_000_000_000, 8_000_000),
        name="address",
    )(
        obs_owner.reshape(1, obs_slots),
        obs_cell.reshape(1, obs_slots),
        weight,
        innovations.T,
        kappa,
        control,
    )
    received = lax.all_to_all(
        payload.reshape(devices_all, 1, (quarter + 1) * 128),
        ("lat", "lon"),
        split_axis=0,
        concat_axis=0,
        tiled=True,
    ).reshape(payload.shape)

    def with_sides(tile, low, high):
        return jnp.concatenate([tile, east[:, low:high], west[:, low:high]], axis=2)

    north, south = exchange_rims(
        with_sides(top, 0, NSTEP), with_sides(bottom, lat_rows - NSTEP, lat_rows)
    )

    evolved, picked, rim_state, rim_kappa, rim_sigma = pl.pallas_call(
        forward_kernel,
        out_shape=(
            pltpu.VMEM((columns // 4, 8 * channels), BF16),
            pltpu.VMEM((4 * channels, 4 * levels), BF16),
            pltpu.VMEM(rim_tile, F32),
            pltpu.VMEM(rim_tile, F32),
            pltpu.VMEM((2, NSTEP, lon_cols, levels), F32),
        ),
        in_specs=[HBM_SPEC] * 2 + vmem_specs(6),
        out_specs=tuple(vmem_specs(5)),
        scratch_shapes=[pltpu.VMEM(wide, F32)] * 3
        + [pltpu.VMEM(control.shape, F32), pltpu.SemaphoreType.DMA((2,))],
        compiler_params=params(24),
        cost_estimate=estimate(4_000_000_000, 16_000_000),
        name="forward",
    )(
        control, sigma, east, west, kappa, vertical, channel_table,
        channel_pick.reshape(1, channels),
    )

    ends = pl.pallas_call(
        ends_kernel,
        out_shape=pltpu.VMEM((2, lon_cols, 8 * channels), BF16),
        in_specs=vmem_specs(6),
        out_specs=vmem_specs(1)[0],
        scratch_shapes=[pltpu.VMEM(rim, F32)] * 3,
        compiler_params=params(12),
        cost_estimate=estimate(1_000_000_000, 2_000_000),
        name="ends",
    )(rim_state, rim_kappa, rim_sigma, north, south, vertical)

    returned, adjoint, left, right, atop, abottom = pl.pallas_call(
        functools.partial(owner_kernel, devices_all, quarter),
        out_shape=(
            pltpu.HBM((rows_half, 128), I32),
            pltpu.HBM(control.shape, F32),
            pltpu.HBM((lat_rows, NSTEP, levels), BF16),
            pltpu.HBM((lat_rows, NSTEP, levels), BF16),
            jax.ShapeDtypeStruct((NSTEP, lon_cols, levels), BF16),
            jax.ShapeDtypeStruct((NSTEP, lon_cols, levels), BF16),
        ),
        in_specs=[HBM_SPEC] * 2 + vmem_specs(4),
        out_specs=(HBM_SPEC,) * 6,
        scratch_shapes=[
            pltpu.VMEM((rows_half, 128), I32),
            pltpu.VMEM((2 * rows_half, 128), I32),
            pltpu.VMEM((columns // 4, 4 * channels), F32),
            pltpu.VMEM((columns // 4, 8 * channels), BF16),
            pltpu.VMEM((2 * channels, 2 * channels), F32),
            pltpu.VMEM((devices_all * (quarter + 1), 128), I32),
            pltpu.VMEM((rows_half, 128), I32),
            pltpu.VMEM(control.shape, F32),
            pltpu.VMEM(control.shape, F32),
            pltpu.VMEM((lat_rows, NSTEP, levels), BF16),
            pltpu.VMEM((lat_rows, NSTEP, levels), BF16),
            pltpu.VMEM((NSTEP, lon_cols, levels), BF16),
            pltpu.VMEM((NSTEP, lon_cols, levels), BF16),
            pltpu.SemaphoreType.DMA((max(8, lat_rows // 16 + 5),)),
        ],
        compiler_params=params(28),
        cost_estimate=estimate(4_000_000_000, 16_000_000),
        name="owner",
    )(received, sigma, evolved, ends, picked, r_inverse)
    returned = pl.pallas_call(
        pass_kernel,
        out_shape=pltpu.HBM(returned.shape, I32),
        in_specs=[HBM_SPEC] * 3,
        out_specs=HBM_SPEC,
        input_output_aliases={0: 0},
        cost_estimate=estimate(1_000_000, 1_000_000),
        name="pass",
    )(in_hbm(returned), in_hbm(left), in_hbm(right))
    home = lax.all_to_all(
        returned.reshape(devices_all, quarter, 128),
        ("lat", "lon"),
        split_axis=0,
        concat_axis=0,
        tiled=True,
    ).reshape(returned.shape)

    aeast, awest = exchange_sides(left, right)
    anorth, asouth = exchange_rims(
        jnp.concatenate([atop, aeast[:NSTEP], awest[:NSTEP]], axis=1),
        jnp.concatenate([abottom, aeast[-NSTEP:], awest[-NSTEP:]], axis=1),
    )
    inner, rim_scaled, rim_kappa, rim_control = pl.pallas_call(
        inner_kernel,
        out_shape=(
            pltpu.HBM(control.shape, F32),
            pltpu.VMEM(rim_tile, F32),
            pltpu.VMEM(rim_tile, F32),
            pltpu.VMEM((2, NSTEP, lon_cols, levels), F32),
        ),
        in_specs=[HBM_SPEC] * 2 + vmem_specs(6),
        out_specs=(HBM_SPEC,) + tuple(vmem_specs(3)),
        scratch_shapes=[pltpu.VMEM(wide, F32)] * 3
        + [pltpu.VMEM(control.shape, F32)] * 2
        + [pltpu.SemaphoreType.DMA((lat_rows // 8,))],
        compiler_params=params(24),
        cost_estimate=estimate(4_000_000_000, 16_000_000),
        name="inner",
    )(in_hbm(adjoint), control, aeast, awest, kappa, east, west, vertical)

    gradient = pl.pallas_call(
        rim_kernel,
        out_shape=jax.ShapeDtypeStruct(control.shape, F32),
        in_specs=vmem_specs(8) + [anywhere],
        out_specs=anywhere,
        scratch_shapes=[pltpu.VMEM(rim, F32)] * 3
        + [
            pltpu.VMEM((2, NSTEP, lon_cols, levels), F32),
            pltpu.SemaphoreType.DMA((2,)),
        ],
        input_output_aliases={8: 0},
        compiler_params=params(12),
        cost_estimate=estimate(1_000_000_000, 2_000_000),
        name="rims",
    )(
        rim_scaled, rim_kappa, rim_control, anorth, asouth, north, south, vertical, inner,
    )

    departures = pl.pallas_call(
        functools.partial(return_kernel, devices_all, quarter),
        out_shape=jax.ShapeDtypeStruct((channels, obs_slots), F32),
        in_specs=vmem_specs(5),
        out_specs=vmem_specs(1)[0],
        scratch_shapes=[pltpu.VMEM((2 * rows_half, 256), BF16)],
        compiler_params=params(10),
        cost_estimate=estimate(500_000_000, 2_000_000),
        name="give_back",
    )(
        home, key, innovations.T, weight,
        r_inverse,
    )
    return (gradient, departures.T)


def solution(mesh):
    return jax.shard_map(
        body,
        mesh=mesh,
        in_specs=(
            P("lat", "lon", None),
            P("lat", "lon"),
            P("lat", "lon", None),
            P(),
            P(),
            P(),
            P(),
            P(("lat", "lon"), None),
            P(("lat", "lon")),
            P(("lat", "lon"), None),
            P(("lat", "lon")),
            P(("lat", "lon")),
        ),
        out_specs=(P("lat", "lon", None), P(("lat", "lon"), None)),
        check_vma=False,
    )
```

```python
import functools

import jax
import jax.numpy as jnp
from jax import lax
from jax.experimental import pallas as pl
from jax.experimental.pallas import tpu as pltpu
from jax.sharding import PartitionSpec as P

NSTEP = 4
F32 = jnp.float32
BF16 = jnp.bfloat16
I32 = jnp.int32
INNOV_MAX = 6.0
INNOV_STEP = INNOV_MAX / 32767.0
WEIGHT_MAX = 4.0
WEIGHT_STEP = WEIGHT_MAX / 65535.0
CODE_FLOOR = -15.0
CODE_STEPS = 1056.0


def split_hi_lo(value):
    high = value.astype(BF16)
    low = (value - high.astype(F32)).astype(BF16)
    return high, low


def encode(value):
    size = jnp.maximum(jnp.abs(value), 2.0**CODE_FLOOR)
    level = (jnp.log2(size) - CODE_FLOOR) * CODE_STEPS + 0.5
    code = jnp.minimum(level, 32767.0).astype(I32)
    return jnp.where(value < 0.0, code + 32768, code)


def decode(code):
    level = code & 32767
    size = jnp.exp2(level.astype(F32) * (1.0 / CODE_STEPS) + CODE_FLOOR)
    size = jnp.where(level == 0, 0.0, size)
    return jnp.where(code >= 32768, -size, size)


def iota(shape, dim):
    return lax.broadcasted_iota(I32, shape, dim)


def dot_f32(left, right):
    return jnp.dot(left, right, preferred_element_type=F32)


def dot_nt(left, right):
    return lax.dot_general(left, right, (((1,), (1,)), ((), ())), preferred_element_type=F32)


def dot_tn(left, right):
    return lax.dot_general(left, right, (((0,), (0,)), ((), ())), preferred_element_type=F32)


def params(mebibytes):
    return pltpu.CompilerParams(vmem_limit_bytes=mebibytes * 1024 * 1024)


HBM_SPEC = pl.BlockSpec(memory_space=pltpu.HBM)


def in_hbm(array):
    return pltpu.with_memory_space_constraint(array, pltpu.HBM)


def start_copies(pairs, sem_ref, first=0):
    copies = []
    for index, (source, target) in enumerate(pairs):
        copy = pltpu.make_async_copy(source, target, sem_ref.at[first + index])
        copy.start()
        copies.append(copy)
    return copies


def wait_copies(copies):
    for copy in copies:
        copy.wait()


def vmem_specs(count):
    return [pl.BlockSpec(memory_space=pltpu.VMEM)] * count


def address_kernel(
    devices_all, quarter, owner_ref, cell_ref, weight_ref, innov_ref, kappa_ref,
    control_hbm, out_ref, key_ref, top_ref, bottom_ref, word_ref, ends_ref, sem_ref,
):
    grid_rows = control_hbm.shape[0]
    ends_in = start_copies(
        [
            (control_hbm.at[pl.ds(0, NSTEP)], ends_ref.at[0]),
            (control_hbm.at[pl.ds(grid_rows - NSTEP, NSTEP)], ends_ref.at[1]),
        ],
        sem_ref,
    )
    obs = owner_ref.shape[1]
    rows_half = devices_all * quarter
    rows = 2 * rows_half
    owner = owner_ref[...]
    cell = cell_ref[...]
    mine = iota((devices_all, obs), 0) == owner
    mine_f = mine.astype(F32)
    mine_b = mine_f.astype(BF16)
    block = min(256, obs)
    earlier = (iota((block, block), 0) < iota((block, block), 1)).astype(F32).astype(BF16)
    running = jnp.zeros((devices_all, 1), F32)
    parts = []
    for start in range(0, obs, block):
        piece = mine_f[:, start : start + block]
        before = dot_f32(mine_b[:, start : start + block], earlier) + running
        parts.append(jnp.sum(piece * before, axis=0, keepdims=True))
        running = running + jnp.sum(piece, axis=1, keepdims=True)
    position = jnp.concatenate(parts, axis=1).astype(I32)
    group = position // quarter
    key = (
        (group // 2) * rows + (group % 2) * rows_half + owner * quarter + position % quarter
    )
    key_ref[...] = key
    weight = jnp.minimum(jnp.floor(weight_ref[...] * (1.0 / WEIGHT_STEP) + 0.5), 65535.0)
    weight_high = jnp.floor(weight * (1.0 / 256.0))
    weight_low = weight - 256.0 * weight_high
    cell_high = (cell // 64).astype(F32)
    cell_low = (cell % 64).astype(F32)
    left = jnp.concatenate(
        [mine_f * piece for piece in (cell_high, cell_low, weight_high, weight_low)], axis=0
    ).astype(BF16)
    place = (iota((128, obs), 0) == position).astype(F32).astype(BF16)
    table = dot_nt(left, place).astype(I32)
    n = devices_all
    cells = table[:n] * 64 + table[n : 2 * n]
    weights = table[2 * n : 3 * n] * 256 + table[3 * n :]
    meta = (cells << 16) | weights

    level = jnp.floor(
        jnp.clip(innov_ref[...], -INNOV_MAX, INNOV_MAX) * (1.0 / INNOV_STEP) + 0.5
    )
    high = jnp.floor(level * (1.0 / 256.0))
    low = (level - 256.0 * high).astype(BF16)
    high = high.astype(BF16)
    bytes_of = [jnp.concatenate([high, low], axis=0), jnp.concatenate([low, high], axis=0)]
    chunk = rows_half
    left_lane = iota((chunk, 128), 1) < 64
    for base in range(0, rows_half, chunk):
        total = []
        for half in range(2):
            row = iota((chunk, obs), 0) + (base + half * rows_half)
            found = []
            for side in range(2):
                hot = (row + side * rows == key).astype(F32).astype(BF16)
                got = dot_nt(hot, bytes_of[side])
                found.append(got * 256.0 + pltpu.roll(got, 64, 1))
            total.append(jnp.where(left_lane, found[0], found[1]).astype(I32))
        word_ref[base : base + chunk, :] = (total[0] << 16) | (total[1] & 0xFFFF)
    for device in range(devices_all):
        at = device * (quarter + 1)
        out_ref[at : at + quarter, :] = word_ref[device * quarter : (device + 1) * quarter, :]
        out_ref[at + quarter : at + quarter + 1, :] = meta[device : device + 1]
    top_ref[1] = spread_kappa(kappa_ref[:NSTEP, :]).astype(BF16)
    bottom_ref[1] = spread_kappa(kappa_ref[grid_rows - NSTEP :, :]).astype(BF16)
    wait_copies(ends_in)
    top_ref[0] = ends_ref[0].astype(BF16)
    bottom_ref[0] = ends_ref[1].astype(BF16)


LEAD = 16


def tile_of(cols):
    return slice(LEAD, LEAD + cols)


def put_sides(wide_ref, at, count, cols, east, west):
    wide_ref[at : at + count, LEAD + cols : LEAD + cols + NSTEP, :] = east.astype(F32)
    wide_ref[at : at + count, LEAD - NSTEP : LEAD, :] = west.astype(F32)


def spread_kappa(kappa, low=0, high=None):
    rows, cols = kappa.shape
    count = (cols if high is None else high) - low
    top, rest = split_hi_lo(kappa)
    pair = jnp.concatenate([top.astype(F32), rest.astype(F32)], axis=1)
    shape = (rows, count, 2 * cols)
    hot = iota(shape, 1) + low == iota(shape, 2) % cols
    spread = jnp.where(hot, pair[:, None, :], 0.0).astype(BF16)
    ones = jnp.ones((2 * cols, 128), BF16)
    return dot_f32(spread.reshape(rows * count, 2 * cols), ones).reshape(rows, count, 128)


def pack_kernel(
    control_hbm, kappa_hbm, near_ref, far_ref, left_ref, right_ref, kappa_ref, sem_ref
):
    cols = control_hbm.shape[1]
    kappa_in = start_copies([(kappa_hbm, kappa_ref)], sem_ref, 2)
    copies = start_copies(
        [
            (control_hbm.at[:, pl.ds(0, 8)], left_ref),
            (control_hbm.at[:, pl.ds(cols - 8, 8)], right_ref),
        ],
        sem_ref,
    )
    wait_copies(kappa_in)
    kappa = kappa_ref[...]
    near_ref[1] = spread_kappa(kappa, 0, 8)[:, :NSTEP].astype(BF16)
    far_ref[1] = spread_kappa(kappa, cols - 8, cols)[:, 8 - NSTEP :].astype(BF16)
    wait_copies(copies)
    near_ref[0] = left_ref[:, :NSTEP].astype(BF16)
    far_ref[0] = right_ref[:, 8 - NSTEP :].astype(BF16)


def sweep_rows(source, target, kap_ref, low, high, block=16):
    width = source.shape[1]
    here_at = slice(8, width - 8)

    def update(first, count):
        rows = [source[first + i, here_at, :] for i in range(-1, count + 1)]
        for i in range(count):
            here = rows[i + 1]
            change = (
                (rows[i] + rows[i + 2])
                + (source[first + i, 7 : width - 9, :] + source[first + i, 9 : width - 7, :])
                - 4.0 * here
            )
            target[first + i, here_at, :] = here + kap_ref[first + i, here_at, :] * change

    whole = (high - low) // block

    def step(index, carry):
        update(low + index * block, block)
        return carry

    lax.fori_loop(0, whole, step, 0)
    if low + whole * block < high:
        update(low + whole * block, high - low - whole * block)


def sweeps(first_ref, second_ref, kap_ref, rows, block=16):
    source, target = first_ref, second_ref
    for sweep in range(1, NSTEP + 1):
        sweep_rows(source, target, kap_ref, sweep, rows - sweep, block)
        source, target = target, source
    return source


def fill_picked(pick_ref, picked):
    channels, levels = picked.shape
    pick_ref[...] = jnp.zeros_like(pick_ref)
    for part in range(4):
        pick_ref[
            part * channels : (part + 1) * channels, part * levels : (part + 1) * levels
        ] = picked


def forward_mixing(vertical):
    high, low = split_hi_lo(vertical)
    pair = jnp.concatenate([high, low], axis=1)
    return jnp.concatenate([pair, pair], axis=0)


def project_rows(rows, dev, mixing):
    count, cols, levels = rows.shape
    pair = jnp.concatenate(split_hi_lo(rows.reshape(count * cols, levels)), axis=1)
    both = dot_f32(pair, mixing)
    state = both[:, :levels] + both[:, levels:]
    prof = (dev.reshape(count * cols, levels) * state).astype(BF16)
    prof = prof.reshape(count // 4, 4, cols, levels)
    return jnp.concatenate(
        [prof[:, part].reshape(count // 4 * cols, levels) for part in range(4)], axis=1
    )


def forward_kernel(
    control_hbm, sigma_hbm, east_ref, west_ref, kappa_ref, vertical_ref, table_ref, choice_ref,
    out_ref, pick_ref, rim_ref, rim_kap_ref, rim_sigma_ref, first_ref, second_ref, kap_ref,
    sigma_ref, sem_ref,
):
    rows, cols, levels = control_hbm.shape
    tile_in = start_copies(
        [(control_hbm, first_ref.at[pl.ds(0, rows), pl.ds(LEAD, cols)])], sem_ref
    )
    put_sides(first_ref, 0, rows, cols, east_ref[0], west_ref[0])
    kap_ref[:rows, tile_of(cols), :] = spread_kappa(kappa_ref[...])
    put_sides(kap_ref, 0, rows, cols, east_ref[1], west_ref[1])
    wait_copies(tile_in)
    sigma_in = start_copies([(sigma_hbm, sigma_ref)], sem_ref, 1)
    keep_rims(rim_ref, first_ref, rows)
    keep_rims(rim_kap_ref, kap_ref, rows)
    done = sweeps(first_ref, second_ref, kap_ref, rows)
    channels = choice_ref.shape[1]
    table_rows = table_ref.shape[0]
    hot = (iota((table_rows, channels), 0) == choice_ref[...]).astype(F32).astype(BF16)
    fill_picked(pick_ref, dot_tn(hot, table_ref[...]).astype(BF16))
    mixing = forward_mixing(vertical_ref[...])
    wait_copies(sigma_in)
    rim_sigma_ref[0] = sigma_ref[:NSTEP]
    rim_sigma_ref[1] = sigma_ref[rows - NSTEP :]
    count = 8
    for index in range((rows - 2 * NSTEP) // count):
        row = NSTEP + index * count
        where = pl.ds(row // 4 * cols, count // 4 * cols)
        out_ref[where, :] = project_rows(
            done[row : row + count, tile_of(cols), :], sigma_ref[row : row + count], mixing
        )


def keep_rims(rim_ref, wide_ref, rows):
    span = 2 * NSTEP
    for end, low in enumerate((0, rows - span)):
        rim_ref[end * span : (end + 1) * span] = wide_ref[low : low + span]


def pole_flags():
    at = lax.axis_index("lat")
    last = lax.axis_size("lat") - 1
    return jnp.where(at > 0, 1.0, 0.0), jnp.where(at < last, 1.0, 0.0)


def put_rims(wide_ref, rim_ref, north, south, cols):
    wide_ref[NSTEP : 5 * NSTEP] = rim_ref[...]
    for at, rim in ((0, north), (5 * NSTEP, south)):
        wide_ref[at : at + NSTEP, tile_of(cols), :] = rim[:, :cols]
        put_sides(
            wide_ref, at, NSTEP, cols, rim[:, cols : cols + NSTEP], rim[:, cols + NSTEP :]
        )


def ends_kernel(
    rim_ref, rim_kap_ref, sigma_ref, north_ref, south_ref, vertical_ref, out_ref,
    first_ref, second_ref, kap_ref,
):
    cols = sigma_ref.shape[2]
    north_on, south_on = pole_flags()
    put_rims(
        kap_ref, rim_kap_ref, north_ref[1].astype(F32) * north_on,
        south_ref[1].astype(F32) * south_on, cols,
    )
    put_rims(
        first_ref, rim_ref, north_ref[0].astype(F32) * north_on,
        south_ref[0].astype(F32) * south_on, cols,
    )
    done = sweeps(first_ref, second_ref, kap_ref, 6 * NSTEP)
    mixing = forward_mixing(vertical_ref[...])
    for end in range(2):
        at = slice((1 + 3 * end) * NSTEP, (2 + 3 * end) * NSTEP)
        out_ref[end] = project_rows(done[at, tile_of(cols), :], sigma_ref[end], mixing)


def owner_kernel(
    devices_all, quarter, recv_hbm, sigma_hbm, inner_ref, ends_ref, pick_ref, rinv_ref,
    ret_hbm, adj_hbm, left_hbm, right_hbm, top_hbm, bottom_hbm,
    word_ref, dep_ref, acc_ref, table_ref, pair_ref,
    recv_ref, ret_ref, sigma_ref, adj_ref, left_ref, right_ref, top_ref, bottom_ref,
    sem_ref,
):
    lat_rows, cols, levels = sigma_hbm.shape
    cells_part = inner_ref.shape[0]
    others_in = start_copies([(recv_hbm, recv_ref)], sem_ref)
    sigma_in = start_copies([(sigma_hbm, sigma_ref)], sem_ref, 1)
    table_ref[:cols, :] = ends_ref[0]
    table_ref[cols : cells_part - cols, :] = inner_ref[cols : cells_part - cols, :]
    table_ref[cells_part - cols :, :] = ends_ref[1]
    wait_copies(others_in)
    rows_half = devices_all * quarter
    rows = 2 * rows_half
    metas = []
    for device in range(devices_all):
        at = device * (quarter + 1)
        word_ref[device * quarter : (device + 1) * quarter, :] = recv_ref[at : at + quarter, :]
        metas.append(recv_ref[at + quarter : at + quarter + 1, :])
    meta = jnp.concatenate(metas, axis=0)
    cells, weights = meta >> 16, meta & 0xFFFF
    facts = jnp.concatenate(
        [
            piece.astype(F32).astype(BF16)
            for piece in (cells >> 6, cells & 63, weights >> 8, weights & 255)
        ],
        axis=1,
    )
    channels = rinv_ref.shape[0]
    pair_ref[...] = jnp.zeros_like(pair_ref)
    pair_ref[:channels, :channels] = rinv_ref[...]
    pair_ref[channels:, channels:] = rinv_ref[...]
    high, low = split_hi_lo(pair_ref[...])
    zero = jnp.zeros_like(high)
    mixing = jnp.concatenate(
        [jnp.concatenate([high, low], axis=1), jnp.concatenate([high, zero], axis=1)], axis=0
    )
    pick_pair = jnp.transpose(
        pick_ref[: 2 * channels, : 2 * levels].astype(F32)
    ).astype(BF16)
    all_hots, all_wides = [], []
    chunk = min(512, rows_half)
    left_lane = iota((chunk, 128), 1) < 64
    lane_half = iota((chunk, 128), 1) // 64
    zero_hot = jnp.zeros((chunk, 128), BF16)
    per_half = rows_half // chunk
    for step in range(rows // chunk):
        half = step // per_half
        base = (step % per_half) * chunk
        row = iota((chunk, devices_all), 0) + base
        spread = (row // quarter == iota((chunk, devices_all), 1)).astype(F32).astype(BF16)
        found = dot_f32(spread, facts)
        lat_lane = found[:, :128]
        lon_lane = found[:, 128:256]
        weight_lane = (found[:, 256:384] * 256.0 + found[:, 384:]) * WEIGHT_STEP
        lane = iota((chunk, 128), 1)
        r = (iota((chunk, 128), 0) + base) % quarter
        hots, parts, weight, values = [], [], [], []
        for side in range(2):
            take = lane == (2 * side + half) * quarter + r
            lat = jnp.sum(jnp.where(take, lat_lane, 0.0), axis=1, keepdims=True).astype(I32)
            lon = jnp.sum(jnp.where(take, lon_lane, 0.0), axis=1, keepdims=True).astype(I32)
            weight.append(jnp.sum(jnp.where(take, weight_lane, 0.0), axis=1, keepdims=True))
            part = lat & 3
            lon_hot = (lane % cols == lon).astype(F32).astype(BF16)
            band = jnp.broadcast_to((lat >> 2).astype(F32), (chunk, 128)).astype(BF16)
            hot = jnp.concatenate(
                [
                    jnp.where(
                        band == (lane // cols + first).astype(F32).astype(BF16), lon_hot, zero_hot
                    )
                    for first in range(0, lat_rows // 4, 128 // cols)
                ],
                axis=1,
            )
            got = dot_f32(hot, table_ref[...])
            low_parts = jnp.where(part == 0, got[:, :levels], got[:, levels : 2 * levels])
            high_parts = jnp.where(
                part == 2, got[:, 2 * levels : 3 * levels], got[:, 3 * levels :]
            )
            values.append(jnp.where(part < 2, low_parts, high_parts).astype(BF16))
            hots.append(hot)
            parts.append(part)
        evolved = dot_f32(jnp.concatenate(values, axis=1), pick_pair)
        words = word_ref[base : base + chunk, :]
        words = (words if half == 0 else words << 16) >> 16
        gap = evolved - words.astype(F32) * INNOV_STEP
        both = dot_f32(jnp.concatenate(split_hi_lo(gap), axis=1), mixing)
        dep = (both[:, :128] + both[:, 128:]) * jnp.where(left_lane, weight[0], weight[1])
        dep_ref[step * chunk : (step + 1) * chunk, :] = encode(evolved)
        rounded = dep.astype(BF16).astype(F32)
        swapped = pltpu.roll(rounded, 64, 1)
        for side in range(2):
            twice = (
                jnp.where(left_lane, rounded, swapped)
                if side == 0
                else jnp.where(left_lane, swapped, rounded)
            )
            wide = jnp.concatenate(
                [
                    jnp.where(parts[side] == lane_half, twice, 0.0).astype(BF16),
                    jnp.where(parts[side] == lane_half + 2, twice, 0.0).astype(BF16),
                ],
                axis=1,
            )
            all_hots.append(hots[side])
            all_wides.append(wide)
    acc_ref[...] = dot_tn(
        jnp.concatenate(all_hots, axis=0), jnp.concatenate(all_wides, axis=0)
    )
    ret_ref[...] = (dep_ref[:rows_half, :] << 16) | dep_ref[rows_half:, :]
    copies = start_copies([(ret_ref, ret_hbm)], sem_ref)
    wait_copies(sigma_in)
    groups = 4
    count = groups * 4
    for step in range(lat_rows // count):
        high, low = split_hi_lo(acc_ref[step * groups * cols : (step + 1) * groups * cols, :])
        both = dot_f32(high, pick_ref[...]) + dot_f32(low, pick_ref[...])
        for group in range(groups):
            for part in range(4):
                at = step * count + group * 4 + part
                value = sigma_ref[at] * both[
                    group * cols : (group + 1) * cols, part * levels : (part + 1) * levels
                ]
                adj_ref[at] = value
                left_ref[at] = value[:NSTEP].astype(BF16)
                right_ref[at] = value[cols - NSTEP :].astype(BF16)
                if at < NSTEP:
                    top_ref[at] = value.astype(BF16)
                if at >= lat_rows - NSTEP:
                    bottom_ref[at - (lat_rows - NSTEP)] = value.astype(BF16)
        where = pl.ds(step * count, count)
        copies += start_copies([(adj_ref.at[where], adj_hbm.at[where])], sem_ref, step + 1)
    copies += start_copies(
        [
            (left_ref, left_hbm),
            (right_ref, right_hbm),
            (top_ref, top_hbm),
            (bottom_ref, bottom_hbm),
        ],
        sem_ref,
        lat_rows // count + 1,
    )
    wait_copies(copies)


def backward_mixing(vertical):
    high, low = split_hi_lo(vertical)
    return jnp.concatenate(
        [jnp.concatenate([high, high], axis=1), jnp.concatenate([low, low], axis=1)], axis=0
    )


def finish_rows(scaled, kap, mixing):
    count, cols, levels = scaled.shape
    adjoint = (scaled / kap).reshape(count * cols, levels)
    both = dot_nt(jnp.concatenate(split_hi_lo(adjoint), axis=1), mixing)
    return (both[:, :levels] + both[:, levels:]).reshape(count, cols, levels)


def inner_kernel(
    adj_hbm, control_hbm, east_ref, west_ref, kappa_ref, keast_ref, kwest_ref, vertical_ref,
    out_hbm, rim_ref, rim_kap_ref, rim_control_ref, first_ref, second_ref, kap_ref, out_ref,
    control_ref, sem_ref,
):
    rows, cols, levels = control_hbm.shape
    tile_in = start_copies([(adj_hbm, first_ref.at[pl.ds(0, rows), pl.ds(LEAD, cols)])], sem_ref)
    kap_ref[:rows, tile_of(cols), :] = spread_kappa(kappa_ref[...])
    put_sides(kap_ref, 0, rows, cols, keast_ref[1], kwest_ref[1])
    put_sides(first_ref, 0, rows, cols, east_ref[...], west_ref[...])
    wait_copies(tile_in)
    control_in = start_copies([(control_hbm, control_ref)], sem_ref, 1)
    first_ref[:rows] = first_ref[:rows] * kap_ref[:rows]
    keep_rims(rim_ref, first_ref, rows)
    keep_rims(rim_kap_ref, kap_ref, rows)
    done = sweeps(first_ref, second_ref, kap_ref, rows)
    mixing = backward_mixing(vertical_ref[...])
    wait_copies(control_in)
    rim_control_ref[0] = control_ref[:NSTEP]
    rim_control_ref[1] = control_ref[rows - NSTEP :]
    count = 8
    copies = []
    for index in range((rows - 2 * NSTEP) // count):
        row = NSTEP + index * count
        at = pl.ds(row, count)
        out_ref[at] = control_ref[at] + finish_rows(
            done[row : row + count, tile_of(cols), :], kap_ref[row : row + count, tile_of(cols), :], mixing
        )
        copies += start_copies([(out_ref.at[at], out_hbm.at[at])], sem_ref, index)
    wait_copies(copies)


def rim_kernel(
    rim_ref, rim_kap_ref, control_ref, north_ref, south_ref, knorth_ref, ksouth_ref, vertical_ref,
    inner_ref, out_ref, first_ref, second_ref, kap_ref, edge_ref, sem_ref,
):
    del inner_ref
    lat_rows = out_ref.shape[0]
    cols = out_ref.shape[1]
    north_on, south_on = pole_flags()
    put_rims(
        kap_ref, rim_kap_ref, knorth_ref[1].astype(F32) * north_on,
        ksouth_ref[1].astype(F32) * south_on, cols,
    )
    put_rims(
        first_ref, rim_ref, north_ref[...].astype(F32), south_ref[...].astype(F32), cols
    )
    for at in (0, 5 * NSTEP):
        first_ref[at : at + NSTEP] = first_ref[at : at + NSTEP] * kap_ref[at : at + NSTEP]
    done = sweeps(first_ref, second_ref, kap_ref, 6 * NSTEP)
    mixing = backward_mixing(vertical_ref[...])
    copies = []
    for end in range(2):
        at = pl.ds((1 + 3 * end) * NSTEP, NSTEP)
        back = finish_rows(done[at, tile_of(cols), :], kap_ref[at, tile_of(cols), :], mixing)
        edge_ref[end] = control_ref[end] + back
        copies += start_copies(
            [(edge_ref.at[end], out_ref.at[pl.ds(end * (lat_rows - NSTEP), NSTEP)])], sem_ref, end
        )
    wait_copies(copies)


def pass_kernel(array_hbm, first_hbm, second_hbm, out_hbm):
    del array_hbm, first_hbm, second_hbm, out_hbm


def return_kernel(
    devices_all, quarter, recv_ref, key_ref, innov_ref, weight_ref, rinv_ref, out_ref,
    pair_ref,
):
    rows_half = devices_all * quarter
    rows = 2 * rows_half
    channels, obs = out_ref.shape
    words = recv_ref[...]
    for half in range(2):
        code = (words >> 16) & 0xFFFF if half == 0 else words & 0xFFFF
        high, low = split_hi_lo(decode(code))
        pair_ref[half * rows_half : (half + 1) * rows_half, :128] = high
        pair_ref[half * rows_half : (half + 1) * rows_half, 128:] = low
    weight = weight_ref[...]
    chunk = obs
    for start in range(0, obs, chunk):
        key = key_ref[:, start : start + chunk]
        side = key >= rows
        row = jnp.where(side, key - rows, key)
        hot = (iota((rows, chunk), 0) == row).astype(F32).astype(BF16)
        both = dot_tn(pair_ref[...], hot)
        both = both[:128] + both[128:]
        evolved = jnp.where(side, both[channels:], both[:channels])
        gap = evolved - innov_ref[:, start : start + chunk]
        mixed = lax.dot_general(
            rinv_ref[...], gap, (((0,), (0,)), ((), ())), precision=lax.Precision.HIGHEST,
            preferred_element_type=F32,
        )
        out_ref[:, start : start + chunk] = mixed * weight[:, start : start + chunk]


def shifts(axis):
    count = lax.axis_size(axis)
    forward = [(i, (i + 1) % count) for i in range(count)]
    return forward, [(target, source) for source, target in forward]


def exchange_sides(left, right):
    forward, backward = shifts("lon")
    return lax.ppermute(left, "lon", backward), lax.ppermute(right, "lon", forward)


def exchange_rims(top, bottom):
    forward, backward = shifts("lat")
    return lax.ppermute(bottom, "lat", forward), lax.ppermute(top, "lat", backward)


def estimate(flops, bytes_accessed):
    return pl.CostEstimate(flops=flops, bytes_accessed=bytes_accessed, transcendentals=0)


def body(
    control,
    kappa,
    sigma,
    vertical,
    channel_table,
    channel_pick,
    r_inverse,
    innovations,
    error_scale,
    obs_owner,
    obs_cell,
    obs_count,
):
    lat_rows, lon_cols, levels = control.shape
    obs_slots = obs_cell.shape[0]
    channels = innovations.shape[1]
    devices_all = lax.axis_size("lat") * lax.axis_size("lon")
    capacity = max(4, 2 * obs_slots // devices_all)
    quarter = capacity // 4
    rows_half = devices_all * quarter
    columns = lat_rows * lon_cols
    wide = (lat_rows + 1, lon_cols + 2 * LEAD, levels)
    rim_tile = (4 * NSTEP, lon_cols + 2 * LEAD, levels)
    rim = (6 * NSTEP, lon_cols + 2 * LEAD, levels)
    anywhere = pl.BlockSpec(memory_space=pl.ANY)

    control, sigma = in_hbm(control), in_hbm(sigma)
    near, far = pl.pallas_call(
        pack_kernel,
        out_shape=(jax.ShapeDtypeStruct((2, lat_rows, NSTEP, levels), BF16),) * 2,
        in_specs=[HBM_SPEC] * 2,
        out_specs=tuple(vmem_specs(2)),
        scratch_shapes=[
            pltpu.VMEM((lat_rows, 8, levels), F32),
            pltpu.VMEM((lat_rows, 8, levels), F32),
            pltpu.VMEM(kappa.shape, F32),
            pltpu.SemaphoreType.DMA((3,)),
        ],
        compiler_params=params(6),
        name="pack",
    )(control, in_hbm(kappa))
    valid = jnp.arange(obs_slots, dtype=I32) < obs_count[0]
    weight = jnp.where(valid, 1.0 / (error_scale * error_scale), F32(0.0))
    weight = weight.reshape(1, obs_slots)
    near, far, obs_cell = lax.optimization_barrier((near, far, obs_cell))
    east, west = exchange_sides(near, far)

    payload, key, top, bottom = pl.pallas_call(
        functools.partial(address_kernel, devices_all, quarter),
        out_shape=(
            jax.ShapeDtypeStruct((devices_all * (quarter + 1), 128), I32),
            jax.ShapeDtypeStruct((1, obs_slots), I32),
            jax.ShapeDtypeStruct((2, NSTEP, lon_cols, levels), BF16),
            jax.ShapeDtypeStruct((2, NSTEP, lon_cols, levels), BF16),
        ),
        in_specs=vmem_specs(5) + [HBM_SPEC],
        out_specs=tuple(vmem_specs(4)),
        scratch_shapes=[
            pltpu.VMEM((rows_half, 128), I32),
            pltpu.VMEM((2, NSTEP, lon_cols, levels), F32),
            pltpu.SemaphoreType.DMA((2,)),
        ],
        compiler_params=params(16),
        cost_estimate=estimate(2_000_000_000, 8_000_000),
        name="address",
    )(
        obs_owner.reshape(1, obs_slots),
        obs_cell.reshape(1, obs_slots),
        weight,
        innovations.T,
        kappa,
        control,
    )
    received = lax.all_to_all(
        payload.reshape(devices_all, 1, (quarter + 1) * 128),
        ("lat", "lon"),
        split_axis=0,
        concat_axis=0,
        tiled=True,
    ).reshape(payload.shape)

    def with_sides(tile, low, high):
        return jnp.concatenate([tile, east[:, low:high], west[:, low:high]], axis=2)

    north, south = exchange_rims(
        with_sides(top, 0, NSTEP), with_sides(bottom, lat_rows - NSTEP, lat_rows)
    )

    evolved, picked, rim_state, rim_kappa, rim_sigma = pl.pallas_call(
        forward_kernel,
        out_shape=(
            pltpu.VMEM((columns // 4, 8 * channels), BF16),
            pltpu.VMEM((4 * channels, 4 * levels), BF16),
            pltpu.VMEM(rim_tile, F32),
            pltpu.VMEM(rim_tile, F32),
            pltpu.VMEM((2, NSTEP, lon_cols, levels), F32),
        ),
        in_specs=[HBM_SPEC] * 2 + vmem_specs(6),
        out_specs=tuple(vmem_specs(5)),
        scratch_shapes=[pltpu.VMEM(wide, F32)] * 3
        + [pltpu.VMEM(control.shape, F32), pltpu.SemaphoreType.DMA((2,))],
        compiler_params=params(24),
        cost_estimate=estimate(4_000_000_000, 16_000_000),
        name="forward",
    )(
        control, sigma, east, west, kappa, vertical, channel_table,
        channel_pick.reshape(1, channels),
    )

    ends = pl.pallas_call(
        ends_kernel,
        out_shape=pltpu.VMEM((2, lon_cols, 8 * channels), BF16),
        in_specs=vmem_specs(6),
        out_specs=vmem_specs(1)[0],
        scratch_shapes=[pltpu.VMEM(rim, F32)] * 3,
        compiler_params=params(12),
        cost_estimate=estimate(1_000_000_000, 2_000_000),
        name="ends",
    )(rim_state, rim_kappa, rim_sigma, north, south, vertical)

    returned, adjoint, left, right, atop, abottom = pl.pallas_call(
        functools.partial(owner_kernel, devices_all, quarter),
        out_shape=(
            pltpu.HBM((rows_half, 128), I32),
            pltpu.HBM(control.shape, F32),
            pltpu.HBM((lat_rows, NSTEP, levels), BF16),
            pltpu.HBM((lat_rows, NSTEP, levels), BF16),
            jax.ShapeDtypeStruct((NSTEP, lon_cols, levels), BF16),
            jax.ShapeDtypeStruct((NSTEP, lon_cols, levels), BF16),
        ),
        in_specs=[HBM_SPEC] * 2 + vmem_specs(4),
        out_specs=(HBM_SPEC,) * 6,
        scratch_shapes=[
            pltpu.VMEM((rows_half, 128), I32),
            pltpu.VMEM((2 * rows_half, 128), I32),
            pltpu.VMEM((columns // 4, 4 * channels), F32),
            pltpu.VMEM((columns // 4, 8 * channels), BF16),
            pltpu.VMEM((2 * channels, 2 * channels), F32),
            pltpu.VMEM((devices_all * (quarter + 1), 128), I32),
            pltpu.VMEM((rows_half, 128), I32),
            pltpu.VMEM(control.shape, F32),
            pltpu.VMEM(control.shape, F32),
            pltpu.VMEM((lat_rows, NSTEP, levels), BF16),
            pltpu.VMEM((lat_rows, NSTEP, levels), BF16),
            pltpu.VMEM((NSTEP, lon_cols, levels), BF16),
            pltpu.VMEM((NSTEP, lon_cols, levels), BF16),
            pltpu.SemaphoreType.DMA((max(8, lat_rows // 16 + 5),)),
        ],
        compiler_params=params(28),
        cost_estimate=estimate(4_000_000_000, 16_000_000),
        name="owner",
    )(received, sigma, evolved, ends, picked, r_inverse)
    returned = pl.pallas_call(
        pass_kernel,
        out_shape=pltpu.HBM(returned.shape, I32),
        in_specs=[HBM_SPEC] * 3,
        out_specs=HBM_SPEC,
        input_output_aliases={0: 0},
        cost_estimate=estimate(1_000_000, 1_000_000),
        name="pass",
    )(in_hbm(returned), in_hbm(left), in_hbm(right))
    home = lax.all_to_all(
        returned.reshape(devices_all, quarter, 128),
        ("lat", "lon"),
        split_axis=0,
        concat_axis=0,
        tiled=True,
    ).reshape(returned.shape)

    aeast, awest = exchange_sides(left, right)
    anorth, asouth = exchange_rims(
        jnp.concatenate([atop, aeast[:NSTEP], awest[:NSTEP]], axis=1),
        jnp.concatenate([abottom, aeast[-NSTEP:], awest[-NSTEP:]], axis=1),
    )
    inner, rim_scaled, rim_kappa, rim_control = pl.pallas_call(
        inner_kernel,
        out_shape=(
            pltpu.HBM(control.shape, F32),
            pltpu.VMEM(rim_tile, F32),
            pltpu.VMEM(rim_tile, F32),
            pltpu.VMEM((2, NSTEP, lon_cols, levels), F32),
        ),
        in_specs=[HBM_SPEC] * 2 + vmem_specs(6),
        out_specs=(HBM_SPEC,) + tuple(vmem_specs(3)),
        scratch_shapes=[pltpu.VMEM(wide, F32)] * 3
        + [pltpu.VMEM(control.shape, F32)] * 2
        + [pltpu.SemaphoreType.DMA((lat_rows // 8,))],
        compiler_params=params(24),
        cost_estimate=estimate(4_000_000_000, 16_000_000),
        name="inner",
    )(in_hbm(adjoint), control, aeast, awest, kappa, east, west, vertical)

    gradient = pl.pallas_call(
        rim_kernel,
        out_shape=jax.ShapeDtypeStruct(control.shape, F32),
        in_specs=vmem_specs(8) + [anywhere],
        out_specs=anywhere,
        scratch_shapes=[pltpu.VMEM(rim, F32)] * 3
        + [
            pltpu.VMEM((2, NSTEP, lon_cols, levels), F32),
            pltpu.SemaphoreType.DMA((2,)),
        ],
        input_output_aliases={8: 0},
        compiler_params=params(12),
        cost_estimate=estimate(1_000_000_000, 2_000_000),
        name="rims",
    )(
        rim_scaled, rim_kappa, rim_control, anorth, asouth, north, south, vertical, inner,
    )

    departures = pl.pallas_call(
        functools.partial(return_kernel, devices_all, quarter),
        out_shape=jax.ShapeDtypeStruct((channels, obs_slots), F32),
        in_specs=vmem_specs(5),
        out_specs=vmem_specs(1)[0],
        scratch_shapes=[pltpu.VMEM((2 * rows_half, 256), BF16)],
        compiler_params=params(16),
        cost_estimate=estimate(500_000_000, 2_000_000),
        name="give_back",
    )(
        home, key, innovations.T, weight,
        r_inverse,
    )
    return (gradient, departures.T)


def solution(mesh):
    return jax.shard_map(
        body,
        mesh=mesh,
        in_specs=(
            P("lat", "lon", None),
            P("lat", "lon"),
            P("lat", "lon", None),
            P(),
            P(),
            P(),
            P(),
            P(("lat", "lon"), None),
            P(("lat", "lon")),
            P(("lat", "lon"), None),
            P(("lat", "lon")),
            P(("lat", "lon")),
        ),
        out_specs=(P("lat", "lon", None), P(("lat", "lon"), None)),
        check_vma=False,
    )
```

```python
import functools

import jax
import jax.numpy as jnp
from jax import lax
from jax.experimental import pallas as pl
from jax.experimental.pallas import tpu as pltpu
from jax.sharding import PartitionSpec as P

NSTEP = 4
F32 = jnp.float32
BF16 = jnp.bfloat16
I32 = jnp.int32
INNOV_MAX = 6.0
INNOV_STEP = INNOV_MAX / 32767.0
WEIGHT_MAX = 4.0
WEIGHT_STEP = WEIGHT_MAX / 65535.0
CODE_FLOOR = -15.0
CODE_STEPS = 1056.0


def split_hi_lo(value):
    high = value.astype(BF16)
    low = (value - high.astype(F32)).astype(BF16)
    return high, low


def encode(value):
    size = jnp.maximum(jnp.abs(value), 2.0**CODE_FLOOR)
    level = (jnp.log2(size) - CODE_FLOOR) * CODE_STEPS + 0.5
    code = jnp.minimum(level, 32767.0).astype(I32)
    return jnp.where(value < 0.0, code + 32768, code)


def decode(code):
    level = code & 32767
    size = jnp.exp2(level.astype(F32) * (1.0 / CODE_STEPS) + CODE_FLOOR)
    size = jnp.where(level == 0, 0.0, size)
    return jnp.where(code >= 32768, -size, size)


def iota(shape, dim):
    return lax.broadcasted_iota(I32, shape, dim)


def dot_f32(left, right):
    return jnp.dot(left, right, preferred_element_type=F32)


def dot_nt(left, right):
    return lax.dot_general(left, right, (((1,), (1,)), ((), ())), preferred_element_type=F32)


def dot_tn(left, right):
    return lax.dot_general(left, right, (((0,), (0,)), ((), ())), preferred_element_type=F32)


def params(mebibytes):
    return pltpu.CompilerParams(vmem_limit_bytes=mebibytes * 1024 * 1024)


HBM_SPEC = pl.BlockSpec(memory_space=pltpu.HBM)


def in_hbm(array):
    return pltpu.with_memory_space_constraint(array, pltpu.HBM)


def start_copies(pairs, sem_ref, first=0):
    copies = []
    for index, (source, target) in enumerate(pairs):
        copy = pltpu.make_async_copy(source, target, sem_ref.at[first + index])
        copy.start()
        copies.append(copy)
    return copies


def wait_copies(copies):
    for copy in copies:
        copy.wait()


def vmem_specs(count):
    return [pl.BlockSpec(memory_space=pltpu.VMEM)] * count


def address_kernel(
    devices_all, quarter, owner_ref, cell_ref, weight_ref, innov_ref, kappa_ref,
    control_hbm, out_ref, key_ref, top_ref, bottom_ref, word_ref, ends_ref, sem_ref,
):
    grid_rows = control_hbm.shape[0]
    ends_in = start_copies(
        [
            (control_hbm.at[pl.ds(0, NSTEP)], ends_ref.at[0]),
            (control_hbm.at[pl.ds(grid_rows - NSTEP, NSTEP)], ends_ref.at[1]),
        ],
        sem_ref,
    )
    obs = owner_ref.shape[1]
    rows_half = devices_all * quarter
    rows = 2 * rows_half
    owner = owner_ref[...]
    cell = cell_ref[...]
    mine = iota((devices_all, obs), 0) == owner
    mine_f = mine.astype(F32)
    mine_b = mine_f.astype(BF16)
    block = min(256, obs)
    earlier = (iota((block, block), 0) < iota((block, block), 1)).astype(F32).astype(BF16)
    running = jnp.zeros((devices_all, 1), F32)
    parts = []
    for start in range(0, obs, block):
        piece = mine_f[:, start : start + block]
        before = dot_f32(mine_b[:, start : start + block], earlier) + running
        parts.append(jnp.sum(piece * before, axis=0, keepdims=True))
        running = running + jnp.sum(piece, axis=1, keepdims=True)
    position = jnp.concatenate(parts, axis=1).astype(I32)
    group = position // quarter
    key = (
        (group // 2) * rows + (group % 2) * rows_half + owner * quarter + position % quarter
    )
    key_ref[...] = key
    weight = jnp.minimum(jnp.floor(weight_ref[...] * (1.0 / WEIGHT_STEP) + 0.5), 65535.0)
    weight_high = jnp.floor(weight * (1.0 / 256.0))
    weight_low = weight - 256.0 * weight_high
    cell_high = (cell // 64).astype(F32)
    cell_low = (cell % 64).astype(F32)
    left = jnp.concatenate(
        [mine_f * piece for piece in (cell_high, cell_low, weight_high, weight_low)], axis=0
    ).astype(BF16)
    place = (iota((128, obs), 0) == position).astype(F32).astype(BF16)
    table = dot_nt(left, place).astype(I32)
    n = devices_all
    cells = table[:n] * 64 + table[n : 2 * n]
    weights = table[2 * n : 3 * n] * 256 + table[3 * n :]
    meta = (cells << 16) | weights

    level = jnp.floor(
        jnp.clip(innov_ref[...], -INNOV_MAX, INNOV_MAX) * (1.0 / INNOV_STEP) + 0.5
    )
    high = jnp.floor(level * (1.0 / 256.0))
    low = (level - 256.0 * high).astype(BF16)
    high = high.astype(BF16)
    bytes_of = [jnp.concatenate([high, low], axis=0), jnp.concatenate([low, high], axis=0)]
    chunk = rows_half
    left_lane = iota((chunk, 128), 1) < 64
    for base in range(0, rows_half, chunk):
        total = []
        for half in range(2):
            row = iota((chunk, obs), 0) + (base + half * rows_half)
            found = []
            for side in range(2):
                hot = (row + side * rows == key).astype(F32).astype(BF16)
                got = dot_nt(hot, bytes_of[side])
                found.append(got * 256.0 + pltpu.roll(got, 64, 1))
            total.append(jnp.where(left_lane, found[0], found[1]).astype(I32))
        word_ref[base : base + chunk, :] = (total[0] << 16) | (total[1] & 0xFFFF)
    for device in range(devices_all):
        at = device * (quarter + 1)
        out_ref[at : at + quarter, :] = word_ref[device * quarter : (device + 1) * quarter, :]
        out_ref[at + quarter : at + quarter + 1, :] = meta[device : device + 1]
    top_ref[1] = spread_kappa(kappa_ref[:NSTEP, :]).astype(BF16)
    bottom_ref[1] = spread_kappa(kappa_ref[grid_rows - NSTEP :, :]).astype(BF16)
    wait_copies(ends_in)
    top_ref[0] = ends_ref[0].astype(BF16)
    bottom_ref[0] = ends_ref[1].astype(BF16)


LEAD = 16


def tile_of(cols):
    return slice(LEAD, LEAD + cols)


def put_sides(wide_ref, at, count, cols, east, west):
    wide_ref[at : at + count, LEAD + cols : LEAD + cols + NSTEP, :] = east.astype(F32)
    wide_ref[at : at + count, LEAD - NSTEP : LEAD, :] = west.astype(F32)


def spread_kappa(kappa, low=0, high=None):
    rows, cols = kappa.shape
    count = (cols if high is None else high) - low
    top, rest = split_hi_lo(kappa)
    pair = jnp.concatenate([top.astype(F32), rest.astype(F32)], axis=1)
    shape = (rows, count, 2 * cols)
    hot = iota(shape, 1) + low == iota(shape, 2) % cols
    spread = jnp.where(hot, pair[:, None, :], 0.0).astype(BF16)
    ones = jnp.ones((2 * cols, 128), BF16)
    return dot_f32(spread.reshape(rows * count, 2 * cols), ones).reshape(rows, count, 128)


def pack_kernel(
    control_hbm, kappa_hbm, near_ref, far_ref, left_ref, right_ref, kappa_ref, sem_ref
):
    cols = control_hbm.shape[1]
    kappa_in = start_copies([(kappa_hbm, kappa_ref)], sem_ref, 2)
    copies = start_copies(
        [
            (control_hbm.at[:, pl.ds(0, 8)], left_ref),
            (control_hbm.at[:, pl.ds(cols - 8, 8)], right_ref),
        ],
        sem_ref,
    )
    wait_copies(kappa_in)
    kappa = kappa_ref[...]
    near_ref[1] = spread_kappa(kappa, 0, 8)[:, :NSTEP].astype(BF16)
    far_ref[1] = spread_kappa(kappa, cols - 8, cols)[:, 8 - NSTEP :].astype(BF16)
    wait_copies(copies)
    near_ref[0] = left_ref[:, :NSTEP].astype(BF16)
    far_ref[0] = right_ref[:, 8 - NSTEP :].astype(BF16)


def sweep_rows(source, target, kap_ref, low, high, block=32):
    width = source.shape[1]
    here_at = slice(8, width - 8)

    def update(first, count):
        rows = [source[first + i, here_at, :] for i in range(-1, count + 1)]
        for i in range(count):
            here = rows[i + 1]
            change = (
                (rows[i] + rows[i + 2])
                + (source[first + i, 7 : width - 9, :] + source[first + i, 9 : width - 7, :])
                - 4.0 * here
            )
            target[first + i, here_at, :] = here + kap_ref[first + i, here_at, :] * change

    whole = (high - low) // block

    def step(index, carry):
        update(low + index * block, block)
        return carry

    lax.fori_loop(0, whole, step, 0)
    if low + whole * block < high:
        update(low + whole * block, high - low - whole * block)


def sweeps(first_ref, second_ref, kap_ref, rows, block=32):
    source, target = first_ref, second_ref
    for sweep in range(1, NSTEP + 1):
        sweep_rows(source, target, kap_ref, sweep, rows - sweep, block)
        source, target = target, source
    return source


def fill_picked(pick_ref, picked):
    channels, levels = picked.shape
    pick_ref[...] = jnp.zeros_like(pick_ref)
    for part in range(4):
        pick_ref[
            part * channels : (part + 1) * channels, part * levels : (part + 1) * levels
        ] = picked


def forward_mixing(vertical):
    high, low = split_hi_lo(vertical)
    pair = jnp.concatenate([high, low], axis=1)
    return jnp.concatenate([pair, pair], axis=0)


def project_rows(rows, dev, mixing):
    count, cols, levels = rows.shape
    pair = jnp.concatenate(split_hi_lo(rows.reshape(count * cols, levels)), axis=1)
    both = dot_f32(pair, mixing)
    state = both[:, :levels] + both[:, levels:]
    prof = (dev.reshape(count * cols, levels) * state).astype(BF16)
    prof = prof.reshape(count // 4, 4, cols, levels)
    return jnp.concatenate(
        [prof[:, part].reshape(count // 4 * cols, levels) for part in range(4)], axis=1
    )


def forward_kernel(
    control_hbm, sigma_hbm, east_ref, west_ref, kappa_ref, vertical_ref, table_ref, choice_ref,
    out_ref, pick_ref, rim_ref, rim_kap_ref, rim_sigma_ref, first_ref, second_ref, kap_ref,
    sigma_ref, sem_ref,
):
    rows, cols, levels = control_hbm.shape
    tile_in = start_copies(
        [(control_hbm, first_ref.at[pl.ds(0, rows), pl.ds(LEAD, cols)])], sem_ref
    )
    put_sides(first_ref, 0, rows, cols, east_ref[0], west_ref[0])
    kap_ref[:rows, tile_of(cols), :] = spread_kappa(kappa_ref[...])
    put_sides(kap_ref, 0, rows, cols, east_ref[1], west_ref[1])
    wait_copies(tile_in)
    sigma_in = start_copies([(sigma_hbm, sigma_ref)], sem_ref, 1)
    keep_rims(rim_ref, first_ref, rows)
    keep_rims(rim_kap_ref, kap_ref, rows)
    done = sweeps(first_ref, second_ref, kap_ref, rows)
    channels = choice_ref.shape[1]
    table_rows = table_ref.shape[0]
    hot = (iota((table_rows, channels), 0) == choice_ref[...]).astype(F32).astype(BF16)
    fill_picked(pick_ref, dot_tn(hot, table_ref[...]).astype(BF16))
    mixing = forward_mixing(vertical_ref[...])
    wait_copies(sigma_in)
    rim_sigma_ref[0] = sigma_ref[:NSTEP]
    rim_sigma_ref[1] = sigma_ref[rows - NSTEP :]
    count = 8
    for index in range((rows - 2 * NSTEP) // count):
        row = NSTEP + index * count
        where = pl.ds(row // 4 * cols, count // 4 * cols)
        out_ref[where, :] = project_rows(
            done[row : row + count, tile_of(cols), :], sigma_ref[row : row + count], mixing
        )


def keep_rims(rim_ref, wide_ref, rows):
    span = 2 * NSTEP
    for end, low in enumerate((0, rows - span)):
        rim_ref[end * span : (end + 1) * span] = wide_ref[low : low + span]


def pole_flags():
    at = lax.axis_index("lat")
    last = lax.axis_size("lat") - 1
    return jnp.where(at > 0, 1.0, 0.0), jnp.where(at < last, 1.0, 0.0)


def put_rims(wide_ref, rim_ref, north, south, cols):
    wide_ref[NSTEP : 5 * NSTEP] = rim_ref[...]
    for at, rim in ((0, north), (5 * NSTEP, south)):
        wide_ref[at : at + NSTEP, tile_of(cols), :] = rim[:, :cols]
        put_sides(
            wide_ref, at, NSTEP, cols, rim[:, cols : cols + NSTEP], rim[:, cols + NSTEP :]
        )


def ends_kernel(
    rim_ref, rim_kap_ref, sigma_ref, north_ref, south_ref, vertical_ref, out_ref,
    first_ref, second_ref, kap_ref,
):
    cols = sigma_ref.shape[2]
    north_on, south_on = pole_flags()
    put_rims(
        kap_ref, rim_kap_ref, north_ref[1].astype(F32) * north_on,
        south_ref[1].astype(F32) * south_on, cols,
    )
    put_rims(
        first_ref, rim_ref, north_ref[0].astype(F32) * north_on,
        south_ref[0].astype(F32) * south_on, cols,
    )
    done = sweeps(first_ref, second_ref, kap_ref, 6 * NSTEP)
    mixing = forward_mixing(vertical_ref[...])
    for end in range(2):
        at = slice((1 + 3 * end) * NSTEP, (2 + 3 * end) * NSTEP)
        out_ref[end] = project_rows(done[at, tile_of(cols), :], sigma_ref[end], mixing)


def owner_kernel(
    devices_all, quarter, recv_hbm, sigma_hbm, inner_ref, ends_ref, pick_ref, rinv_ref,
    ret_hbm, adj_hbm, left_hbm, right_hbm, top_hbm, bottom_hbm,
    word_ref, dep_ref, acc_ref, table_ref, pair_ref,
    recv_ref, ret_ref, sigma_ref, adj_ref, left_ref, right_ref, top_ref, bottom_ref,
    sem_ref,
):
    lat_rows, cols, levels = sigma_hbm.shape
    cells_part = inner_ref.shape[0]
    others_in = start_copies([(recv_hbm, recv_ref)], sem_ref)
    sigma_in = start_copies([(sigma_hbm, sigma_ref)], sem_ref, 1)
    table_ref[:cols, :] = ends_ref[0]
    table_ref[cols : cells_part - cols, :] = inner_ref[cols : cells_part - cols, :]
    table_ref[cells_part - cols :, :] = ends_ref[1]
    wait_copies(others_in)
    rows_half = devices_all * quarter
    rows = 2 * rows_half
    metas = []
    for device in range(devices_all):
        at = device * (quarter + 1)
        word_ref[device * quarter : (device + 1) * quarter, :] = recv_ref[at : at + quarter, :]
        metas.append(recv_ref[at + quarter : at + quarter + 1, :])
    meta = jnp.concatenate(metas, axis=0)
    cells, weights = meta >> 16, meta & 0xFFFF
    facts = jnp.concatenate(
        [
            piece.astype(F32).astype(BF16)
            for piece in (cells >> 6, cells & 63, weights >> 8, weights & 255)
        ],
        axis=1,
    )
    channels = rinv_ref.shape[0]
    pair_ref[...] = jnp.zeros_like(pair_ref)
    pair_ref[:channels, :channels] = rinv_ref[...]
    pair_ref[channels:, channels:] = rinv_ref[...]
    high, low = split_hi_lo(pair_ref[...])
    zero = jnp.zeros_like(high)
    mixing = jnp.concatenate(
        [jnp.concatenate([high, low], axis=1), jnp.concatenate([high, zero], axis=1)], axis=0
    )
    pick_pair = jnp.transpose(
        pick_ref[: 2 * channels, : 2 * levels].astype(F32)
    ).astype(BF16)
    all_hots, all_wides = [], []
    chunk = min(512, rows_half)
    left_lane = iota((chunk, 128), 1) < 64
    lane_half = iota((chunk, 128), 1) // 64
    zero_hot = jnp.zeros((chunk, 128), BF16)
    per_half = rows_half // chunk
    for step in range(rows // chunk):
        half = step // per_half
        base = (step % per_half) * chunk
        row = iota((chunk, devices_all), 0) + base
        spread = (row // quarter == iota((chunk, devices_all), 1)).astype(F32).astype(BF16)
        found = dot_f32(spread, facts)
        lat_lane = found[:, :128]
        lon_lane = found[:, 128:256]
        weight_lane = (found[:, 256:384] * 256.0 + found[:, 384:]) * WEIGHT_STEP
        lane = iota((chunk, 128), 1)
        r = (iota((chunk, 128), 0) + base) % quarter
        hots, parts, weight, values = [], [], [], []
        for side in range(2):
            take = lane == (2 * side + half) * quarter + r
            lat = jnp.sum(jnp.where(take, lat_lane, 0.0), axis=1, keepdims=True).astype(I32)
            lon = jnp.sum(jnp.where(take, lon_lane, 0.0), axis=1, keepdims=True).astype(I32)
            weight.append(jnp.sum(jnp.where(take, weight_lane, 0.0), axis=1, keepdims=True))
            part = lat & 3
            lon_hot = (lane % cols == lon).astype(F32).astype(BF16)
            band = jnp.broadcast_to((lat >> 2).astype(F32), (chunk, 128)).astype(BF16)
            hot = jnp.concatenate(
                [
                    jnp.where(
                        band == (lane // cols + first).astype(F32).astype(BF16), lon_hot, zero_hot
                    )
                    for first in range(0, lat_rows // 4, 128 // cols)
                ],
                axis=1,
            )
            got = dot_f32(hot, table_ref[...])
            low_parts = jnp.where(part == 0, got[:, :levels], got[:, levels : 2 * levels])
            high_parts = jnp.where(
                part == 2, got[:, 2 * levels : 3 * levels], got[:, 3 * levels :]
            )
            values.append(jnp.where(part < 2, low_parts, high_parts).astype(BF16))
            hots.append(hot)
            parts.append(part)
        evolved = dot_f32(jnp.concatenate(values, axis=1), pick_pair)
        words = word_ref[base : base + chunk, :]
        words = (words if half == 0 else words << 16) >> 16
        gap = evolved - words.astype(F32) * INNOV_STEP
        both = dot_f32(jnp.concatenate(split_hi_lo(gap), axis=1), mixing)
        dep = (both[:, :128] + both[:, 128:]) * jnp.where(left_lane, weight[0], weight[1])
        dep_ref[step * chunk : (step + 1) * chunk, :] = encode(evolved)
        rounded = dep.astype(BF16).astype(F32)
        swapped = pltpu.roll(rounded, 64, 1)
        for side in range(2):
            twice = (
                jnp.where(left_lane, rounded, swapped)
                if side == 0
                else jnp.where(left_lane, swapped, rounded)
            )
            wide = jnp.concatenate(
                [
                    jnp.where(parts[side] == lane_half, twice, 0.0).astype(BF16),
                    jnp.where(parts[side] == lane_half + 2, twice, 0.0).astype(BF16),
                ],
                axis=1,
            )
            all_hots.append(hots[side])
            all_wides.append(wide)
    acc_ref[...] = dot_tn(
        jnp.concatenate(all_hots, axis=0), jnp.concatenate(all_wides, axis=0)
    )
    ret_ref[...] = (dep_ref[:rows_half, :] << 16) | dep_ref[rows_half:, :]
    copies = start_copies([(ret_ref, ret_hbm)], sem_ref)
    wait_copies(sigma_in)
    groups = 4
    count = groups * 4
    for step in range(lat_rows // count):
        high, low = split_hi_lo(acc_ref[step * groups * cols : (step + 1) * groups * cols, :])
        both = dot_f32(high, pick_ref[...]) + dot_f32(low, pick_ref[...])
        for group in range(groups):
            for part in range(4):
                at = step * count + group * 4 + part
                value = sigma_ref[at] * both[
                    group * cols : (group + 1) * cols, part * levels : (part + 1) * levels
                ]
                adj_ref[at] = value
                left_ref[at] = value[:NSTEP].astype(BF16)
                right_ref[at] = value[cols - NSTEP :].astype(BF16)
                if at < NSTEP:
                    top_ref[at] = value.astype(BF16)
                if at >= lat_rows - NSTEP:
                    bottom_ref[at - (lat_rows - NSTEP)] = value.astype(BF16)
        where = pl.ds(step * count, count)
        copies += start_copies([(adj_ref.at[where], adj_hbm.at[where])], sem_ref, step + 1)
    copies += start_copies(
        [
            (left_ref, left_hbm),
            (right_ref, right_hbm),
            (top_ref, top_hbm),
            (bottom_ref, bottom_hbm),
        ],
        sem_ref,
        lat_rows // count + 1,
    )
    wait_copies(copies)


def backward_mixing(vertical):
    high, low = split_hi_lo(vertical)
    return jnp.concatenate(
        [jnp.concatenate([high, high], axis=1), jnp.concatenate([low, low], axis=1)], axis=0
    )


def finish_rows(scaled, kap, mixing):
    count, cols, levels = scaled.shape
    adjoint = (scaled / kap).reshape(count * cols, levels)
    both = dot_nt(jnp.concatenate(split_hi_lo(adjoint), axis=1), mixing)
    return (both[:, :levels] + both[:, levels:]).reshape(count, cols, levels)


def inner_kernel(
    adj_hbm, control_hbm, east_ref, west_ref, kappa_ref, keast_ref, kwest_ref, vertical_ref,
    out_hbm, rim_ref, rim_kap_ref, rim_control_ref, first_ref, second_ref, kap_ref, out_ref,
    control_ref, sem_ref,
):
    rows, cols, levels = control_hbm.shape
    tile_in = start_copies([(adj_hbm, first_ref.at[pl.ds(0, rows), pl.ds(LEAD, cols)])], sem_ref)
    kap_ref[:rows, tile_of(cols), :] = spread_kappa(kappa_ref[...])
    put_sides(kap_ref, 0, rows, cols, keast_ref[1], kwest_ref[1])
    put_sides(first_ref, 0, rows, cols, east_ref[...], west_ref[...])
    wait_copies(tile_in)
    control_in = start_copies([(control_hbm, control_ref)], sem_ref, 1)
    first_ref[:rows] = first_ref[:rows] * kap_ref[:rows]
    keep_rims(rim_ref, first_ref, rows)
    keep_rims(rim_kap_ref, kap_ref, rows)
    done = sweeps(first_ref, second_ref, kap_ref, rows)
    mixing = backward_mixing(vertical_ref[...])
    wait_copies(control_in)
    rim_control_ref[0] = control_ref[:NSTEP]
    rim_control_ref[1] = control_ref[rows - NSTEP :]
    count = 8
    copies = []
    for index in range((rows - 2 * NSTEP) // count):
        row = NSTEP + index * count
        at = pl.ds(row, count)
        out_ref[at] = control_ref[at] + finish_rows(
            done[row : row + count, tile_of(cols), :], kap_ref[row : row + count, tile_of(cols), :], mixing
        )
        copies += start_copies([(out_ref.at[at], out_hbm.at[at])], sem_ref, index)
    wait_copies(copies)


def rim_kernel(
    rim_ref, rim_kap_ref, control_ref, north_ref, south_ref, knorth_ref, ksouth_ref, vertical_ref,
    inner_ref, out_ref, first_ref, second_ref, kap_ref, edge_ref, sem_ref,
):
    del inner_ref
    lat_rows = out_ref.shape[0]
    cols = out_ref.shape[1]
    north_on, south_on = pole_flags()
    put_rims(
        kap_ref, rim_kap_ref, knorth_ref[1].astype(F32) * north_on,
        ksouth_ref[1].astype(F32) * south_on, cols,
    )
    put_rims(
        first_ref, rim_ref, north_ref[...].astype(F32), south_ref[...].astype(F32), cols
    )
    for at in (0, 5 * NSTEP):
        first_ref[at : at + NSTEP] = first_ref[at : at + NSTEP] * kap_ref[at : at + NSTEP]
    done = sweeps(first_ref, second_ref, kap_ref, 6 * NSTEP)
    mixing = backward_mixing(vertical_ref[...])
    copies = []
    for end in range(2):
        at = pl.ds((1 + 3 * end) * NSTEP, NSTEP)
        back = finish_rows(done[at, tile_of(cols), :], kap_ref[at, tile_of(cols), :], mixing)
        edge_ref[end] = control_ref[end] + back
        copies += start_copies(
            [(edge_ref.at[end], out_ref.at[pl.ds(end * (lat_rows - NSTEP), NSTEP)])], sem_ref, end
        )
    wait_copies(copies)


def pass_kernel(array_hbm, first_hbm, second_hbm, out_hbm):
    del array_hbm, first_hbm, second_hbm, out_hbm


def return_kernel(
    devices_all, quarter, recv_ref, key_ref, innov_ref, weight_ref, rinv_ref, out_ref,
    pair_ref,
):
    rows_half = devices_all * quarter
    rows = 2 * rows_half
    channels, obs = out_ref.shape
    words = recv_ref[...]
    for half in range(2):
        code = (words >> 16) & 0xFFFF if half == 0 else words & 0xFFFF
        high, low = split_hi_lo(decode(code))
        pair_ref[half * rows_half : (half + 1) * rows_half, :128] = high
        pair_ref[half * rows_half : (half + 1) * rows_half, 128:] = low
    weight = weight_ref[...]
    chunk = obs
    for start in range(0, obs, chunk):
        key = key_ref[:, start : start + chunk]
        side = key >= rows
        row = jnp.where(side, key - rows, key)
        hot = (iota((rows, chunk), 0) == row).astype(F32).astype(BF16)
        both = dot_tn(pair_ref[...], hot)
        both = both[:128] + both[128:]
        evolved = jnp.where(side, both[channels:], both[:channels])
        gap = evolved - innov_ref[:, start : start + chunk]
        mixed = lax.dot_general(
            rinv_ref[...], gap, (((0,), (0,)), ((), ())), precision=lax.Precision.HIGHEST,
            preferred_element_type=F32,
        )
        out_ref[:, start : start + chunk] = mixed * weight[:, start : start + chunk]


def shifts(axis):
    count = lax.axis_size(axis)
    forward = [(i, (i + 1) % count) for i in range(count)]
    return forward, [(target, source) for source, target in forward]


def exchange_sides(left, right):
    forward, backward = shifts("lon")
    return lax.ppermute(left, "lon", backward), lax.ppermute(right, "lon", forward)


def exchange_rims(top, bottom):
    forward, backward = shifts("lat")
    return lax.ppermute(bottom, "lat", forward), lax.ppermute(top, "lat", backward)


def estimate(flops, bytes_accessed):
    return pl.CostEstimate(flops=flops, bytes_accessed=bytes_accessed, transcendentals=0)


def body(
    control,
    kappa,
    sigma,
    vertical,
    channel_table,
    channel_pick,
    r_inverse,
    innovations,
    error_scale,
    obs_owner,
    obs_cell,
    obs_count,
):
    lat_rows, lon_cols, levels = control.shape
    obs_slots = obs_cell.shape[0]
    channels = innovations.shape[1]
    devices_all = lax.axis_size("lat") * lax.axis_size("lon")
    capacity = max(4, 2 * obs_slots // devices_all)
    quarter = capacity // 4
    rows_half = devices_all * quarter
    columns = lat_rows * lon_cols
    wide = (lat_rows + 1, lon_cols + 2 * LEAD, levels)
    rim_tile = (4 * NSTEP, lon_cols + 2 * LEAD, levels)
    rim = (6 * NSTEP, lon_cols + 2 * LEAD, levels)
    anywhere = pl.BlockSpec(memory_space=pl.ANY)

    control, sigma = in_hbm(control), in_hbm(sigma)
    near, far = pl.pallas_call(
        pack_kernel,
        out_shape=(jax.ShapeDtypeStruct((2, lat_rows, NSTEP, levels), BF16),) * 2,
        in_specs=[HBM_SPEC] * 2,
        out_specs=tuple(vmem_specs(2)),
        scratch_shapes=[
            pltpu.VMEM((lat_rows, 8, levels), F32),
            pltpu.VMEM((lat_rows, 8, levels), F32),
            pltpu.VMEM(kappa.shape, F32),
            pltpu.SemaphoreType.DMA((3,)),
        ],
        compiler_params=params(6),
        name="pack",
    )(control, in_hbm(kappa))
    valid = jnp.arange(obs_slots, dtype=I32) < obs_count[0]
    weight = jnp.where(valid, 1.0 / (error_scale * error_scale), F32(0.0))
    weight = weight.reshape(1, obs_slots)
    near, far, obs_cell = lax.optimization_barrier((near, far, obs_cell))
    east, west = exchange_sides(near, far)

    payload, key, top, bottom = pl.pallas_call(
        functools.partial(address_kernel, devices_all, quarter),
        out_shape=(
            jax.ShapeDtypeStruct((devices_all * (quarter + 1), 128), I32),
            jax.ShapeDtypeStruct((1, obs_slots), I32),
            jax.ShapeDtypeStruct((2, NSTEP, lon_cols, levels), BF16),
            jax.ShapeDtypeStruct((2, NSTEP, lon_cols, levels), BF16),
        ),
        in_specs=vmem_specs(5) + [HBM_SPEC],
        out_specs=tuple(vmem_specs(4)),
        scratch_shapes=[
            pltpu.VMEM((rows_half, 128), I32),
            pltpu.VMEM((2, NSTEP, lon_cols, levels), F32),
            pltpu.SemaphoreType.DMA((2,)),
        ],
        compiler_params=params(16),
        cost_estimate=estimate(2_000_000_000, 8_000_000),
        name="address",
    )(
        obs_owner.reshape(1, obs_slots),
        obs_cell.reshape(1, obs_slots),
        weight,
        innovations.T,
        kappa,
        control,
    )
    received = lax.all_to_all(
        payload.reshape(devices_all, 1, (quarter + 1) * 128),
        ("lat", "lon"),
        split_axis=0,
        concat_axis=0,
        tiled=True,
    ).reshape(payload.shape)

    def with_sides(tile, low, high):
        return jnp.concatenate([tile, east[:, low:high], west[:, low:high]], axis=2)

    north, south = exchange_rims(
        with_sides(top, 0, NSTEP), with_sides(bottom, lat_rows - NSTEP, lat_rows)
    )

    evolved, picked, rim_state, rim_kappa, rim_sigma = pl.pallas_call(
        forward_kernel,
        out_shape=(
            pltpu.VMEM((columns // 4, 8 * channels), BF16),
            pltpu.VMEM((4 * channels, 4 * levels), BF16),
            pltpu.VMEM(rim_tile, F32),
            pltpu.VMEM(rim_tile, F32),
            pltpu.VMEM((2, NSTEP, lon_cols, levels), F32),
        ),
        in_specs=[HBM_SPEC] * 2 + vmem_specs(6),
        out_specs=tuple(vmem_specs(5)),
        scratch_shapes=[pltpu.VMEM(wide, F32)] * 3
        + [pltpu.VMEM(control.shape, F32), pltpu.SemaphoreType.DMA((2,))],
        compiler_params=params(24),
        cost_estimate=estimate(4_000_000_000, 16_000_000),
        name="forward",
    )(
        control, sigma, east, west, kappa, vertical, channel_table,
        channel_pick.reshape(1, channels),
    )

    ends = pl.pallas_call(
        ends_kernel,
        out_shape=pltpu.VMEM((2, lon_cols, 8 * channels), BF16),
        in_specs=vmem_specs(6),
        out_specs=vmem_specs(1)[0],
        scratch_shapes=[pltpu.VMEM(rim, F32)] * 3,
        compiler_params=params(12),
        cost_estimate=estimate(1_000_000_000, 2_000_000),
        name="ends",
    )(rim_state, rim_kappa, rim_sigma, north, south, vertical)

    returned, adjoint, left, right, atop, abottom = pl.pallas_call(
        functools.partial(owner_kernel, devices_all, quarter),
        out_shape=(
            pltpu.HBM((rows_half, 128), I32),
            pltpu.HBM(control.shape, F32),
            pltpu.HBM((lat_rows, NSTEP, levels), BF16),
            pltpu.HBM((lat_rows, NSTEP, levels), BF16),
            jax.ShapeDtypeStruct((NSTEP, lon_cols, levels), BF16),
            jax.ShapeDtypeStruct((NSTEP, lon_cols, levels), BF16),
        ),
        in_specs=[HBM_SPEC] * 2 + vmem_specs(4),
        out_specs=(HBM_SPEC,) * 6,
        scratch_shapes=[
            pltpu.VMEM((rows_half, 128), I32),
            pltpu.VMEM((2 * rows_half, 128), I32),
            pltpu.VMEM((columns // 4, 4 * channels), F32),
            pltpu.VMEM((columns // 4, 8 * channels), BF16),
            pltpu.VMEM((2 * channels, 2 * channels), F32),
            pltpu.VMEM((devices_all * (quarter + 1), 128), I32),
            pltpu.VMEM((rows_half, 128), I32),
            pltpu.VMEM(control.shape, F32),
            pltpu.VMEM(control.shape, F32),
            pltpu.VMEM((lat_rows, NSTEP, levels), BF16),
            pltpu.VMEM((lat_rows, NSTEP, levels), BF16),
            pltpu.VMEM((NSTEP, lon_cols, levels), BF16),
            pltpu.VMEM((NSTEP, lon_cols, levels), BF16),
            pltpu.SemaphoreType.DMA((max(8, lat_rows // 16 + 5),)),
        ],
        compiler_params=params(28),
        cost_estimate=estimate(4_000_000_000, 16_000_000),
        name="owner",
    )(received, sigma, evolved, ends, picked, r_inverse)
    returned = pl.pallas_call(
        pass_kernel,
        out_shape=pltpu.HBM(returned.shape, I32),
        in_specs=[HBM_SPEC] * 3,
        out_specs=HBM_SPEC,
        input_output_aliases={0: 0},
        cost_estimate=estimate(1_000_000, 1_000_000),
        name="pass",
    )(in_hbm(returned), in_hbm(left), in_hbm(right))
    home = lax.all_to_all(
        returned.reshape(devices_all, quarter, 128),
        ("lat", "lon"),
        split_axis=0,
        concat_axis=0,
        tiled=True,
    ).reshape(returned.shape)

    aeast, awest = exchange_sides(left, right)
    anorth, asouth = exchange_rims(
        jnp.concatenate([atop, aeast[:NSTEP], awest[:NSTEP]], axis=1),
        jnp.concatenate([abottom, aeast[-NSTEP:], awest[-NSTEP:]], axis=1),
    )
    inner, rim_scaled, rim_kappa, rim_control = pl.pallas_call(
        inner_kernel,
        out_shape=(
            pltpu.HBM(control.shape, F32),
            pltpu.VMEM(rim_tile, F32),
            pltpu.VMEM(rim_tile, F32),
            pltpu.VMEM((2, NSTEP, lon_cols, levels), F32),
        ),
        in_specs=[HBM_SPEC] * 2 + vmem_specs(6),
        out_specs=(HBM_SPEC,) + tuple(vmem_specs(3)),
        scratch_shapes=[pltpu.VMEM(wide, F32)] * 3
        + [pltpu.VMEM(control.shape, F32)] * 2
        + [pltpu.SemaphoreType.DMA((lat_rows // 8,))],
        compiler_params=params(24),
        cost_estimate=estimate(4_000_000_000, 16_000_000),
        name="inner",
    )(in_hbm(adjoint), control, aeast, awest, kappa, east, west, vertical)

    gradient = pl.pallas_call(
        rim_kernel,
        out_shape=jax.ShapeDtypeStruct(control.shape, F32),
        in_specs=vmem_specs(8) + [anywhere],
        out_specs=anywhere,
        scratch_shapes=[pltpu.VMEM(rim, F32)] * 3
        + [
            pltpu.VMEM((2, NSTEP, lon_cols, levels), F32),
            pltpu.SemaphoreType.DMA((2,)),
        ],
        input_output_aliases={8: 0},
        compiler_params=params(12),
        cost_estimate=estimate(1_000_000_000, 2_000_000),
        name="rims",
    )(
        rim_scaled, rim_kappa, rim_control, anorth, asouth, north, south, vertical, inner,
    )

    departures = pl.pallas_call(
        functools.partial(return_kernel, devices_all, quarter),
        out_shape=jax.ShapeDtypeStruct((channels, obs_slots), F32),
        in_specs=vmem_specs(5),
        out_specs=vmem_specs(1)[0],
        scratch_shapes=[pltpu.VMEM((2 * rows_half, 256), BF16)],
        compiler_params=params(16),
        cost_estimate=estimate(500_000_000, 2_000_000),
        name="give_back",
    )(
        home, key, innovations.T, weight,
        r_inverse,
    )
    return (gradient, departures.T)


def solution(mesh):
    return jax.shard_map(
        body,
        mesh=mesh,
        in_specs=(
            P("lat", "lon", None),
            P("lat", "lon"),
            P("lat", "lon", None),
            P(),
            P(),
            P(),
            P(),
            P(("lat", "lon"), None),
            P(("lat", "lon")),
            P(("lat", "lon"), None),
            P(("lat", "lon")),
            P(("lat", "lon")),
        ),
        out_specs=(P("lat", "lon", None), P(("lat", "lon"), None)),
        check_vma=False,
    )
```
